32 devices in a mesh: groups: 2 (over x), docs: 16 (over z, y, core).
Axes of the slice: x: 2, y: 2, z: 4, core: 2. Of those that a mesh axis runs over, the one named last changes fastest.
Arguments:
- embeddings: bfloat16 [4096, 1024], P(('groups', 'docs')), parts along dimension 0, may hold values from -100 to 100
- labels: int32 [4096], P(('groups', 'docs')), parts along dimension 0, may hold values from 0 to 15, as said below
- row_slot: int32 [4096], P(('groups', 'docs')), parts along dimension 0, may hold values from 0 to 2047, as said below
Outputs:
- density: float32 [4096], P(('groups', 'docs')), parts along dimension 0
- neighbour_mean: bfloat16 [4096, 1024], P(('groups', 'docs')), parts along dimension 0
The draws below stay inside these ranges and needn't reach their ends.
There are 2 independent parts, one for each index of `groups`. The reference program is written for one: setup_inputs(seed, part) draws one part's arguments, and reference() takes and returns one part's arrays. A program takes and returns all parts, laid end to end along the dimension named above; each array names one. Nothing has to cross between parts.
Inputs may be any that keep to these rules, and one draw needn't show every extreme that they name: row_slot is a permutation of 0 to 2047; at most 16 documents of one device take rows of one block, and some device places exactly 16 documents in some block. All documents in one block share one label; documents with equal labels lie in blocks at most 3 apart, and some label spans 4 blocks.
All inputs are finite; a program needn't handle non-finite values.
Results may differ from the reference program's by a relative error of at most 0.0029.
Values may be sent and summed in bfloat16 or wider, within the bound.
A program may use at most 64 MiB of HBM per device.

```python
import math
import jax
import jax.numpy as jnp
from jax import lax

D = 1024
ROWS_DEV = 128
REACH = 3
CAP = 16
TOKENS = 2048
N_DOCS = 16


def layout(base_key):
    device_total = N_DOCS
    block_rows = ROWS_DEV
    streams = jax.random.split(jax.random.fold_in(base_key, 7), 7)
    offsets = jnp.arange(device_total * CAP, dtype=jnp.int32) // CAP
    favored = jax.random.randint(streams[0], (), 0, device_total)
    tickets = jax.random.permutation(streams[1], device_total * CAP).astype(jnp.int32)
    tickets = jnp.where(offsets == favored, tickets - device_total * CAP, tickets)
    ordering = jnp.argsort(tickets)
    chosen = offsets[ordering[:block_rows]]
    per_offset = jnp.sum((chosen[:, None] == jnp.arange(device_total, dtype=jnp.int32)[None, :]).astype(jnp.int32), axis=0)
    relabel = jax.random.permutation(streams[2], device_total).astype(jnp.int32)
    sent = per_offset[(relabel[None, :] - relabel[:, None]) % device_total]
    run_ends = jnp.cumsum(sent, axis=1)
    positions = jnp.arange(block_rows, dtype=jnp.int32)
    target = jnp.sum((run_ends[:, None, :] <= positions[None, :, None]).astype(jnp.int32), axis=2)
    run_starts = run_ends - sent
    slot_rank = positions[None, :] - jnp.take_along_axis(run_starts, target, axis=1)
    earlier_sources = jnp.cumsum(sent, axis=0) - sent
    sorted_slots = target * block_rows + jnp.take_along_axis(earlier_sources, target, axis=1) + slot_rank
    shuffles = jax.vmap(lambda one_key: jax.random.permutation(one_key, block_rows))(jax.random.split(streams[3], device_total)).astype(jnp.int32)
    slot_of_row = jnp.take_along_axis(sorted_slots, shuffles, axis=1).reshape(-1).astype(jnp.int32)
    lengths = jax.random.randint(streams[4], (device_total,), 1, REACH + 2)
    forced = jax.random.randint(streams[5], (), 0, max(1, device_total // (REACH + 2)))
    lengths = lengths.at[forced].set(REACH + 1)
    bounds = jnp.cumsum(lengths)
    cluster = jnp.sum((bounds[None, :] <= jnp.arange(device_total, dtype=jnp.int32)[:, None]).astype(jnp.int32), axis=1)
    cluster_names = jax.random.permutation(streams[6], device_total).astype(jnp.int32)
    return (slot_of_row, cluster, cluster_names[cluster])


def draw_row_slot(key, part):
    slot_of_row, cluster, block_label = layout(key)
    return slot_of_row


def draw_labels(key, part):
    slot_of_row, cluster, block_label = layout(key)
    return block_label[slot_of_row // ROWS_DEV].astype(jnp.int32)


def draw_embeddings(key, part):
    slot_of_row, cluster, block_label = layout(key)
    streams = jax.random.split(jax.random.fold_in(key, 11), 2)
    centers = jnp.clip(jax.random.normal(streams[0], (N_DOCS, D), jnp.float32), -5.0, 5.0)
    noise = jnp.clip(jax.random.normal(streams[1], (TOKENS, D), jnp.float32), -5.0, 5.0)
    slot_cluster = cluster[jnp.arange(TOKENS, dtype=jnp.int32) // ROWS_DEV]
    by_slot = 0.5 * centers[slot_cluster] + 0.87 * noise
    return by_slot[slot_of_row].astype(jnp.bfloat16)


def setup_inputs(seed: int = 0, part: int = 0) -> dict:
    key_of = jax.random.split(jax.random.key(seed), 4)
    part_keys = jax.random.split(jax.random.fold_in(key_of[3], part), 4)
    embeddings = draw_embeddings(jax.random.fold_in(jax.random.fold_in(key_of[3], part), 71), part)
    labels = draw_labels(jax.random.fold_in(jax.random.fold_in(key_of[3], part), 71), part)
    row_slot = draw_row_slot(jax.random.fold_in(jax.random.fold_in(key_of[3], part), 71), part)
    return dict(embeddings=embeddings, labels=labels, row_slot=row_slot)


neg_large = -1e+30
kernel_gain = 4.0

def side_terms(scores, same_label, values):
    masked = jnp.where(same_label, scores, neg_large)
    row_max = lax.optimization_barrier(jnp.max(masked, axis=1))
    weights = jnp.where(same_label, jnp.exp(masked - row_max[:, None]), 0.0)
    row_total = lax.optimization_barrier(jnp.sum(weights, axis=1))
    rounded = weights.astype(jnp.bfloat16)
    row_accum = jnp.dot(rounded, values, preferred_element_type=jnp.float32)
    return (row_max, row_total, row_accum)

def block_terms(own_x, own_tag, far_x, far_tag, exclude_self):
    feature_width = own_x.shape[1]
    scores = jnp.dot(own_x, far_x.T, preferred_element_type=jnp.float32) * (kernel_gain / math.sqrt(feature_width))
    same_label = own_tag[:, None] == far_tag[None, :]
    if exclude_self:
        positions = jnp.arange(own_x.shape[0], dtype=jnp.int32)
        same_label = same_label & (positions[:, None] != positions[None, :])
    return side_terms(scores, same_label, far_x)

def combine(first_terms, second_terms):
    row_max = jnp.maximum(first_terms[0], second_terms[0])
    scale_first = jnp.exp(first_terms[0] - row_max)
    scale_second = jnp.exp(second_terms[0] - row_max)
    row_total = first_terms[1] * scale_first + second_terms[1] * scale_second
    row_accum = first_terms[2] * scale_first[:, None] + second_terms[2] * scale_second[:, None]
    return (row_max, row_total, row_accum)

def reference(embeddings, labels, row_slot):
    block_rows = ROWS_DEV
    device_total = N_DOCS
    blocks_x = jnp.zeros((TOKENS, D), jnp.bfloat16).at[row_slot].set(embeddings).reshape(device_total, block_rows, D)
    blocks_tag = jnp.zeros((TOKENS,), jnp.int32).at[row_slot].set(labels + 1).reshape(device_total, block_rows)
    nothing = (jnp.full((block_rows,), neg_large, jnp.float32), jnp.zeros((block_rows,), jnp.float32), jnp.zeros((block_rows, D), jnp.float32))

    def one_block(block_index):
        own_x = blocks_x[block_index]
        own_tag = blocks_tag[block_index]
        running = block_terms(own_x, own_tag, own_x, own_tag, True)

        def with_pairs(far_block, far_labels):
            return block_terms(own_x, own_tag, far_block, far_labels, False)

        def without_pairs(far_block, far_labels):
            return nothing
        for distance in range(1, REACH + 1):
            for direction in (1, -1):
                partner = block_index + direction * distance
                inside = (partner >= 0) & (partner < device_total)
                partner_safe = jnp.clip(partner, 0, device_total - 1).astype(jnp.int32)
                far_block = blocks_x[partner_safe]
                far_labels = jnp.where(inside, blocks_tag[partner_safe], 0)
                has_pairs = jnp.any(own_tag[:, None] == far_labels[None, :])
                partial_terms = lax.cond(has_pairs, with_pairs, without_pairs, far_block, far_labels)
                running = combine(running, partial_terms)
        row_max, row_total, row_accum = running
        return (row_max + jnp.log(row_total), (row_accum / row_total[:, None]).astype(jnp.bfloat16))
    densities, means = lax.map(one_block, jnp.arange(device_total, dtype=jnp.int32))
    return (densities.reshape(-1)[row_slot], means.reshape(TOKENS, D)[row_slot])
```

```python
import functools
import math

import jax
import jax.numpy as jnp
from jax import lax
from jax.experimental import pallas as pl
from jax.experimental.pallas import tpu as pltpu
from jax.sharding import PartitionSpec as P

MESH = pl.DeviceIdType.MESH
CORES = 2
PIECES = 2
HALVES = 1
FOLDED_GRID = (4, 2)

neg_large = -1e30
kernel_gain = 4.0


def chip_grid(device_count):
    chips = device_count // CORES
    fast = 1
    while (2 * fast) * (2 * fast) <= chips and chips % (2 * fast) == 0:
        fast *= 2
    return chips // fast, fast


def kernel(
    grid_slow, grid_fast, x_ref, lab_ref, dens_ref, mean_ref,
    buf, labs, mine, acc, row_max, row_total,
    send_sem, recv_sem, lsend_sem, lrecv_sem, own_sem, own_lab_sem,
):
    rows, width = x_ref.shape
    part = rows // PIECES
    group = PIECES // HALVES
    half_rows = rows // HALVES
    keys = CORES * half_rows
    me = lax.axis_index("docs")
    core = lax.rem(me, CORES)
    chip = me // CORES
    y = lax.rem(chip, grid_fast)
    z = chip // grid_fast

    def device(zz, yy, cc):
        return (zz * grid_fast + yy) * CORES + cc

    targets = (
        (z > 0, device(z - 1, y, core)),
        (z < grid_slow - 1, device(z + 1, y, core)),
        (y > 0, device(z, y - 1, core)),
        (y < grid_fast - 1, device(z, y + 1, core)),
        (z >= 0, device(z, y, 1 - core)),
    )

    barrier = pltpu.get_barrier_semaphore()
    for there, target in targets:
        @pl.when(there)
        def _():
            pl.semaphore_signal(barrier, inc=1, device_id={"docs": target}, device_id_type=MESH)

    def data_of(zz, yy, cc, piece):
        where = ((zz * grid_fast + yy) * HALVES + piece // group) * CORES + cc
        return buf.at[pl.ds(pl.multiple_of((where * group + lax.rem(piece, group)) * part, part), part)]

    own_copies = [pltpu.make_async_copy(x_ref, mine, own_sem.at[PIECES])]
    for piece in range(PIECES):
        own_copies.append(
            pltpu.make_async_copy(
                x_ref.at[pl.ds(piece * part, part)], data_of(z, y, core, piece), own_sem.at[piece]
            )
        )
    own_copies.append(pltpu.make_async_copy(lab_ref, labs.at[me], own_lab_sem.at[0]))
    for copy in own_copies:
        copy.start()
    pl.semaphore_wait(barrier, sum(there.astype(jnp.int32) for there, _ in targets))

    def data_copy(direction, zz, yy, piece, own):
        data = data_of(zz, yy, core, piece)
        return pltpu.make_async_remote_copy(
            x_ref.at[pl.ds(piece * part, part)] if own else data, data,
            send_sem.at[direction, (zz * grid_fast + yy) * PIECES + piece],
            recv_sem.at[device(zz, yy, core) * PIECES + piece],
            device_id={"docs": targets[direction][1]}, device_id_type=MESH,
        )

    def lab_copy(direction, zz, yy, own):
        slot = device(zz, yy, core)
        return pltpu.make_async_remote_copy(
            lab_ref if own else labs.at[slot], labs.at[slot],
            lsend_sem.at[direction, zz * grid_fast + yy], lrecv_sem.at[slot],
            device_id={"docs": targets[direction][1]}, device_id_type=MESH,
        )

    def each(directions, wanted, zz, yy, piece, own, act):
        for direction, want in zip(directions, wanted):
            @pl.when(jnp.logical_and(targets[direction][0], want))
            def _():
                @pl.when(piece == 0)
                def _():
                    act(lab_copy(direction, zz, yy, own))
                act(data_copy(direction, zz, yy, piece, own))

    start = lambda copy: copy.start()
    finish = lambda copy: copy.wait_send()

    def arrived(zz, yy, cc, piece):
        slot = device(zz, yy, cc)
        @pl.when(piece == 0)
        def _():
            pltpu.make_async_remote_copy(
                labs.at[slot], labs.at[slot], lsend_sem.at[0, 0], lrecv_sem.at[slot],
                device_id={"docs": targets[4][1]}, device_id_type=MESH,
            ).wait_recv()
        data = data_of(zz, yy, cc, piece)
        pltpu.make_async_remote_copy(
            data, data, send_sem.at[0, 0], recv_sem.at[slot * PIECES + piece],
            device_id={"docs": targets[4][1]}, device_id_type=MESH,
        ).wait_recv()

    yes = z >= 0
    for piece in range(PIECES):
        each((2, 3, 0, 1, 4), (yes,) * 5, z, y, piece, True, start)

    row_max[...] = jnp.full_like(row_max, neg_large)
    row_total[...] = jnp.zeros_like(row_total)
    acc[...] = jnp.zeros_like(acc)
    own_copies[-1].wait()
    label_column = jnp.transpose(
        jnp.broadcast_to(labs[me].astype(jnp.float32), (rows, rows))
    )[:, :1]
    column = lax.broadcasted_iota(jnp.int32, (rows, keys), 1)
    gap = (
        column + (column // half_rows) * (rows - half_rows)
        - lax.broadcasted_iota(jnp.int32, (rows, keys), 0)
    )
    for copy in own_copies[:-1]:
        copy.wait()

    def compute(zz, yy, half):
        where = zz * grid_fast + yy
        values = buf[pl.ds(pl.multiple_of((where * HALVES + half) * keys, keys), keys), :]
        tags = []
        for cc in range(CORES):
            tag = labs[where * CORES + cc].astype(jnp.float32)
            pieces = [tag[:, h * half_rows:(h + 1) * half_rows] for h in range(HALVES)]
            picked = pieces[0]
            for h in range(1, HALVES):
                picked = jnp.where(half == h, pieces[h], picked)
            tags.append(picked)
        tags = jnp.concatenate(tags, axis=1)
        scores = lax.dot_general(
            mine[...], values, (((1,), (1,)), ((), ())), preferred_element_type=jnp.float32
        ) * (kernel_gain / math.sqrt(width))
        self_gap = jnp.where(where == chip, core * rows - half * half_rows, CORES * rows)
        absorb(scores, (label_column == tags) & (gap != self_gap), values)

    def compute_core(zz, yy, cc):
        slot = device(zz, yy, cc)
        values = buf[pl.ds(pl.multiple_of(slot * rows, rows), rows), :]
        scores = lax.dot_general(
            mine[...], values, (((1,), (1,)), ((), ())), preferred_element_type=jnp.float32
        ) * (kernel_gain / math.sqrt(width))
        absorb(scores, label_column == labs[slot].astype(jnp.float32), values)

    def absorb(scores, near, values):
        masked = jnp.where(near, scores, neg_large)
        before = row_max[...]
        peak = jnp.maximum(before, jnp.max(masked, axis=1, keepdims=True))
        weights = jnp.where(near, jnp.exp(masked - peak), 0.0)
        scale = jnp.exp(before - peak)
        row_max[...] = peak
        row_total[...] = row_total[...] * scale + jnp.sum(weights, axis=1, keepdims=True)
        acc[...] = acc[...] * scale + jnp.dot(
            weights.astype(jnp.bfloat16), values, preferred_element_type=jnp.float32
        )

    def meet(zz, yy, half):
        def one(p, carry):
            arrived(zz, yy, 1 - core, half * group + p)
            return carry
        lax.fori_loop(0, group, one, 0)
        compute(zz, yy, half)

    def visited(distance, side, reach, origin):
        place = origin + jnp.where(side == 0, -distance, distance)
        inside = (distance >= 0) & (distance < reach) & (place >= 0) & (place < reach)
        return place, inside & jnp.logical_or(distance > 0, side == 0)

    def other_columns(body):
        if grid_fast == 2:
            body(1 - y)
            return
        def one(i, carry):
            yy, valid = visited(i // 2 + 1, lax.rem(i, 2), grid_fast, y)
            @pl.when(valid)
            def _():
                body(yy)
            return carry
        lax.fori_loop(0, 2 * (grid_fast - 1), one, 0)

    def along(zz, piece, side, act):
        each((2, 3, 0, 1, 4), (yes, yes, side == 1, side == 0, yes), zz, y, piece, False, act)

    def across(zz, yy, piece, act):
        each((2, 3, 4), (yy > y, yy < y, yes), zz, yy, piece, False, act)

    def receive(zz, yy, piece):
        arrived(zz, yy, core, piece)
        across(zz, yy, piece, start)

    farthest = jnp.where(2 * z >= grid_slow, 0, grid_slow - 1)

    def event(e, carry):
        distance = e // (2 * PIECES)
        piece = lax.rem(e // 2, PIECES)
        side = lax.rem(e, 2)
        half = piece // group

        @pl.when(e == 2 * PIECES * grid_slow)
        def _():
            for p in range(PIECES):
                each((2, 3, 0, 1, 4), (yes,) * 5, z, y, p, True, finish)

        zz, valid = visited(distance, side, grid_slow, z)
        @pl.when(valid & (distance > 0))
        def _():
            arrived(zz, y, core, piece)
            along(zz, piece, side, start)

        z1, valid1 = visited(distance - 1, side, grid_slow, z)
        z2, valid2 = visited(distance - 2, side, grid_slow, z)
        @pl.when(valid2)
        def _():
            other_columns(lambda yy: receive(z2, yy, piece))
            @pl.when(distance > 2)
            def _():
                along(z2, piece, side, finish)

        z3, valid3 = visited(distance - 3, side, grid_slow, z)
        @pl.when(valid3)
        def _():
            other_columns(lambda yy: across(z3, yy, piece, finish))

        near = valid1 & (lax.rem(piece, group) == 0)
        if grid_fast == 2:
            far = valid2 & (lax.rem(piece, group) == group - 1) & (z2 != farthest)
            @pl.when(near | far)
            def _():
                def one(i, carry):
                    @pl.when(jnp.where(i == 0, near, far))
                    def _():
                        meet(jnp.where(i == 0, z1, z2), jnp.where(i == 0, y, 1 - y), half)
                    return carry
                lax.fori_loop(0, 2, one, 0)
        else:
            @pl.when(near)
            def _():
                meet(z1, y, half)
            @pl.when(valid2 & (lax.rem(piece, group) == group - 1))
            def _():
                other_columns(lambda yy: meet(z2, yy, half))
        return carry

    lax.fori_loop(0, 2 * PIECES * (grid_slow + 2), event, 0)
    if grid_fast == 2:
        def last_pair(i, carry):
            cc = jnp.where(i == 0, core, 1 - core)
            @pl.when(i == 1)
            def _():
                for p in range(PIECES):
                    arrived(farthest, 1 - y, 1 - core, p)
            compute_core(farthest, 1 - y, cc)
            return carry
        lax.fori_loop(0, CORES, last_pair, 0)

    total = row_total[...]
    density = row_max[...] + jnp.log(total)
    dens_ref[...] = jnp.transpose(jnp.broadcast_to(density, (rows, rows)))[:1, :]
    mean_ref[...] = (acc[...] / total).astype(mean_ref.dtype)

    for e in range(2 * PIECES):
        last, valid = visited(grid_slow - 1, e % 2, grid_slow, z)
        @pl.when(valid)
        def _():
            other_columns(lambda yy: across(last, yy, e // 2, finish))


def folded_kernel(
    planes, x_ref, lab_ref, dens_ref, mean_ref,
    buf, labs, acc, row_max, row_total,
    send_sem, recv_sem, pair_sem, lsend_sem, lrecv_sem, own_sem,
):
    rows, width = x_ref.shape
    half_rows = rows // 2
    keys = CORES * rows
    me = lax.axis_index("docs")
    core = lax.rem(me, CORES)
    y = lax.rem(me // CORES, 2)
    z = me // (CORES * 2)
    mirrored = 2 * z >= planes
    end = (z == 0) | (z == planes - 1)
    mid = jnp.logical_not(end)
    home = jnp.where(end, 0, 1)

    def chip(k, other):
        zz = jnp.where(mirrored, planes - 1 - k, k)
        return zz * 2 + (1 - y if other is True else y if other is False else jnp.where(other == 1, 1 - y, y))

    def device(k, other, cc):
        return chip(k, other) * CORES + cc

    OUT, IN, SIDE, PAIR = range(4)
    targets = (
        device(0, False, core),
        device(home + 1, False, core),
        device(home, True, core),
        device(home, False, 1 - core),
    )

    barrier = pltpu.get_barrier_semaphore()
    for direction, target in enumerate(targets):
        @pl.when((direction != OUT) | mid)
        def _():
            pl.semaphore_signal(barrier, inc=1, device_id={"docs": target}, device_id_type=MESH)

    own_data = pltpu.make_async_copy(x_ref, buf.at[pl.ds(pl.multiple_of(me * rows, rows), rows)], own_sem.at[0])
    own_data.start()
    own_lab = pltpu.make_async_copy(lab_ref, labs.at[me], own_sem.at[1])
    own_lab.start()
    pl.semaphore_wait(barrier, jnp.where(mid, 4, 3))

    def rows_of(slot, half):
        if half is None:
            return buf.at[pl.ds(pl.multiple_of(slot * rows, rows), rows)]
        return buf.at[pl.ds(pl.multiple_of(slot * rows + half * half_rows, half_rows), half_rows)]

    def data_copy(direction, k, other, half, own=False):
        slot = device(k, other, core)
        place = rows_of(slot, half)
        if own:
            source = x_ref if half is None else x_ref.at[pl.ds(half * half_rows, half_rows)]
        else:
            source = place
        if direction == PAIR:
            done = pair_sem.at[chip(k, other)]
        else:
            done = recv_sem.at[chip(k, other) * 2 + half]
        return pltpu.make_async_remote_copy(
            source, place, send_sem.at[direction], done,
            device_id={"docs": targets[direction]}, device_id_type=MESH,
        )

    def lab_copy(direction, k, other, own=False):
        slot = device(k, other, core)
        return pltpu.make_async_remote_copy(
            lab_ref if own else labs.at[slot], labs.at[slot],
            lsend_sem.at[0], lrecv_sem.at[slot],
            device_id={"docs": targets[direction]}, device_id_type=MESH,
        )

    def send(k, other, half, directions):
        for direction in directions:
            if half != 1:
                lab_copy(direction, k, other).start()
            data_copy(direction, k, other, half).start()

    def arrived(k, other, half):
        if half == 0:
            lab_copy(SIDE, k, other).wait_recv()
        data_copy(SIDE, k, other, half).wait_recv()

    def pass_on(k, other, half, directions):
        arrived(k, other, half)
        send(k, other, half, directions)

    for half in range(2):
        for direction in (SIDE, OUT, IN):
            def _():
                if half == 0:
                    lab_copy(direction, home, False, own=True).start()
                data_copy(direction, home, False, half, own=True).start()
            if direction == OUT:
                pl.when(mid)(_)
            else:
                _()
    lab_copy(PAIR, home, False, own=True).start()
    data_copy(PAIR, home, False, None, own=True).start()

    row_max[...] = jnp.full_like(row_max, neg_large)
    row_total[...] = jnp.zeros_like(row_total)
    acc[...] = jnp.zeros_like(acc)
    own_lab.wait()
    label_column = jnp.transpose(
        jnp.broadcast_to(labs[me].astype(jnp.float32), (rows, rows))
    )[:, :1]
    gap = lax.broadcasted_iota(jnp.int32, (rows, keys), 1) - lax.broadcasted_iota(jnp.int32, (rows, keys), 0)
    own_data.wait()

    def pick(i, values):
        return sum(jnp.where(i == j, value, 0) for j, value in enumerate(values) if value)

    def step(i, carry):
        k = jnp.where(end, pick(i, (0, 1, 0, 2, 1, 3, 2, 3)), pick(i, (1, 2, 0, 1, 3, 0, 2, 3)))
        other = jnp.where(end, pick(i, (0, 0, 1, 0, 1, 0, 1, 1)), pick(i, (0, 0, 0, 1, 0, 1, 1, 1)))

        @pl.when(end & (i == 1))
        def _():
            pass_on(1, False, 0, (SIDE,))
            pass_on(0, True, 0, (IN,))
            pass_on(1, False, 1, (SIDE,))
            send(1, False, None, (PAIR,))
            pass_on(0, True, 1, (IN,))
            send(0, True, None, (PAIR,))

        @pl.when(end & (i == 3))
        def _():
            pass_on(2, False, 0, (SIDE,))
            pass_on(2, False, 1, (SIDE,))
            send(2, False, None, (PAIR,))
            arrived(1, True, 0)
            arrived(1, True, 1)
            send(1, True, None, (PAIR,))

        @pl.when(end & (i == 5))
        def _():
            pass_on(3, False, 0, (SIDE,))
            arrived(3, False, 1)
            send(3, False, None, (PAIR,))
            arrived(2, True, 0)
            arrived(2, True, 1)
            send(2, True, None, (PAIR,))

        @pl.when(mid & (i == 1))
        def _():
            pass_on(2, False, 0, (OUT, SIDE))
            pass_on(0, False, 0, (IN,))
            pass_on(2, False, 1, (OUT, SIDE))
            send(2, False, None, (PAIR,))
            pass_on(0, False, 1, (IN,))
            send(0, False, None, (PAIR,))
            arrived(1, True, 0)
            arrived(1, True, 1)
            send(1, True, None, (PAIR,))

        @pl.when(mid & (i == 3))
        def _():
            pass_on(3, False, 0, (OUT,))

        @pl.when(mid & (i == 4))
        def _():
            pass_on(3, False, 1, (OUT, SIDE))
            send(3, False, 0, (SIDE,))
            send(3, False, None, (PAIR,))
            arrived(0, True, 0)
            arrived(0, True, 1)
            send(0, True, None, (PAIR,))
            arrived(2, True, 0)
            arrived(2, True, 1)
            send(2, True, None, (PAIR,))

        @pl.when(i == 7)
        def _():
            arrived(3, True, 1)
            @pl.when(mid)
            def _():
                send(3, True, 1, (OUT,))
            send(3, True, 1, (PAIR,))
            arrived(3, True, 0)
            send(3, True, 0, (PAIR,))

        where = chip(k, other)
        theirs = where * CORES + 1 - core
        pltpu.make_async_remote_copy(
            labs.at[theirs], labs.at[theirs], lsend_sem.at[0], lrecv_sem.at[theirs],
            device_id={"docs": targets[PAIR]}, device_id_type=MESH,
        ).wait_recv()
        pltpu.make_async_remote_copy(
            rows_of(theirs, None), rows_of(theirs, None), send_sem.at[PAIR], pair_sem.at[where],
            device_id={"docs": targets[PAIR]}, device_id_type=MESH,
        ).wait_recv()

        values = buf[pl.ds(pl.multiple_of(where * keys, keys), keys), :]
        tags = jnp.concatenate([labs[where * CORES + cc].astype(jnp.float32) for cc in range(CORES)], axis=1)
        mine = buf[pl.ds(pl.multiple_of(me * rows, rows), rows), :]
        scores = lax.dot_general(
            mine, values, (((1,), (1,)), ((), ())), preferred_element_type=jnp.float32
        ) * (kernel_gain / math.sqrt(width))
        near = (label_column == tags) & (gap != jnp.where(i == 0, core * rows, keys))
        masked = jnp.where(near, scores, neg_large)
        before = row_max[...]
        peak = jnp.maximum(before, jnp.max(masked, axis=1, keepdims=True))
        weights = jnp.where(near, jnp.exp(masked - peak), 0.0)
        scale = jnp.exp(before - peak)
        row_max[...] = peak
        row_total[...] = row_total[...] * scale + jnp.sum(weights, axis=1, keepdims=True)
        acc[...] = acc[...] * scale + jnp.dot(
            weights.astype(jnp.bfloat16), values, preferred_element_type=jnp.float32
        )
        return carry

    lax.fori_loop(0, 2 * planes, step, 0)

    total = row_total[...]
    density = row_max[...] + jnp.log(total)
    dens_ref[...] = jnp.transpose(jnp.broadcast_to(density, (rows, rows)))[:1, :]
    mean_ref[...] = (acc[...] / total).astype(mean_ref.dtype)

    def sent(direction, halves):
        amount = buf.at[pl.ds(0, halves * half_rows)]
        pltpu.make_async_remote_copy(
            amount, amount, send_sem.at[direction], pair_sem.at[0],
            device_id={"docs": targets[direction]}, device_id_type=MESH,
        ).wait_send()

    def labs_sent(count):
        amount = labs.at[pl.ds(0, count)]
        pltpu.make_async_remote_copy(
            amount, amount, lsend_sem.at[0], lrecv_sem.at[0],
            device_id={"docs": targets[PAIR]}, device_id_type=MESH,
        ).wait_send()

    @pl.when(end)
    def _():
        sent(IN, 4)
        sent(SIDE, 7)
        sent(PAIR, 16)
        labs_sent(14)

    @pl.when(mid)
    def _():
        sent(OUT, 7)
        sent(IN, 4)
        sent(SIDE, 6)
        sent(PAIR, 16)
        labs_sent(16)


def general_call(device_count, rows, width):
    grid_slow, grid_fast = chip_grid(device_count)
    chips = device_count // CORES
    vmem = pl.BlockSpec(memory_space=pltpu.VMEM)
    return pl.pallas_call(
        functools.partial(kernel, grid_slow, grid_fast),
        out_shape=(
            pltpu.VMEM((1, rows), jnp.float32),
            pltpu.VMEM((rows, width), jnp.bfloat16),
        ),
        in_specs=[pl.BlockSpec(memory_space=pl.ANY), pl.BlockSpec(memory_space=pl.ANY)],
        out_specs=(vmem, vmem),
        scratch_shapes=[
            pltpu.VMEM((device_count * rows, width), jnp.bfloat16),
            pltpu.VMEM((device_count, 1, rows), jnp.int32),
            pltpu.VMEM((rows, width), jnp.bfloat16),
            pltpu.VMEM((rows, width), jnp.float32),
            pltpu.VMEM((rows, 1), jnp.float32),
            pltpu.VMEM((rows, 1), jnp.float32),
            pltpu.SemaphoreType.DMA((5, chips * PIECES)),
            pltpu.SemaphoreType.DMA((device_count * PIECES,)),
            pltpu.SemaphoreType.DMA((5, chips)),
            pltpu.SemaphoreType.DMA((device_count,)),
            pltpu.SemaphoreType.DMA((PIECES + 1,)),
            pltpu.SemaphoreType.DMA((1,)),
        ],
        compiler_params=pltpu.CompilerParams(collective_id=0, has_side_effects=True),
    )


def folded_call(device_count, rows, width):
    chips = device_count // CORES
    vmem = pl.BlockSpec(memory_space=pltpu.VMEM)
    return pl.pallas_call(
        functools.partial(folded_kernel, chips // 2),
        out_shape=(
            pltpu.VMEM((1, rows), jnp.float32),
            pltpu.VMEM((rows, width), jnp.bfloat16),
        ),
        in_specs=[pl.BlockSpec(memory_space=pl.ANY), pl.BlockSpec(memory_space=pl.ANY)],
        out_specs=(vmem, vmem),
        scratch_shapes=[
            pltpu.VMEM((device_count * rows, width), jnp.bfloat16),
            pltpu.VMEM((device_count, 1, rows), jnp.int32),
            pltpu.VMEM((rows, width), jnp.float32),
            pltpu.VMEM((rows, 1), jnp.float32),
            pltpu.VMEM((rows, 1), jnp.float32),
            pltpu.SemaphoreType.DMA((4,)),
            pltpu.SemaphoreType.DMA((2 * chips,)),
            pltpu.SemaphoreType.DMA((chips,)),
            pltpu.SemaphoreType.DMA((1,)),
            pltpu.SemaphoreType.DMA((device_count,)),
            pltpu.SemaphoreType.DMA((2,)),
        ],
        compiler_params=pltpu.CompilerParams(collective_id=0, has_side_effects=True),
    )


def per_device(device_count, embeddings, labels, row_slot):
    rows, width = embeddings.shape
    call = folded_call if chip_grid(device_count) == FOLDED_GRID else general_call
    density, mean = call(device_count, rows, width)(embeddings, labels.reshape(1, rows))
    return density.reshape(rows), mean


def solution(mesh):
    return jax.shard_map(
        functools.partial(per_device, mesh.shape["docs"]),
        mesh=mesh,
        in_specs=(P(("groups", "docs"), None), P(("groups", "docs")), P(("groups", "docs"))),
        out_specs=(P(("groups", "docs")), P(("groups", "docs"), None)),
        check_vma=False,
    )
```

```python
import functools
import math

import jax
import jax.numpy as jnp
from jax import lax
from jax.experimental import pallas as pl
from jax.experimental.pallas import tpu as pltpu
from jax.sharding import PartitionSpec as P

MESH = pl.DeviceIdType.MESH
CORES = 2
PIECES = 2
HALVES = 1
FOLDED_GRID = (4, 2)

neg_large = -1e30
kernel_gain = 4.0


def chip_grid(device_count):
    chips = device_count // CORES
    fast = 1
    while (2 * fast) * (2 * fast) <= chips and chips % (2 * fast) == 0:
        fast *= 2
    return chips // fast, fast


def kernel(
    grid_slow, grid_fast, x_ref, lab_ref, dens_ref, mean_ref,
    buf, labs, mine, acc, row_max, row_total,
    send_sem, recv_sem, lsend_sem, lrecv_sem, own_sem, own_lab_sem,
):
    rows, width = x_ref.shape
    part = rows // PIECES
    group = PIECES // HALVES
    half_rows = rows // HALVES
    keys = CORES * half_rows
    me = lax.axis_index("docs")
    core = lax.rem(me, CORES)
    chip = me // CORES
    y = lax.rem(chip, grid_fast)
    z = chip // grid_fast

    def device(zz, yy, cc):
        return (zz * grid_fast + yy) * CORES + cc

    targets = (
        (z > 0, device(z - 1, y, core)),
        (z < grid_slow - 1, device(z + 1, y, core)),
        (y > 0, device(z, y - 1, core)),
        (y < grid_fast - 1, device(z, y + 1, core)),
        (z >= 0, device(z, y, 1 - core)),
    )

    barrier = pltpu.get_barrier_semaphore()
    for there, target in targets:
        @pl.when(there)
        def _():
            pl.semaphore_signal(barrier, inc=1, device_id={"docs": target}, device_id_type=MESH)

    def data_of(zz, yy, cc, piece):
        where = ((zz * grid_fast + yy) * HALVES + piece // group) * CORES + cc
        return buf.at[pl.ds(pl.multiple_of((where * group + lax.rem(piece, group)) * part, part), part)]

    own_copies = [pltpu.make_async_copy(x_ref, mine, own_sem.at[PIECES])]
    for piece in range(PIECES):
        own_copies.append(
            pltpu.make_async_copy(
                x_ref.at[pl.ds(piece * part, part)], data_of(z, y, core, piece), own_sem.at[piece]
            )
        )
    own_copies.append(pltpu.make_async_copy(lab_ref, labs.at[me], own_lab_sem.at[0]))
    for copy in own_copies:
        copy.start()
    pl.semaphore_wait(barrier, sum(there.astype(jnp.int32) for there, _ in targets))

    def data_copy(direction, zz, yy, piece, own):
        data = data_of(zz, yy, core, piece)
        return pltpu.make_async_remote_copy(
            x_ref.at[pl.ds(piece * part, part)] if own else data, data,
            send_sem.at[direction, (zz * grid_fast + yy) * PIECES + piece],
            recv_sem.at[device(zz, yy, core) * PIECES + piece],
            device_id={"docs": targets[direction][1]}, device_id_type=MESH,
        )

    def lab_copy(direction, zz, yy, own):
        slot = device(zz, yy, core)
        return pltpu.make_async_remote_copy(
            lab_ref if own else labs.at[slot], labs.at[slot],
            lsend_sem.at[direction, zz * grid_fast + yy], lrecv_sem.at[slot],
            device_id={"docs": targets[direction][1]}, device_id_type=MESH,
        )

    def each(directions, wanted, zz, yy, piece, own, act):
        for direction, want in zip(directions, wanted):
            @pl.when(jnp.logical_and(targets[direction][0], want))
            def _():
                @pl.when(piece == 0)
                def _():
                    act(lab_copy(direction, zz, yy, own))
                act(data_copy(direction, zz, yy, piece, own))

    start = lambda copy: copy.start()
    finish = lambda copy: copy.wait_send()

    def arrived(zz, yy, cc, piece):
        slot = device(zz, yy, cc)
        @pl.when(piece == 0)
        def _():
            pltpu.make_async_remote_copy(
                labs.at[slot], labs.at[slot], lsend_sem.at[0, 0], lrecv_sem.at[slot],
                device_id={"docs": targets[4][1]}, device_id_type=MESH,
            ).wait_recv()
        data = data_of(zz, yy, cc, piece)
        pltpu.make_async_remote_copy(
            data, data, send_sem.at[0, 0], recv_sem.at[slot * PIECES + piece],
            device_id={"docs": targets[4][1]}, device_id_type=MESH,
        ).wait_recv()

    yes = z >= 0
    for piece in range(PIECES):
        each((2, 3, 0, 1, 4), (yes,) * 5, z, y, piece, True, start)

    row_max[...] = jnp.full_like(row_max, neg_large)
    row_total[...] = jnp.zeros_like(row_total)
    acc[...] = jnp.zeros_like(acc)
    own_copies[-1].wait()
    label_column = jnp.transpose(
        jnp.broadcast_to(labs[me].astype(jnp.float32), (rows, rows))
    )[:, :1]
    column = lax.broadcasted_iota(jnp.int32, (rows, keys), 1)
    gap = (
        column + (column // half_rows) * (rows - half_rows)
        - lax.broadcasted_iota(jnp.int32, (rows, keys), 0)
    )
    for copy in own_copies[:-1]:
        copy.wait()

    def compute(zz, yy, half):
        where = zz * grid_fast + yy
        values = buf[pl.ds(pl.multiple_of((where * HALVES + half) * keys, keys), keys), :]
        tags = []
        for cc in range(CORES):
            tag = labs[where * CORES + cc].astype(jnp.float32)
            pieces = [tag[:, h * half_rows:(h + 1) * half_rows] for h in range(HALVES)]
            picked = pieces[0]
            for h in range(1, HALVES):
                picked = jnp.where(half == h, pieces[h], picked)
            tags.append(picked)
        tags = jnp.concatenate(tags, axis=1)
        scores = lax.dot_general(
            mine[...], values, (((1,), (1,)), ((), ())), preferred_element_type=jnp.float32
        ) * (kernel_gain / math.sqrt(width))
        self_gap = jnp.where(where == chip, core * rows - half * half_rows, CORES * rows)
        absorb(scores, (label_column == tags) & (gap != self_gap), values)

    def compute_core(zz, yy, cc):
        slot = device(zz, yy, cc)
        values = buf[pl.ds(pl.multiple_of(slot * rows, rows), rows), :]
        scores = lax.dot_general(
            mine[...], values, (((1,), (1,)), ((), ())), preferred_element_type=jnp.float32
        ) * (kernel_gain / math.sqrt(width))
        absorb(scores, label_column == labs[slot].astype(jnp.float32), values)

    def absorb(scores, near, values):
        masked = jnp.where(near, scores, neg_large)
        before = row_max[...]
        peak = jnp.maximum(before, jnp.max(masked, axis=1, keepdims=True))
        weights = jnp.where(near, jnp.exp(masked - peak), 0.0)
        scale = jnp.exp(before - peak)
        row_max[...] = peak
        row_total[...] = row_total[...] * scale + jnp.sum(weights, axis=1, keepdims=True)
        acc[...] = acc[...] * scale + jnp.dot(
            weights.astype(jnp.bfloat16), values, preferred_element_type=jnp.float32
        )

    def meet(zz, yy, half):
        def one(p, carry):
            arrived(zz, yy, 1 - core, half * group + p)
            return carry
        lax.fori_loop(0, group, one, 0)
        compute(zz, yy, half)

    def visited(distance, side, reach, origin):
        place = origin + jnp.where(side == 0, -distance, distance)
        inside = (distance >= 0) & (distance < reach) & (place >= 0) & (place < reach)
        return place, inside & jnp.logical_or(distance > 0, side == 0)

    def other_columns(body):
        if grid_fast == 2:
            body(1 - y)
            return
        def one(i, carry):
            yy, valid = visited(i // 2 + 1, lax.rem(i, 2), grid_fast, y)
            @pl.when(valid)
            def _():
                body(yy)
            return carry
        lax.fori_loop(0, 2 * (grid_fast - 1), one, 0)

    def along(zz, piece, side, act):
        each((2, 3, 0, 1, 4), (yes, yes, side == 1, side == 0, yes), zz, y, piece, False, act)

    def across(zz, yy, piece, act):
        each((2, 3, 4), (yy > y, yy < y, yes), zz, yy, piece, False, act)

    def receive(zz, yy, piece):
        arrived(zz, yy, core, piece)
        across(zz, yy, piece, start)

    farthest = jnp.where(2 * z >= grid_slow, 0, grid_slow - 1)

    def event(e, carry):
        distance = e // (2 * PIECES)
        piece = lax.rem(e // 2, PIECES)
        side = lax.rem(e, 2)
        half = piece // group

        @pl.when(e == 2 * PIECES * grid_slow)
        def _():
            for p in range(PIECES):
                each((2, 3, 0, 1, 4), (yes,) * 5, z, y, p, True, finish)

        zz, valid = visited(distance, side, grid_slow, z)
        @pl.when(valid & (distance > 0))
        def _():
            arrived(zz, y, core, piece)
            along(zz, piece, side, start)

        z1, valid1 = visited(distance - 1, side, grid_slow, z)
        z2, valid2 = visited(distance - 2, side, grid_slow, z)
        @pl.when(valid2)
        def _():
            other_columns(lambda yy: receive(z2, yy, piece))
            @pl.when(distance > 2)
            def _():
                along(z2, piece, side, finish)

        z3, valid3 = visited(distance - 3, side, grid_slow, z)
        @pl.when(valid3)
        def _():
            other_columns(lambda yy: across(z3, yy, piece, finish))

        near = valid1 & (lax.rem(piece, group) == 0)
        if grid_fast == 2:
            far = valid2 & (lax.rem(piece, group) == group - 1) & (z2 != farthest)
            @pl.when(near | far)
            def _():
                def one(i, carry):
                    @pl.when(jnp.where(i == 0, near, far))
                    def _():
                        meet(jnp.where(i == 0, z1, z2), jnp.where(i == 0, y, 1 - y), half)
                    return carry
                lax.fori_loop(0, 2, one, 0)
        else:
            @pl.when(near)
            def _():
                meet(z1, y, half)
            @pl.when(valid2 & (lax.rem(piece, group) == group - 1))
            def _():
                other_columns(lambda yy: meet(z2, yy, half))
        return carry

    lax.fori_loop(0, 2 * PIECES * (grid_slow + 2), event, 0)
    if grid_fast == 2:
        def last_pair(i, carry):
            cc = jnp.where(i == 0, core, 1 - core)
            @pl.when(i == 1)
            def _():
                for p in range(PIECES):
                    arrived(farthest, 1 - y, 1 - core, p)
            compute_core(farthest, 1 - y, cc)
            return carry
        lax.fori_loop(0, CORES, last_pair, 0)

    total = row_total[...]
    density = row_max[...] + jnp.log(total)
    dens_ref[...] = jnp.transpose(jnp.broadcast_to(density, (rows, rows)))[:1, :]
    mean_ref[...] = (acc[...] / total).astype(mean_ref.dtype)

    for e in range(2 * PIECES):
        last, valid = visited(grid_slow - 1, e % 2, grid_slow, z)
        @pl.when(valid)
        def _():
            other_columns(lambda yy: across(last, yy, e // 2, finish))


def folded_kernel(
    planes, x_ref, lab_ref, dens_ref, mean_ref,
    buf, labs, acc, row_max, row_total,
    send_sem, recv_sem, pair_sem, lsend_sem, lrecv_sem, own_sem, ready_sem,
):
    rows, width = x_ref.shape
    half_rows = rows // 2
    keys = CORES * rows
    me = lax.axis_index("docs")
    core = lax.rem(me, CORES)
    y = lax.rem(me // CORES, 2)
    z = me // (CORES * 2)
    mirrored = 2 * z >= planes
    end = (z == 0) | (z == planes - 1)
    mid = jnp.logical_not(end)
    home = jnp.where(end, 0, 1)

    def chip(k, other):
        zz = jnp.where(mirrored, planes - 1 - k, k)
        return zz * 2 + (1 - y if other is True else y if other is False else jnp.where(other == 1, 1 - y, y))

    def device(k, other, cc):
        return chip(k, other) * CORES + cc

    OUT, IN, SIDE, PAIR = range(4)
    AXIS = (0, 0, 1, 2)
    targets = (
        device(0, False, core),
        device(home + 1, False, core),
        device(home, True, core),
        device(home, False, 1 - core),
    )

    up = (mid & mirrored, jnp.logical_not(mirrored), y == 0, core == 0)
    down = (mid & jnp.logical_not(mirrored), mirrored, y == 1, core == 1)
    barrier = pltpu.get_barrier_semaphore()
    for target, higher in zip(targets, up):
        @pl.when(higher)
        def _():
            pl.semaphore_signal(barrier, inc=1, device_id={"docs": target}, device_id_type=MESH)

    own_data = pltpu.make_async_copy(x_ref, buf.at[pl.ds(pl.multiple_of(me * rows, rows), rows)], own_sem.at[0])
    own_data.start()
    own_lab = pltpu.make_async_copy(lab_ref, labs.at[me], own_sem.at[1])
    own_lab.start()
    lower_count = sum(lower.astype(jnp.int32) for lower in down)
    @pl.when(lower_count > 0)
    def _():
        pl.semaphore_wait(barrier, lower_count)
    for direction, lower in enumerate(down):
        @pl.when(lower)
        def _():
            pl.semaphore_signal(
                ready_sem.at[AXIS[direction]], inc=1,
                device_id={"docs": targets[direction]}, device_id_type=MESH,
            )

    def rows_of(slot, half):
        if half is None:
            return buf.at[pl.ds(pl.multiple_of(slot * rows, rows), rows)]
        return buf.at[pl.ds(pl.multiple_of(slot * rows + half * half_rows, half_rows), half_rows)]

    def data_copy(direction, k, other, half, own=False):
        slot = device(k, other, core)
        place = rows_of(slot, half)
        if own:
            source = x_ref if half is None else x_ref.at[pl.ds(half * half_rows, half_rows)]
        else:
            source = place
        if direction == PAIR:
            done = pair_sem.at[chip(k, other)]
        else:
            done = recv_sem.at[chip(k, other) * 2 + half]
        return pltpu.make_async_remote_copy(
            source, place, send_sem.at[direction], done,
            device_id={"docs": targets[direction]}, device_id_type=MESH,
        )

    def lab_copy(direction, k, other, own=False):
        slot = device(k, other, core)
        return pltpu.make_async_remote_copy(
            lab_ref if own else labs.at[slot], labs.at[slot],
            lsend_sem.at[0], lrecv_sem.at[slot],
            device_id={"docs": targets[direction]}, device_id_type=MESH,
        )

    def send(k, other, half, directions):
        for direction in directions:
            if half != 1:
                lab_copy(direction, k, other).start()
            data_copy(direction, k, other, half).start()

    def arrived(k, other, half):
        if half == 0:
            lab_copy(SIDE, k, other).wait_recv()
        data_copy(SIDE, k, other, half).wait_recv()

    def pass_on(k, other, half, directions):
        arrived(k, other, half)
        send(k, other, half, directions)

    def start_own(direction):
        lab_copy(direction, home, False, own=True).start()
        for half in {SIDE: (1, 0), PAIR: (None,)}.get(direction, (0, 1)):
            data_copy(direction, home, False, half, own=True).start()

    for direction, lower in enumerate(down):
        @pl.when(lower)
        def _():
            start_own(direction)
    for direction, higher in reversed(tuple(enumerate(up))):
        @pl.when(higher)
        def _():
            pl.semaphore_wait(ready_sem.at[AXIS[direction]], 1)
            start_own(direction)

    row_max[...] = jnp.full_like(row_max, neg_large)
    row_total[...] = jnp.zeros_like(row_total)
    acc[...] = jnp.zeros_like(acc)
    own_lab.wait()
    label_column = jnp.transpose(
        jnp.broadcast_to(labs[me].astype(jnp.float32), (rows, rows))
    )[:, :1]
    gap = lax.broadcasted_iota(jnp.int32, (rows, keys), 1) - lax.broadcasted_iota(jnp.int32, (rows, keys), 0)
    own_data.wait()

    def pick(i, values):
        return sum(jnp.where(i == j, value, 0) for j, value in enumerate(values) if value)

    def step(i, carry):
        k = jnp.where(end, pick(i, (0, 1, 0, 2, 1, 3, 2, 3)), pick(i, (1, 2, 0, 1, 3, 0, 2, 3)))
        other = jnp.where(end, pick(i, (0, 0, 1, 0, 1, 0, 1, 1)), pick(i, (0, 0, 0, 1, 0, 1, 1, 1)))

        @pl.when(end & (i == 1))
        def _():
            pass_on(1, False, 0, (SIDE,))
            pass_on(0, True, 1, (IN,))
            pass_on(1, False, 1, (SIDE,))
            send(1, False, None, (PAIR,))
            pass_on(0, True, 0, (IN,))
            send(0, True, None, (PAIR,))

        @pl.when(end & (i == 3))
        def _():
            pass_on(2, False, 0, (SIDE,))
            pass_on(2, False, 1, (SIDE,))
            send(2, False, None, (PAIR,))
            arrived(1, True, 0)
            arrived(1, True, 1)
            send(1, True, None, (PAIR,))

        @pl.when(end & (i == 5))
        def _():
            pass_on(3, False, 0, (SIDE,))
            arrived(3, False, 1)
            send(3, False, None, (PAIR,))
            arrived(2, True, 0)
            arrived(2, True, 1)
            send(2, True, None, (PAIR,))

        @pl.when(mid & (i == 1))
        def _():
            pass_on(2, False, 0, (OUT, SIDE))
            pass_on(0, False, 0, (IN,))
            pass_on(2, False, 1, (OUT, SIDE))
            send(2, False, None, (PAIR,))
            pass_on(0, False, 1, (IN,))
            send(0, False, None, (PAIR,))
            arrived(1, True, 0)
            arrived(1, True, 1)
            send(1, True, None, (PAIR,))

        @pl.when(mid & (i == 3))
        def _():
            pass_on(3, False, 0, (OUT, SIDE))
            pass_on(0, True, 1, (IN,))

        @pl.when(mid & (i == 4))
        def _():
            pass_on(3, False, 1, (OUT,))
            send(3, False, None, (PAIR,))
            arrived(0, True, 0)
            send(0, True, None, (PAIR,))
            arrived(2, True, 0)
            arrived(2, True, 1)
            send(2, True, None, (PAIR,))

        @pl.when(i == 7)
        def _():
            arrived(3, True, 1)
            @pl.when(mid)
            def _():
                send(3, True, 1, (OUT,))
            send(3, True, 1, (PAIR,))
            arrived(3, True, 0)
            send(3, True, 0, (PAIR,))

        where = chip(k, other)
        theirs = where * CORES + 1 - core
        pltpu.make_async_remote_copy(
            labs.at[theirs], labs.at[theirs], lsend_sem.at[0], lrecv_sem.at[theirs],
            device_id={"docs": targets[PAIR]}, device_id_type=MESH,
        ).wait_recv()
        pltpu.make_async_remote_copy(
            rows_of(theirs, None), rows_of(theirs, None), send_sem.at[PAIR], pair_sem.at[where],
            device_id={"docs": targets[PAIR]}, device_id_type=MESH,
        ).wait_recv()

        values = buf[pl.ds(pl.multiple_of(where * keys, keys), keys), :]
        tags = jnp.concatenate([labs[where * CORES + cc].astype(jnp.float32) for cc in range(CORES)], axis=1)
        mine = buf[pl.ds(pl.multiple_of(me * rows, rows), rows), :]
        scores = lax.dot_general(
            mine, values, (((1,), (1,)), ((), ())), preferred_element_type=jnp.float32
        ) * (kernel_gain / math.sqrt(width))
        near = (label_column == tags) & (gap != jnp.where(i == 0, core * rows, keys))
        masked = jnp.where(near, scores, neg_large)
        before = row_max[...]
        peak = jnp.maximum(before, jnp.max(masked, axis=1, keepdims=True))
        weights = jnp.where(near, jnp.exp(masked - peak), 0.0)
        scale = jnp.exp(before - peak)
        row_max[...] = peak
        row_total[...] = row_total[...] * scale + jnp.sum(weights, axis=1, keepdims=True)
        acc[...] = acc[...] * scale + jnp.dot(
            weights.astype(jnp.bfloat16), values, preferred_element_type=jnp.float32
        )
        return carry

    lax.fori_loop(0, 2 * planes, step, 0)

    total = row_total[...]
    density = row_max[...] + jnp.log(total)
    dens_ref[...] = jnp.transpose(jnp.broadcast_to(density, (rows, rows)))[:1, :]
    mean_ref[...] = (acc[...] / total).astype(mean_ref.dtype)

    def sent(direction, halves):
        amount = buf.at[pl.ds(0, halves * half_rows)]
        pltpu.make_async_remote_copy(
            amount, amount, send_sem.at[direction], pair_sem.at[0],
            device_id={"docs": targets[direction]}, device_id_type=MESH,
        ).wait_send()

    def labs_sent(count):
        amount = labs.at[pl.ds(0, count)]
        pltpu.make_async_remote_copy(
            amount, amount, lsend_sem.at[0], lrecv_sem.at[0],
            device_id={"docs": targets[PAIR]}, device_id_type=MESH,
        ).wait_send()

    @pl.when(end)
    def _():
        sent(IN, 4)
        sent(SIDE, 7)
        sent(PAIR, 16)
        labs_sent(14)

    @pl.when(mid)
    def _():
        sent(OUT, 7)
        sent(IN, 5)
        sent(SIDE, 5)
        sent(PAIR, 16)
        labs_sent(16)


def general_call(device_count, rows, width):
    grid_slow, grid_fast = chip_grid(device_count)
    chips = device_count // CORES
    vmem = pl.BlockSpec(memory_space=pltpu.VMEM)
    return pl.pallas_call(
        functools.partial(kernel, grid_slow, grid_fast),
        out_shape=(
            pltpu.VMEM((1, rows), jnp.float32),
            pltpu.VMEM((rows, width), jnp.bfloat16),
        ),
        in_specs=[pl.BlockSpec(memory_space=pl.ANY), pl.BlockSpec(memory_space=pl.ANY)],
        out_specs=(vmem, vmem),
        scratch_shapes=[
            pltpu.VMEM((device_count * rows, width), jnp.bfloat16),
            pltpu.VMEM((device_count, 1, rows), jnp.int32),
            pltpu.VMEM((rows, width), jnp.bfloat16),
            pltpu.VMEM((rows, width), jnp.float32),
            pltpu.VMEM((rows, 1), jnp.float32),
            pltpu.VMEM((rows, 1), jnp.float32),
            pltpu.SemaphoreType.DMA((5, chips * PIECES)),
            pltpu.SemaphoreType.DMA((device_count * PIECES,)),
            pltpu.SemaphoreType.DMA((5, chips)),
            pltpu.SemaphoreType.DMA((device_count,)),
            pltpu.SemaphoreType.DMA((PIECES + 1,)),
            pltpu.SemaphoreType.DMA((1,)),
        ],
        compiler_params=pltpu.CompilerParams(collective_id=0, has_side_effects=True),
    )


def folded_call(device_count, rows, width):
    chips = device_count // CORES
    vmem = pl.BlockSpec(memory_space=pltpu.VMEM)
    return pl.pallas_call(
        functools.partial(folded_kernel, chips // 2),
        out_shape=(
            pltpu.VMEM((1, rows), jnp.float32),
            pltpu.VMEM((rows, width), jnp.bfloat16),
        ),
        in_specs=[pl.BlockSpec(memory_space=pl.ANY), pl.BlockSpec(memory_space=pl.ANY)],
        out_specs=(vmem, vmem),
        scratch_shapes=[
            pltpu.VMEM((device_count * rows, width), jnp.bfloat16),
            pltpu.VMEM((device_count, 1, rows), jnp.int32),
            pltpu.VMEM((rows, width), jnp.float32),
            pltpu.VMEM((rows, 1), jnp.float32),
            pltpu.VMEM((rows, 1), jnp.float32),
            pltpu.SemaphoreType.DMA((4,)),
            pltpu.SemaphoreType.DMA((2 * chips,)),
            pltpu.SemaphoreType.DMA((chips,)),
            pltpu.SemaphoreType.DMA((1,)),
            pltpu.SemaphoreType.DMA((device_count,)),
            pltpu.SemaphoreType.DMA((2,)),
            pltpu.SemaphoreType.REGULAR((3,)),
        ],
        compiler_params=pltpu.CompilerParams(collective_id=0, has_side_effects=True),
    )


def per_device(device_count, embeddings, labels, row_slot):
    rows, width = embeddings.shape
    call = folded_call if chip_grid(device_count) == FOLDED_GRID else general_call
    density, mean = call(device_count, rows, width)(embeddings, labels.reshape(1, rows))
    return density.reshape(rows), mean


def solution(mesh):
    return jax.shard_map(
        functools.partial(per_device, mesh.shape["docs"]),
        mesh=mesh,
        in_specs=(P(("groups", "docs"), None), P(("groups", "docs")), P(("groups", "docs"))),
        out_specs=(P(("groups", "docs")), P(("groups", "docs"), None)),
        check_vma=False,
    )
```

```python
import functools
import math

import jax
import jax.numpy as jnp
from jax import lax
from jax.experimental import pallas as pl
from jax.experimental.pallas import tpu as pltpu
from jax.sharding import PartitionSpec as P

MESH = pl.DeviceIdType.MESH
CORES = 2
PIECES = 2
HALVES = 1
FOLDED_GRID = (4, 2)

neg_large = -1e30
neg_start = -1e29
kernel_gain = 4.0


def chip_grid(device_count):
    chips = device_count // CORES
    fast = 1
    while (2 * fast) * (2 * fast) <= chips and chips % (2 * fast) == 0:
        fast *= 2
    return chips // fast, fast


def kernel(
    grid_slow, grid_fast, x_ref, lab_ref, dens_ref, mean_ref,
    buf, labs, mine, acc, row_max, row_total,
    send_sem, recv_sem, lsend_sem, lrecv_sem, own_sem, own_lab_sem,
):
    rows, width = x_ref.shape
    part = rows // PIECES
    group = PIECES // HALVES
    half_rows = rows // HALVES
    keys = CORES * half_rows
    me = lax.axis_index("docs")
    core = lax.rem(me, CORES)
    chip = me // CORES
    y = lax.rem(chip, grid_fast)
    z = chip // grid_fast

    def device(zz, yy, cc):
        return (zz * grid_fast + yy) * CORES + cc

    targets = (
        (z > 0, device(z - 1, y, core)),
        (z < grid_slow - 1, device(z + 1, y, core)),
        (y > 0, device(z, y - 1, core)),
        (y < grid_fast - 1, device(z, y + 1, core)),
        (z >= 0, device(z, y, 1 - core)),
    )

    barrier = pltpu.get_barrier_semaphore()
    for there, target in targets:
        @pl.when(there)
        def _():
            pl.semaphore_signal(barrier, inc=1, device_id={"docs": target}, device_id_type=MESH)

    def data_of(zz, yy, cc, piece):
        where = ((zz * grid_fast + yy) * HALVES + piece // group) * CORES + cc
        return buf.at[pl.ds(pl.multiple_of((where * group + lax.rem(piece, group)) * part, part), part)]

    own_copies = [pltpu.make_async_copy(x_ref, mine, own_sem.at[PIECES])]
    for piece in range(PIECES):
        own_copies.append(
            pltpu.make_async_copy(
                x_ref.at[pl.ds(piece * part, part)], data_of(z, y, core, piece), own_sem.at[piece]
            )
        )
    own_copies.append(pltpu.make_async_copy(lab_ref, labs.at[me], own_lab_sem.at[0]))
    for copy in own_copies:
        copy.start()
    pl.semaphore_wait(barrier, sum(there.astype(jnp.int32) for there, _ in targets))

    def data_copy(direction, zz, yy, piece, own):
        data = data_of(zz, yy, core, piece)
        return pltpu.make_async_remote_copy(
            x_ref.at[pl.ds(piece * part, part)] if own else data, data,
            send_sem.at[direction, (zz * grid_fast + yy) * PIECES + piece],
            recv_sem.at[device(zz, yy, core) * PIECES + piece],
            device_id={"docs": targets[direction][1]}, device_id_type=MESH,
        )

    def lab_copy(direction, zz, yy, own):
        slot = device(zz, yy, core)
        return pltpu.make_async_remote_copy(
            lab_ref if own else labs.at[slot], labs.at[slot],
            lsend_sem.at[direction, zz * grid_fast + yy], lrecv_sem.at[slot],
            device_id={"docs": targets[direction][1]}, device_id_type=MESH,
        )

    def each(directions, wanted, zz, yy, piece, own, act):
        for direction, want in zip(directions, wanted):
            @pl.when(jnp.logical_and(targets[direction][0], want))
            def _():
                @pl.when(piece == 0)
                def _():
                    act(lab_copy(direction, zz, yy, own))
                act(data_copy(direction, zz, yy, piece, own))

    start = lambda copy: copy.start()
    finish = lambda copy: copy.wait_send()

    def arrived(zz, yy, cc, piece):
        slot = device(zz, yy, cc)
        @pl.when(piece == 0)
        def _():
            pltpu.make_async_remote_copy(
                labs.at[slot], labs.at[slot], lsend_sem.at[0, 0], lrecv_sem.at[slot],
                device_id={"docs": targets[4][1]}, device_id_type=MESH,
            ).wait_recv()
        data = data_of(zz, yy, cc, piece)
        pltpu.make_async_remote_copy(
            data, data, send_sem.at[0, 0], recv_sem.at[slot * PIECES + piece],
            device_id={"docs": targets[4][1]}, device_id_type=MESH,
        ).wait_recv()

    yes = z >= 0
    for piece in range(PIECES):
        each((2, 3, 0, 1, 4), (yes,) * 5, z, y, piece, True, start)

    row_max[...] = jnp.full_like(row_max, neg_large)
    row_total[...] = jnp.zeros_like(row_total)
    acc[...] = jnp.zeros_like(acc)
    own_copies[-1].wait()
    label_column = jnp.transpose(
        jnp.broadcast_to(labs[me].astype(jnp.float32), (rows, rows))
    )[:, :1]
    column = lax.broadcasted_iota(jnp.int32, (rows, keys), 1)
    gap = (
        column + (column // half_rows) * (rows - half_rows)
        - lax.broadcasted_iota(jnp.int32, (rows, keys), 0)
    )
    for copy in own_copies[:-1]:
        copy.wait()

    def compute(zz, yy, half):
        where = zz * grid_fast + yy
        values = buf[pl.ds(pl.multiple_of((where * HALVES + half) * keys, keys), keys), :]
        tags = []
        for cc in range(CORES):
            tag = labs[where * CORES + cc].astype(jnp.float32)
            pieces = [tag[:, h * half_rows:(h + 1) * half_rows] for h in range(HALVES)]
            picked = pieces[0]
            for h in range(1, HALVES):
                picked = jnp.where(half == h, pieces[h], picked)
            tags.append(picked)
        tags = jnp.concatenate(tags, axis=1)
        scores = lax.dot_general(
            mine[...], values, (((1,), (1,)), ((), ())), preferred_element_type=jnp.float32
        ) * (kernel_gain / math.sqrt(width))
        self_gap = jnp.where(where == chip, core * rows - half * half_rows, CORES * rows)
        absorb(scores, (label_column == tags) & (gap != self_gap), values)

    def compute_core(zz, yy, cc):
        slot = device(zz, yy, cc)
        values = buf[pl.ds(pl.multiple_of(slot * rows, rows), rows), :]
        scores = lax.dot_general(
            mine[...], values, (((1,), (1,)), ((), ())), preferred_element_type=jnp.float32
        ) * (kernel_gain / math.sqrt(width))
        absorb(scores, label_column == labs[slot].astype(jnp.float32), values)

    def absorb(scores, near, values):
        masked = jnp.where(near, scores, neg_large)
        before = row_max[...]
        peak = jnp.maximum(before, jnp.max(masked, axis=1, keepdims=True))
        weights = jnp.where(near, jnp.exp(masked - peak), 0.0)
        scale = jnp.exp(before - peak)
        row_max[...] = peak
        row_total[...] = row_total[...] * scale + jnp.sum(weights, axis=1, keepdims=True)
        acc[...] = acc[...] * scale + jnp.dot(
            weights.astype(jnp.bfloat16), values, preferred_element_type=jnp.float32
        )

    def meet(zz, yy, half):
        def one(p, carry):
            arrived(zz, yy, 1 - core, half * group + p)
            return carry
        lax.fori_loop(0, group, one, 0)
        compute(zz, yy, half)

    def visited(distance, side, reach, origin):
        place = origin + jnp.where(side == 0, -distance, distance)
        inside = (distance >= 0) & (distance < reach) & (place >= 0) & (place < reach)
        return place, inside & jnp.logical_or(distance > 0, side == 0)

    def other_columns(body):
        if grid_fast == 2:
            body(1 - y)
            return
        def one(i, carry):
            yy, valid = visited(i // 2 + 1, lax.rem(i, 2), grid_fast, y)
            @pl.when(valid)
            def _():
                body(yy)
            return carry
        lax.fori_loop(0, 2 * (grid_fast - 1), one, 0)

    def along(zz, piece, side, act):
        each((2, 3, 0, 1, 4), (yes, yes, side == 1, side == 0, yes), zz, y, piece, False, act)

    def across(zz, yy, piece, act):
        each((2, 3, 4), (yy > y, yy < y, yes), zz, yy, piece, False, act)

    def receive(zz, yy, piece):
        arrived(zz, yy, core, piece)
        across(zz, yy, piece, start)

    farthest = jnp.where(2 * z >= grid_slow, 0, grid_slow - 1)

    def event(e, carry):
        distance = e // (2 * PIECES)
        piece = lax.rem(e // 2, PIECES)
        side = lax.rem(e, 2)
        half = piece // group

        @pl.when(e == 2 * PIECES * grid_slow)
        def _():
            for p in range(PIECES):
                each((2, 3, 0, 1, 4), (yes,) * 5, z, y, p, True, finish)

        zz, valid = visited(distance, side, grid_slow, z)
        @pl.when(valid & (distance > 0))
        def _():
            arrived(zz, y, core, piece)
            along(zz, piece, side, start)

        z1, valid1 = visited(distance - 1, side, grid_slow, z)
        z2, valid2 = visited(distance - 2, side, grid_slow, z)
        @pl.when(valid2)
        def _():
            other_columns(lambda yy: receive(z2, yy, piece))
            @pl.when(distance > 2)
            def _():
                along(z2, piece, side, finish)

        z3, valid3 = visited(distance - 3, side, grid_slow, z)
        @pl.when(valid3)
        def _():
            other_columns(lambda yy: across(z3, yy, piece, finish))

        near = valid1 & (lax.rem(piece, group) == 0)
        if grid_fast == 2:
            far = valid2 & (lax.rem(piece, group) == group - 1) & (z2 != farthest)
            @pl.when(near | far)
            def _():
                def one(i, carry):
                    @pl.when(jnp.where(i == 0, near, far))
                    def _():
                        meet(jnp.where(i == 0, z1, z2), jnp.where(i == 0, y, 1 - y), half)
                    return carry
                lax.fori_loop(0, 2, one, 0)
        else:
            @pl.when(near)
            def _():
                meet(z1, y, half)
            @pl.when(valid2 & (lax.rem(piece, group) == group - 1))
            def _():
                other_columns(lambda yy: meet(z2, yy, half))
        return carry

    lax.fori_loop(0, 2 * PIECES * (grid_slow + 2), event, 0)
    if grid_fast == 2:
        def last_pair(i, carry):
            cc = jnp.where(i == 0, core, 1 - core)
            @pl.when(i == 1)
            def _():
                for p in range(PIECES):
                    arrived(farthest, 1 - y, 1 - core, p)
            compute_core(farthest, 1 - y, cc)
            return carry
        lax.fori_loop(0, CORES, last_pair, 0)

    total = row_total[...]
    density = row_max[...] + jnp.log(total)
    dens_ref[...] = jnp.transpose(jnp.broadcast_to(density, (rows, rows)))[:1, :]
    mean_ref[...] = (acc[...] / total).astype(mean_ref.dtype)

    for e in range(2 * PIECES):
        last, valid = visited(grid_slow - 1, e % 2, grid_slow, z)
        @pl.when(valid)
        def _():
            other_columns(lambda yy: across(last, yy, e // 2, finish))


def folded_kernel(
    planes, x_ref, lab_ref, dens_ref, mean_ref,
    buf, labs, acc, row_max, row_total,
    send_sem, recv_sem, pair_sem, lsend_sem, lrecv_sem, own_sem, ready_sem,
):
    rows, width = x_ref.shape
    half_rows = rows // 2
    me = lax.axis_index("docs")
    core = lax.rem(me, CORES)
    y = lax.rem(me // CORES, 2)
    z = me // (CORES * 2)
    mirrored = 2 * z >= planes
    end = (z == 0) | (z == planes - 1)
    mid = jnp.logical_not(end)

    def device(k, column, cc):
        zz = jnp.where(mirrored, planes - 1 - k, k)
        return (zz * 2 + column) * CORES + cc

    OUT, IN, SIDE, PAIR = range(4)
    AXIS = (0, 0, 1, 2)
    home = jnp.where(end, 0, 1)
    targets = (
        device(0, y, core),
        device(home + 1, y, core),
        device(home, 1 - y, core),
        device(home, y, 1 - core),
    )
    END_ORDER = ((0, 0), (1, 0), (0, 1), (2, 0), (1, 1), (3, 0), (2, 1), (3, 1))
    MID_ORDER = ((1, 0), (2, 0), (0, 0), (3, 0), (0, 1), (1, 1), (2, 1), (3, 1))

    up = (mid & mirrored, jnp.logical_not(mirrored), y == 0, core == 0)
    down = (mid & jnp.logical_not(mirrored), mirrored, y == 1, core == 1)
    barrier = pltpu.get_barrier_semaphore()
    for target, higher in zip(targets, up):
        @pl.when(higher)
        def _():
            pl.semaphore_signal(barrier, inc=1, device_id={"docs": target}, device_id_type=MESH)

    def rows_of(slot, cc, half):
        first = (slot * CORES + cc) * rows
        if half is None:
            return buf.at[pl.ds(pl.multiple_of(first, rows), rows)]
        return buf.at[pl.ds(pl.multiple_of(first + half * half_rows, half_rows), half_rows)]

    own_data = pltpu.make_async_copy(x_ref, rows_of(0, core, None), own_sem.at[0])
    own_data.start()
    own_lab = pltpu.make_async_copy(lab_ref, labs.at[core], own_sem.at[1])
    own_lab.start()
    lower_count = sum(lower.astype(jnp.int32) for lower in down)
    @pl.when(lower_count > 0)
    def _():
        pl.semaphore_wait(barrier, lower_count)
    for direction, lower in enumerate(down):
        @pl.when(lower)
        def _():
            pl.semaphore_signal(
                ready_sem.at[AXIS[direction]], inc=1,
                device_id={"docs": targets[direction]}, device_id_type=MESH,
            )

    def data_copy(direction, slot, there, half, own=False):
        if not own:
            source = rows_of(slot, core, half)
        else:
            source = x_ref if half is None else x_ref.at[pl.ds(half * half_rows, half_rows)]
        done = pair_sem.at[there] if direction == PAIR else recv_sem.at[there * 2 + half]
        return pltpu.make_async_remote_copy(
            source, rows_of(there, core, half), send_sem.at[direction], done,
            device_id={"docs": targets[direction]}, device_id_type=MESH,
        )

    def lab_copy(direction, slot, there, own=False):
        there = there * CORES + core
        return pltpu.make_async_remote_copy(
            lab_ref if own else labs.at[slot * CORES + core], labs.at[there],
            lsend_sem.at[0], lrecv_sem.at[there],
            device_id={"docs": targets[direction]}, device_id_type=MESH,
        )

    class Role:
        def __init__(self, is_end):
            self.is_end = is_end
            self.order = END_ORDER if is_end else MID_ORDER

        def slot(self, k, other):
            return self.order.index((k, other))

        def there(self, direction, k, other):
            if direction == SIDE:
                return self.slot(k, 1 - other)
            if direction == PAIR:
                return self.slot(k, other)
            if direction == OUT:
                return END_ORDER.index((k, other))
            return MID_ORDER.index((k if self.is_end else planes - 1 - k, other))

        def send(self, k, other, half, directions, own=False):
            for direction in directions:
                slot, there = self.slot(k, other), self.there(direction, k, other)
                if half != 1:
                    lab_copy(direction, slot, there, own).start()
                data_copy(direction, slot, there, half, own).start()

        def arrived(self, k, other, half):
            slot = self.slot(k, other)
            if half == 0:
                lab_copy(SIDE, slot, slot).wait_recv()
            data_copy(SIDE, slot, slot, half).wait_recv()

        def pass_on(self, k, other, half, directions):
            self.arrived(k, other, half)
            self.send(k, other, half, directions)

        def pair(self, k, other):
            self.send(k, other, None, (PAIR,))

        def gather(self, k, other):
            self.arrived(k, other, 1)
            self.arrived(k, other, 0)
            self.pair(k, other)

    at_end, at_mid = Role(True), Role(False)

    def start_own(direction):
        def by(role):
            k = 0 if role.is_end else 1
            for half in {SIDE: (1, 0), PAIR: (None,)}.get(direction, (0, 1)):
                role.send(k, 0, half, (direction,), own=True)

        if direction == OUT:
            by(at_mid)
        elif direction == PAIR:
            by(at_end)
        else:
            pl.when(end)(lambda: by(at_end))
            pl.when(mid)(lambda: by(at_mid))

    for direction, lower in enumerate(down):
        @pl.when(lower)
        def _():
            start_own(direction)
    for direction, higher in reversed(tuple(enumerate(up))):
        @pl.when(higher)
        def _():
            pl.semaphore_wait(ready_sem.at[AXIS[direction]], 1)
            start_own(direction)

    own_lab.wait()
    label_column = jnp.transpose(
        jnp.broadcast_to(labs[core].astype(jnp.float32), (rows, rows))
    )[:, :1]
    own_data.wait()

    def from_pair(slot):
        theirs = slot * CORES + 1 - core
        pltpu.make_async_remote_copy(
            labs.at[theirs], labs.at[theirs], lsend_sem.at[0], lrecv_sem.at[theirs],
            device_id={"docs": targets[PAIR]}, device_id_type=MESH,
        ).wait_recv()
        place = rows_of(slot, 1 - core, None)
        pltpu.make_async_remote_copy(
            place, place, send_sem.at[PAIR], pair_sem.at[slot],
            device_id={"docs": targets[PAIR]}, device_id_type=MESH,
        ).wait_recv()

    def masked_scores(slot, count):
        keys = count * CORES * rows
        values = buf[pl.ds(pl.multiple_of(slot * CORES * rows, rows), keys), :]
        mine = buf[pl.ds(pl.multiple_of(core * rows, rows), rows), :]
        tags = jnp.concatenate(
            [labs[slot * CORES + n].astype(jnp.float32) for n in range(count * CORES)], axis=1
        )
        scores = lax.dot_general(
            mine, values, (((1,), (1,)), ((), ())), preferred_element_type=jnp.float32
        ) * (kernel_gain / math.sqrt(width))
        return scores, label_column == tags, values

    def first_block():
        scores, near, values = masked_scores(0, 1)
        gap = lax.broadcasted_iota(jnp.int32, near.shape, 1) - lax.broadcasted_iota(jnp.int32, near.shape, 0)
        masked = jnp.where(near & (gap != core * rows), scores, neg_large)
        peak = jnp.maximum(jnp.max(masked, axis=1, keepdims=True), neg_start)
        weights = jnp.exp(masked - peak)
        row_max[...] = peak
        row_total[...] = jnp.sum(weights, axis=1, keepdims=True)
        acc[...] = jnp.dot(weights.astype(jnp.bfloat16), values, preferred_element_type=jnp.float32)

    def absorb(slot, count):
        scores, near, values = masked_scores(slot, count)
        masked = jnp.where(near, scores, neg_large)
        before = row_max[...]
        peak = jnp.maximum(before, jnp.max(masked, axis=1, keepdims=True))
        weights = jnp.exp(masked - peak)
        scale = jnp.exp(before - peak)
        total = row_total[...] * scale + jnp.sum(weights, axis=1, keepdims=True)
        gained = jnp.dot(weights.astype(jnp.bfloat16), values, preferred_element_type=jnp.float32)
        return peak, total, scale, gained

    from_pair(0)
    first_block()

    def step(j, carry):
        @pl.when(end & (j == 1))
        def _():
            r = at_end
            r.pass_on(1, 0, 0, (SIDE,))
            r.pass_on(0, 1, 1, (IN,))
            r.pass_on(1, 0, 1, (SIDE,))
            r.pair(1, 0)
            r.pass_on(0, 1, 0, (IN,))
            r.pair(0, 1)
            r.pass_on(2, 0, 0, (SIDE,))

        @pl.when(end & (j == 2))
        def _():
            r = at_end
            r.pass_on(2, 0, 1, (SIDE,))
            r.pair(2, 0)
            r.gather(1, 1)
            r.pass_on(3, 0, 0, (SIDE,))

        @pl.when(end & (j == 3))
        def _():
            r = at_end
            r.arrived(3, 0, 1)
            r.pair(3, 0)
            r.gather(2, 1)

        @pl.when(mid & (j == 1))
        def _():
            r = at_mid
            r.pass_on(2, 0, 0, (OUT, SIDE))
            r.pass_on(0, 0, 0, (IN,))
            r.pass_on(2, 0, 1, (OUT, SIDE))
            r.pair(2, 0)
            r.pass_on(0, 0, 1, (IN,))
            r.pair(0, 0)
            r.gather(1, 1)
            r.pass_on(3, 0, 0, (OUT, SIDE))
            r.pass_on(0, 1, 1, (IN,))

        @pl.when(mid & (j == 2))
        def _():
            r = at_mid
            r.pass_on(3, 0, 1, (OUT,))
            r.pair(3, 0)
            r.arrived(0, 1, 0)
            r.pair(0, 1)
            r.gather(2, 1)

        @pl.when(mid & (j == 3))
        def _():
            at_mid.pass_on(3, 1, 1, (OUT,))

        slot = 2 * j - 1
        from_pair(slot)
        from_pair(slot + 1)
        peak, total, scale, gained = absorb(slot, 2)
        row_max[...] = peak
        row_total[...] = total
        acc[...] = acc[...] * scale + gained
        return carry

    lax.fori_loop(1, planes, step, 0)

    @pl.when(end)
    def _():
        at_end.arrived(3, 1, 1)

    last = at_end
    last.send(3, 1, 1, (PAIR,))
    last.arrived(3, 1, 0)
    last.send(3, 1, 0, (PAIR,))
    from_pair(last.slot(3, 1))
    peak, total, scale, gained = absorb(last.slot(3, 1), 1)
    density = peak + jnp.log(total)
    dens_ref[...] = jnp.transpose(jnp.broadcast_to(density, (rows, rows)))[:1, :]
    inverse = 1.0 / total
    mean_ref[...] = ((acc[...] * scale + gained) * inverse).astype(mean_ref.dtype)

    def sent(direction, halves):
        amount = buf.at[pl.ds(0, halves * half_rows)]
        pltpu.make_async_remote_copy(
            amount, amount, send_sem.at[direction], pair_sem.at[0],
            device_id={"docs": targets[direction]}, device_id_type=MESH,
        ).wait_send()

    def labs_sent(count):
        amount = labs.at[pl.ds(0, count)]
        pltpu.make_async_remote_copy(
            amount, amount, lsend_sem.at[0], lrecv_sem.at[0],
            device_id={"docs": targets[PAIR]}, device_id_type=MESH,
        ).wait_send()

    @pl.when(end)
    def _():
        sent(IN, 4)
        sent(SIDE, 7)
        sent(PAIR, 16)
        labs_sent(14)

    @pl.when(mid)
    def _():
        sent(OUT, 7)
        sent(IN, 5)
        sent(SIDE, 5)
        sent(PAIR, 16)
        labs_sent(16)


def publish_kernel(dens_ref, mean_ref, dens_out, mean_out, sem):
    copies = (
        pltpu.make_async_copy(mean_ref, mean_out, sem.at[0]),
        pltpu.make_async_copy(dens_ref, dens_out, sem.at[1]),
    )
    for copy in copies:
        copy.start()
    for copy in copies:
        copy.wait()


def publish(density, mean):
    held = [pltpu.with_memory_space_constraint(a, pltpu.VMEM) for a in (density, mean)]
    return pl.pallas_call(
        publish_kernel,
        out_shape=tuple(jax.ShapeDtypeStruct(a.shape, a.dtype) for a in (density, mean)),
        in_specs=[pl.BlockSpec(memory_space=pltpu.VMEM)] * 2,
        out_specs=(pl.BlockSpec(memory_space=pltpu.HBM),) * 2,
        scratch_shapes=[pltpu.SemaphoreType.DMA((2,))],
    )(*held)


def general_call(device_count, rows, width):
    grid_slow, grid_fast = chip_grid(device_count)
    chips = device_count // CORES
    vmem = pl.BlockSpec(memory_space=pltpu.VMEM)
    return pl.pallas_call(
        functools.partial(kernel, grid_slow, grid_fast),
        out_shape=(
            pltpu.VMEM((1, rows), jnp.float32),
            pltpu.VMEM((rows, width), jnp.bfloat16),
        ),
        in_specs=[pl.BlockSpec(memory_space=pl.ANY), pl.BlockSpec(memory_space=pl.ANY)],
        out_specs=(vmem, vmem),
        scratch_shapes=[
            pltpu.VMEM((device_count * rows, width), jnp.bfloat16),
            pltpu.VMEM((device_count, 1, rows), jnp.int32),
            pltpu.VMEM((rows, width), jnp.bfloat16),
            pltpu.VMEM((rows, width), jnp.float32),
            pltpu.VMEM((rows, 1), jnp.float32),
            pltpu.VMEM((rows, 1), jnp.float32),
            pltpu.SemaphoreType.DMA((5, chips * PIECES)),
            pltpu.SemaphoreType.DMA((device_count * PIECES,)),
            pltpu.SemaphoreType.DMA((5, chips)),
            pltpu.SemaphoreType.DMA((device_count,)),
            pltpu.SemaphoreType.DMA((PIECES + 1,)),
            pltpu.SemaphoreType.DMA((1,)),
        ],
        compiler_params=pltpu.CompilerParams(collective_id=0, has_side_effects=True),
    )


def folded_call(device_count, rows, width):
    chips = device_count // CORES
    vmem = pl.BlockSpec(memory_space=pltpu.VMEM)
    return pl.pallas_call(
        functools.partial(folded_kernel, chips // 2),
        out_shape=(
            pltpu.VMEM((1, rows), jnp.float32),
            pltpu.VMEM((rows, width), jnp.bfloat16),
        ),
        in_specs=[pl.BlockSpec(memory_space=pl.ANY), pl.BlockSpec(memory_space=pl.ANY)],
        out_specs=(vmem, vmem),
        scratch_shapes=[
            pltpu.VMEM((device_count * rows, width), jnp.bfloat16),
            pltpu.VMEM((device_count, 1, rows), jnp.int32),
            pltpu.VMEM((rows, width), jnp.float32),
            pltpu.VMEM((rows, 1), jnp.float32),
            pltpu.VMEM((rows, 1), jnp.float32),
            pltpu.SemaphoreType.DMA((4,)),
            pltpu.SemaphoreType.DMA((2 * chips,)),
            pltpu.SemaphoreType.DMA((chips,)),
            pltpu.SemaphoreType.DMA((1,)),
            pltpu.SemaphoreType.DMA((device_count,)),
            pltpu.SemaphoreType.DMA((2,)),
            pltpu.SemaphoreType.REGULAR((3,)),
        ],
        compiler_params=pltpu.CompilerParams(collective_id=0, has_side_effects=True),
    )


def per_device(device_count, embeddings, labels, row_slot):
    rows, width = embeddings.shape
    call = folded_call if chip_grid(device_count) == FOLDED_GRID else general_call
    density, mean = call(device_count, rows, width)(embeddings, labels.reshape(1, rows))
    density, mean = publish(density, mean)
    return density.reshape(rows), mean


def solution(mesh):
    return jax.shard_map(
        functools.partial(per_device, mesh.shape["docs"]),
        mesh=mesh,
        in_specs=(P(("groups", "docs"), None), P(("groups", "docs")), P(("groups", "docs"))),
        out_specs=(P(("groups", "docs")), P(("groups", "docs"), None)),
        check_vma=False,
    )
```

```python
import functools
import math

import jax
import jax.numpy as jnp
from jax import lax
from jax.experimental import pallas as pl
from jax.experimental.pallas import tpu as pltpu
from jax.sharding import PartitionSpec as P

MESH = pl.DeviceIdType.MESH
CORES = 2
PIECES = 2
HALVES = 1
FOLDED_GRID = (4, 2)

neg_large = -1e30
neg_start = -1e29
kernel_gain = 4.0


def chip_grid(device_count):
    chips = device_count // CORES
    fast = 1
    while (2 * fast) * (2 * fast) <= chips and chips % (2 * fast) == 0:
        fast *= 2
    return chips // fast, fast


def kernel(
    grid_slow, grid_fast, x_ref, lab_ref, dens_ref, mean_ref,
    buf, labs, mine, acc, row_max, row_total,
    send_sem, recv_sem, lsend_sem, lrecv_sem, own_sem, own_lab_sem,
):
    rows, width = x_ref.shape
    part = rows // PIECES
    group = PIECES // HALVES
    half_rows = rows // HALVES
    keys = CORES * half_rows
    me = lax.axis_index("docs")
    core = lax.rem(me, CORES)
    chip = me // CORES
    y = lax.rem(chip, grid_fast)
    z = chip // grid_fast

    def device(zz, yy, cc):
        return (zz * grid_fast + yy) * CORES + cc

    targets = (
        (z > 0, device(z - 1, y, core)),
        (z < grid_slow - 1, device(z + 1, y, core)),
        (y > 0, device(z, y - 1, core)),
        (y < grid_fast - 1, device(z, y + 1, core)),
        (z >= 0, device(z, y, 1 - core)),
    )

    barrier = pltpu.get_barrier_semaphore()
    for there, target in targets:
        @pl.when(there)
        def _():
            pl.semaphore_signal(barrier, inc=1, device_id={"docs": target}, device_id_type=MESH)

    def data_of(zz, yy, cc, piece):
        where = ((zz * grid_fast + yy) * HALVES + piece // group) * CORES + cc
        return buf.at[pl.ds(pl.multiple_of((where * group + lax.rem(piece, group)) * part, part), part)]

    own_copies = [pltpu.make_async_copy(x_ref, mine, own_sem.at[PIECES])]
    for piece in range(PIECES):
        own_copies.append(
            pltpu.make_async_copy(
                x_ref.at[pl.ds(piece * part, part)], data_of(z, y, core, piece), own_sem.at[piece]
            )
        )
    own_copies.append(pltpu.make_async_copy(lab_ref, labs.at[me], own_lab_sem.at[0]))
    for copy in own_copies:
        copy.start()
    pl.semaphore_wait(barrier, sum(there.astype(jnp.int32) for there, _ in targets))

    def data_copy(direction, zz, yy, piece, own):
        data = data_of(zz, yy, core, piece)
        return pltpu.make_async_remote_copy(
            x_ref.at[pl.ds(piece * part, part)] if own else data, data,
            send_sem.at[direction, (zz * grid_fast + yy) * PIECES + piece],
            recv_sem.at[device(zz, yy, core) * PIECES + piece],
            device_id={"docs": targets[direction][1]}, device_id_type=MESH,
        )

    def lab_copy(direction, zz, yy, own):
        slot = device(zz, yy, core)
        return pltpu.make_async_remote_copy(
            lab_ref if own else labs.at[slot], labs.at[slot],
            lsend_sem.at[direction, zz * grid_fast + yy], lrecv_sem.at[slot],
            device_id={"docs": targets[direction][1]}, device_id_type=MESH,
        )

    def each(directions, wanted, zz, yy, piece, own, act):
        for direction, want in zip(directions, wanted):
            @pl.when(jnp.logical_and(targets[direction][0], want))
            def _():
                @pl.when(piece == 0)
                def _():
                    act(lab_copy(direction, zz, yy, own))
                act(data_copy(direction, zz, yy, piece, own))

    start = lambda copy: copy.start()
    finish = lambda copy: copy.wait_send()

    def arrived(zz, yy, cc, piece):
        slot = device(zz, yy, cc)
        @pl.when(piece == 0)
        def _():
            pltpu.make_async_remote_copy(
                labs.at[slot], labs.at[slot], lsend_sem.at[0, 0], lrecv_sem.at[slot],
                device_id={"docs": targets[4][1]}, device_id_type=MESH,
            ).wait_recv()
        data = data_of(zz, yy, cc, piece)
        pltpu.make_async_remote_copy(
            data, data, send_sem.at[0, 0], recv_sem.at[slot * PIECES + piece],
            device_id={"docs": targets[4][1]}, device_id_type=MESH,
        ).wait_recv()

    yes = z >= 0
    for piece in range(PIECES):
        each((2, 3, 0, 1, 4), (yes,) * 5, z, y, piece, True, start)

    row_max[...] = jnp.full_like(row_max, neg_large)
    row_total[...] = jnp.zeros_like(row_total)
    acc[...] = jnp.zeros_like(acc)
    own_copies[-1].wait()
    label_column = jnp.transpose(
        jnp.broadcast_to(labs[me].astype(jnp.float32), (rows, rows))
    )[:, :1]
    column = lax.broadcasted_iota(jnp.int32, (rows, keys), 1)
    gap = (
        column + (column // half_rows) * (rows - half_rows)
        - lax.broadcasted_iota(jnp.int32, (rows, keys), 0)
    )
    for copy in own_copies[:-1]:
        copy.wait()

    def compute(zz, yy, half):
        where = zz * grid_fast + yy
        values = buf[pl.ds(pl.multiple_of((where * HALVES + half) * keys, keys), keys), :]
        tags = []
        for cc in range(CORES):
            tag = labs[where * CORES + cc].astype(jnp.float32)
            pieces = [tag[:, h * half_rows:(h + 1) * half_rows] for h in range(HALVES)]
            picked = pieces[0]
            for h in range(1, HALVES):
                picked = jnp.where(half == h, pieces[h], picked)
            tags.append(picked)
        tags = jnp.concatenate(tags, axis=1)
        scores = lax.dot_general(
            mine[...], values, (((1,), (1,)), ((), ())), preferred_element_type=jnp.float32
        ) * (kernel_gain / math.sqrt(width))
        self_gap = jnp.where(where == chip, core * rows - half * half_rows, CORES * rows)
        absorb(scores, (label_column == tags) & (gap != self_gap), values)

    def compute_core(zz, yy, cc):
        slot = device(zz, yy, cc)
        values = buf[pl.ds(pl.multiple_of(slot * rows, rows), rows), :]
        scores = lax.dot_general(
            mine[...], values, (((1,), (1,)), ((), ())), preferred_element_type=jnp.float32
        ) * (kernel_gain / math.sqrt(width))
        absorb(scores, label_column == labs[slot].astype(jnp.float32), values)

    def absorb(scores, near, values):
        masked = jnp.where(near, scores, neg_large)
        before = row_max[...]
        peak = jnp.maximum(before, jnp.max(masked, axis=1, keepdims=True))
        weights = jnp.where(near, jnp.exp(masked - peak), 0.0)
        scale = jnp.exp(before - peak)
        row_max[...] = peak
        row_total[...] = row_total[...] * scale + jnp.sum(weights, axis=1, keepdims=True)
        acc[...] = acc[...] * scale + jnp.dot(
            weights.astype(jnp.bfloat16), values, preferred_element_type=jnp.float32
        )

    def meet(zz, yy, half):
        def one(p, carry):
            arrived(zz, yy, 1 - core, half * group + p)
            return carry
        lax.fori_loop(0, group, one, 0)
        compute(zz, yy, half)

    def visited(distance, side, reach, origin):
        place = origin + jnp.where(side == 0, -distance, distance)
        inside = (distance >= 0) & (distance < reach) & (place >= 0) & (place < reach)
        return place, inside & jnp.logical_or(distance > 0, side == 0)

    def other_columns(body):
        if grid_fast == 2:
            body(1 - y)
            return
        def one(i, carry):
            yy, valid = visited(i // 2 + 1, lax.rem(i, 2), grid_fast, y)
            @pl.when(valid)
            def _():
                body(yy)
            return carry
        lax.fori_loop(0, 2 * (grid_fast - 1), one, 0)

    def along(zz, piece, side, act):
        each((2, 3, 0, 1, 4), (yes, yes, side == 1, side == 0, yes), zz, y, piece, False, act)

    def across(zz, yy, piece, act):
        each((2, 3, 4), (yy > y, yy < y, yes), zz, yy, piece, False, act)

    def receive(zz, yy, piece):
        arrived(zz, yy, core, piece)
        across(zz, yy, piece, start)

    farthest = jnp.where(2 * z >= grid_slow, 0, grid_slow - 1)

    def event(e, carry):
        distance = e // (2 * PIECES)
        piece = lax.rem(e // 2, PIECES)
        side = lax.rem(e, 2)
        half = piece // group

        @pl.when(e == 2 * PIECES * grid_slow)
        def _():
            for p in range(PIECES):
                each((2, 3, 0, 1, 4), (yes,) * 5, z, y, p, True, finish)

        zz, valid = visited(distance, side, grid_slow, z)
        @pl.when(valid & (distance > 0))
        def _():
            arrived(zz, y, core, piece)
            along(zz, piece, side, start)

        z1, valid1 = visited(distance - 1, side, grid_slow, z)
        z2, valid2 = visited(distance - 2, side, grid_slow, z)
        @pl.when(valid2)
        def _():
            other_columns(lambda yy: receive(z2, yy, piece))
            @pl.when(distance > 2)
            def _():
                along(z2, piece, side, finish)

        z3, valid3 = visited(distance - 3, side, grid_slow, z)
        @pl.when(valid3)
        def _():
            other_columns(lambda yy: across(z3, yy, piece, finish))

        near = valid1 & (lax.rem(piece, group) == 0)
        if grid_fast == 2:
            far = valid2 & (lax.rem(piece, group) == group - 1) & (z2 != farthest)
            @pl.when(near | far)
            def _():
                def one(i, carry):
                    @pl.when(jnp.where(i == 0, near, far))
                    def _():
                        meet(jnp.where(i == 0, z1, z2), jnp.where(i == 0, y, 1 - y), half)
                    return carry
                lax.fori_loop(0, 2, one, 0)
        else:
            @pl.when(near)
            def _():
                meet(z1, y, half)
            @pl.when(valid2 & (lax.rem(piece, group) == group - 1))
            def _():
                other_columns(lambda yy: meet(z2, yy, half))
        return carry

    lax.fori_loop(0, 2 * PIECES * (grid_slow + 2), event, 0)
    if grid_fast == 2:
        def last_pair(i, carry):
            cc = jnp.where(i == 0, core, 1 - core)
            @pl.when(i == 1)
            def _():
                for p in range(PIECES):
                    arrived(farthest, 1 - y, 1 - core, p)
            compute_core(farthest, 1 - y, cc)
            return carry
        lax.fori_loop(0, CORES, last_pair, 0)

    total = row_total[...]
    density = row_max[...] + jnp.log(total)
    dens_ref[...] = jnp.transpose(jnp.broadcast_to(density, (rows, rows)))[:1, :]
    mean_ref[...] = (acc[...] / total).astype(mean_ref.dtype)

    for e in range(2 * PIECES):
        last, valid = visited(grid_slow - 1, e % 2, grid_slow, z)
        @pl.when(valid)
        def _():
            other_columns(lambda yy: across(last, yy, e // 2, finish))


def folded_kernel(
    planes, x_ref, lab_ref, dens_ref, mean_ref,
    buf, labs, acc, row_max, row_total,
    send_sem, recv_sem, pair_sem, lsend_sem, lrecv_sem, own_sem, ready_sem,
):
    rows, width = x_ref.shape
    half_rows = rows // 2
    me = lax.axis_index("docs")
    core = lax.rem(me, CORES)
    y = lax.rem(me // CORES, 2)
    z = me // (CORES * 2)
    mirrored = 2 * z >= planes
    end = (z == 0) | (z == planes - 1)
    mid = jnp.logical_not(end)

    def device(k, column, cc):
        zz = jnp.where(mirrored, planes - 1 - k, k)
        return (zz * 2 + column) * CORES + cc

    OUT, IN, SIDE, PAIR = range(4)
    AXIS = (0, 0, 1, 2)
    home = jnp.where(end, 0, 1)
    targets = (
        device(0, y, core),
        device(home + 1, y, core),
        device(home, 1 - y, core),
        device(home, y, 1 - core),
    )
    END_ORDER = ((0, 0), (1, 0), (0, 1), (2, 0), (1, 1), (3, 0), (2, 1), (3, 1))
    MID_ORDER = ((1, 0), (2, 0), (0, 0), (3, 0), (0, 1), (1, 1), (2, 1), (3, 1))

    up = (mid & mirrored, jnp.logical_not(mirrored), y == 0, core == 0)
    down = (mid & jnp.logical_not(mirrored), mirrored, y == 1, core == 1)
    barrier = pltpu.get_barrier_semaphore()
    for target, higher in zip(targets, up):
        @pl.when(higher)
        def _():
            pl.semaphore_signal(barrier, inc=1, device_id={"docs": target}, device_id_type=MESH)

    def rows_of(slot, cc, half):
        first = (slot * CORES + cc) * rows
        if half is None:
            return buf.at[pl.ds(pl.multiple_of(first, rows), rows)]
        return buf.at[pl.ds(pl.multiple_of(first + half * half_rows, half_rows), half_rows)]

    own_data = pltpu.make_async_copy(x_ref, rows_of(0, core, None), own_sem.at[0])
    own_data.start()
    own_lab = pltpu.make_async_copy(lab_ref, labs.at[core], own_sem.at[1])
    own_lab.start()
    lower_count = sum(lower.astype(jnp.int32) for lower in down)
    @pl.when(lower_count > 0)
    def _():
        pl.semaphore_wait(barrier, lower_count)
    for direction, lower in enumerate(down):
        @pl.when(lower)
        def _():
            pl.semaphore_signal(
                ready_sem.at[AXIS[direction]], inc=1,
                device_id={"docs": targets[direction]}, device_id_type=MESH,
            )

    def data_copy(direction, slot, there, half, own=False):
        if not own:
            source = rows_of(slot, core, half)
        else:
            source = x_ref if half is None else x_ref.at[pl.ds(half * half_rows, half_rows)]
        done = pair_sem.at[there] if direction == PAIR else recv_sem.at[there * 2 + half]
        return pltpu.make_async_remote_copy(
            source, rows_of(there, core, half), send_sem.at[direction], done,
            device_id={"docs": targets[direction]}, device_id_type=MESH,
        )

    def lab_copy(direction, slot, there, own=False):
        there = there * CORES + core
        return pltpu.make_async_remote_copy(
            lab_ref if own else labs.at[slot * CORES + core], labs.at[there],
            lsend_sem.at[0], lrecv_sem.at[there],
            device_id={"docs": targets[direction]}, device_id_type=MESH,
        )

    class Role:
        def __init__(self, is_end):
            self.is_end = is_end
            self.order = END_ORDER if is_end else MID_ORDER

        def slot(self, k, other):
            return self.order.index((k, other))

        def there(self, direction, k, other):
            if direction == SIDE:
                return self.slot(k, 1 - other)
            if direction == PAIR:
                return self.slot(k, other)
            if direction == OUT:
                return END_ORDER.index((k, other))
            return MID_ORDER.index((k if self.is_end else planes - 1 - k, other))

        def send(self, k, other, half, directions, own=False):
            for direction in directions:
                slot, there = self.slot(k, other), self.there(direction, k, other)
                if half != 1:
                    lab_copy(direction, slot, there, own).start()
                data_copy(direction, slot, there, half, own).start()

        def arrived(self, k, other, half):
            slot = self.slot(k, other)
            if half == 0:
                lab_copy(SIDE, slot, slot).wait_recv()
            data_copy(SIDE, slot, slot, half).wait_recv()

        def pass_on(self, k, other, half, directions):
            self.arrived(k, other, half)
            self.send(k, other, half, directions)

        def pair(self, k, other):
            self.send(k, other, None, (PAIR,))

        def gather(self, k, other):
            self.arrived(k, other, 1)
            self.arrived(k, other, 0)
            self.pair(k, other)

    at_end, at_mid = Role(True), Role(False)

    def start_own(direction):
        def by(role):
            k = 0 if role.is_end else 1
            for half in {SIDE: (1, 0), PAIR: (None,)}.get(direction, (0, 1)):
                role.send(k, 0, half, (direction,), own=True)

        if direction == OUT:
            by(at_mid)
        elif direction == PAIR:
            by(at_end)
        else:
            pl.when(end)(lambda: by(at_end))
            pl.when(mid)(lambda: by(at_mid))

    for direction, lower in enumerate(down):
        @pl.when(lower)
        def _():
            start_own(direction)
    for direction, higher in reversed(tuple(enumerate(up))):
        @pl.when(higher)
        def _():
            pl.semaphore_wait(ready_sem.at[AXIS[direction]], 1)
            start_own(direction)

    own_lab.wait()
    label_column = jnp.transpose(
        jnp.broadcast_to(labs[core].astype(jnp.float32), (rows, rows))
    )[:, :1]
    own_data.wait()

    def from_pair(slot):
        theirs = slot * CORES + 1 - core
        pltpu.make_async_remote_copy(
            labs.at[theirs], labs.at[theirs], lsend_sem.at[0], lrecv_sem.at[theirs],
            device_id={"docs": targets[PAIR]}, device_id_type=MESH,
        ).wait_recv()
        place = rows_of(slot, 1 - core, None)
        pltpu.make_async_remote_copy(
            place, place, send_sem.at[PAIR], pair_sem.at[slot],
            device_id={"docs": targets[PAIR]}, device_id_type=MESH,
        ).wait_recv()

    def masked_scores(slot, count):
        keys = count * CORES * rows
        values = buf[pl.ds(pl.multiple_of(slot * CORES * rows, rows), keys), :]
        mine = buf[pl.ds(pl.multiple_of(core * rows, rows), rows), :]
        tags = jnp.concatenate(
            [labs[slot * CORES + n].astype(jnp.float32) for n in range(count * CORES)], axis=1
        )
        scores = lax.dot_general(
            mine, values, (((1,), (1,)), ((), ())), preferred_element_type=jnp.float32
        ) * (kernel_gain / math.sqrt(width))
        return scores, label_column == tags, values

    def first_block():
        scores, near, values = masked_scores(0, 1)
        gap = lax.broadcasted_iota(jnp.int32, near.shape, 1) - lax.broadcasted_iota(jnp.int32, near.shape, 0)
        masked = jnp.where(near & (gap != core * rows), scores, neg_large)
        peak = jnp.maximum(jnp.max(masked, axis=1, keepdims=True), neg_start)
        weights = jnp.exp(masked - peak)
        row_max[...] = peak
        row_total[...] = jnp.sum(weights, axis=1, keepdims=True)
        acc[...] = jnp.dot(weights.astype(jnp.bfloat16), values, preferred_element_type=jnp.float32)

    def absorb(slot, count):
        scores, near, values = masked_scores(slot, count)
        masked = jnp.where(near, scores, neg_large)
        before = row_max[...]
        peak = jnp.maximum(before, jnp.max(masked, axis=1, keepdims=True))
        weights = jnp.exp(masked - peak)
        scale = jnp.exp(before - peak)
        total = row_total[...] * scale + jnp.sum(weights, axis=1, keepdims=True)
        gained = jnp.dot(weights.astype(jnp.bfloat16), values, preferred_element_type=jnp.float32)
        return peak, total, scale, gained

    from_pair(0)
    first_block()

    last = at_end

    def step(j, carry):
        @pl.when(end & (j == 1))
        def _():
            r = at_end
            r.pass_on(1, 0, 0, (SIDE,))
            r.pass_on(0, 1, 1, (IN,))
            r.pass_on(1, 0, 1, (SIDE,))
            r.pair(1, 0)
            r.pass_on(0, 1, 0, (IN,))
            r.pair(0, 1)
            r.pass_on(2, 0, 0, (SIDE,))

        @pl.when(end & (j == 2))
        def _():
            r = at_end
            r.pass_on(2, 0, 1, (SIDE,))
            r.pair(2, 0)
            r.gather(1, 1)
            r.pass_on(3, 0, 0, (SIDE,))

        @pl.when(end & (j == 3))
        def _():
            r = at_end
            r.arrived(3, 0, 1)
            r.pair(3, 0)
            r.gather(2, 1)

        @pl.when(mid & (j == 1))
        def _():
            r = at_mid
            r.pass_on(2, 0, 0, (OUT, SIDE))
            r.pass_on(0, 0, 0, (IN,))
            r.pass_on(2, 0, 1, (OUT, SIDE))
            r.pair(2, 0)
            r.pass_on(0, 0, 1, (IN,))
            r.pair(0, 0)
            r.gather(1, 1)
            r.pass_on(3, 0, 0, (OUT, SIDE))
            r.pass_on(0, 1, 1, (IN,))

        @pl.when(mid & (j == 2))
        def _():
            r = at_mid
            r.pass_on(3, 0, 1, (OUT,))
            r.pair(3, 0)
            r.arrived(0, 1, 0)
            r.pair(0, 1)
            r.gather(2, 1)

        @pl.when(mid & (j == 3))
        def _():
            at_mid.pass_on(3, 1, 1, (OUT,))

        @pl.when(j == planes - 1)
        def _():
            @pl.when(end)
            def _():
                at_end.arrived(3, 1, 1)

            last.send(3, 1, 1, (PAIR,))
            last.arrived(3, 1, 0)
            last.send(3, 1, 0, (PAIR,))

        slot = 2 * j - 1
        from_pair(slot)
        from_pair(slot + 1)
        peak, total, scale, gained = absorb(slot, 2)
        row_max[...] = peak
        row_total[...] = total
        acc[...] = acc[...] * scale + gained
        return carry

    lax.fori_loop(1, planes, step, 0)

    from_pair(last.slot(3, 1))
    peak, total, scale, gained = absorb(last.slot(3, 1), 1)
    density = peak + jnp.log(total)
    dens_ref[...] = jnp.transpose(jnp.broadcast_to(density, (rows, rows)))[:1, :]
    inverse = 1.0 / total
    mean_ref[...] = ((acc[...] * scale + gained) * inverse).astype(mean_ref.dtype)

    def sent(direction, halves):
        amount = buf.at[pl.ds(0, halves * half_rows)]
        pltpu.make_async_remote_copy(
            amount, amount, send_sem.at[direction], pair_sem.at[0],
            device_id={"docs": targets[direction]}, device_id_type=MESH,
        ).wait_send()

    def labs_sent(count):
        amount = labs.at[pl.ds(0, count)]
        pltpu.make_async_remote_copy(
            amount, amount, lsend_sem.at[0], lrecv_sem.at[0],
            device_id={"docs": targets[PAIR]}, device_id_type=MESH,
        ).wait_send()

    @pl.when(end)
    def _():
        sent(IN, 4)
        sent(SIDE, 7)
        sent(PAIR, 16)
        labs_sent(14)

    @pl.when(mid)
    def _():
        sent(OUT, 7)
        sent(IN, 5)
        sent(SIDE, 5)
        sent(PAIR, 16)
        labs_sent(16)


def publish_kernel(dens_ref, mean_ref, dens_out, mean_out, sem):
    copies = (
        pltpu.make_async_copy(mean_ref, mean_out, sem.at[0]),
        pltpu.make_async_copy(dens_ref, dens_out, sem.at[1]),
    )
    for copy in copies:
        copy.start()
    for copy in copies:
        copy.wait()


def publish(density, mean):
    held = [pltpu.with_memory_space_constraint(a, pltpu.VMEM) for a in (density, mean)]
    return pl.pallas_call(
        publish_kernel,
        out_shape=tuple(jax.ShapeDtypeStruct(a.shape, a.dtype) for a in (density, mean)),
        in_specs=[pl.BlockSpec(memory_space=pltpu.VMEM)] * 2,
        out_specs=(pl.BlockSpec(memory_space=pltpu.HBM),) * 2,
        scratch_shapes=[pltpu.SemaphoreType.DMA((2,))],
    )(*held)


def general_call(device_count, rows, width):
    grid_slow, grid_fast = chip_grid(device_count)
    chips = device_count // CORES
    vmem = pl.BlockSpec(memory_space=pltpu.VMEM)
    return pl.pallas_call(
        functools.partial(kernel, grid_slow, grid_fast),
        out_shape=(
            pltpu.VMEM((1, rows), jnp.float32),
            pltpu.VMEM((rows, width), jnp.bfloat16),
        ),
        in_specs=[pl.BlockSpec(memory_space=pl.ANY), pl.BlockSpec(memory_space=pl.ANY)],
        out_specs=(vmem, vmem),
        scratch_shapes=[
            pltpu.VMEM((device_count * rows, width), jnp.bfloat16),
            pltpu.VMEM((device_count, 1, rows), jnp.int32),
            pltpu.VMEM((rows, width), jnp.bfloat16),
            pltpu.VMEM((rows, width), jnp.float32),
            pltpu.VMEM((rows, 1), jnp.float32),
            pltpu.VMEM((rows, 1), jnp.float32),
            pltpu.SemaphoreType.DMA((5, chips * PIECES)),
            pltpu.SemaphoreType.DMA((device_count * PIECES,)),
            pltpu.SemaphoreType.DMA((5, chips)),
            pltpu.SemaphoreType.DMA((device_count,)),
            pltpu.SemaphoreType.DMA((PIECES + 1,)),
            pltpu.SemaphoreType.DMA((1,)),
        ],
        compiler_params=pltpu.CompilerParams(collective_id=0, has_side_effects=True),
    )


def folded_call(device_count, rows, width):
    chips = device_count // CORES
    vmem = pl.BlockSpec(memory_space=pltpu.VMEM)
    return pl.pallas_call(
        functools.partial(folded_kernel, chips // 2),
        out_shape=(
            pltpu.VMEM((1, rows), jnp.float32),
            pltpu.VMEM((rows, width), jnp.bfloat16),
        ),
        in_specs=[pl.BlockSpec(memory_space=pl.ANY), pl.BlockSpec(memory_space=pl.ANY)],
        out_specs=(vmem, vmem),
        scratch_shapes=[
            pltpu.VMEM((device_count * rows, width), jnp.bfloat16),
            pltpu.VMEM((device_count, 1, rows), jnp.int32),
            pltpu.VMEM((rows, width), jnp.float32),
            pltpu.VMEM((rows, 1), jnp.float32),
            pltpu.VMEM((rows, 1), jnp.float32),
            pltpu.SemaphoreType.DMA((4,)),
            pltpu.SemaphoreType.DMA((2 * chips,)),
            pltpu.SemaphoreType.DMA((chips,)),
            pltpu.SemaphoreType.DMA((1,)),
            pltpu.SemaphoreType.DMA((device_count,)),
            pltpu.SemaphoreType.DMA((2,)),
            pltpu.SemaphoreType.REGULAR((3,)),
        ],
        compiler_params=pltpu.CompilerParams(collective_id=0, has_side_effects=True),
    )


def per_device(device_count, embeddings, labels, row_slot):
    rows, width = embeddings.shape
    call = folded_call if chip_grid(device_count) == FOLDED_GRID else general_call
    density, mean = call(device_count, rows, width)(embeddings, labels.reshape(1, rows))
    density, mean = publish(density, mean)
    return density.reshape(rows), mean


def solution(mesh):
    return jax.shard_map(
        functools.partial(per_device, mesh.shape["docs"]),
        mesh=mesh,
        in_specs=(P(("groups", "docs"), None), P(("groups", "docs")), P(("groups", "docs"))),
        out_specs=(P(("groups", "docs")), P(("groups", "docs"), None)),
        check_vma=False,
    )
```

```python
import functools
import math

import jax
import jax.numpy as jnp
from jax import lax
from jax.experimental import pallas as pl
from jax.experimental.pallas import tpu as pltpu
from jax.sharding import PartitionSpec as P

MESH = pl.DeviceIdType.MESH
CORES = 2
PIECES = 2
HALVES = 1
FOLDED_GRID = (4, 2)

neg_large = -1e30
neg_start = -1e29
kernel_gain = 4.0


def chip_grid(device_count):
    chips = device_count // CORES
    fast = 1
    while (2 * fast) * (2 * fast) <= chips and chips % (2 * fast) == 0:
        fast *= 2
    return chips // fast, fast


def kernel(
    grid_slow, grid_fast, x_ref, lab_ref, dens_ref, mean_ref,
    buf, labs, mine, acc, row_max, row_total,
    send_sem, recv_sem, lsend_sem, lrecv_sem, own_sem, own_lab_sem,
):
    rows, width = x_ref.shape
    part = rows // PIECES
    group = PIECES // HALVES
    half_rows = rows // HALVES
    keys = CORES * half_rows
    me = lax.axis_index("docs")
    core = lax.rem(me, CORES)
    chip = me // CORES
    y = lax.rem(chip, grid_fast)
    z = chip // grid_fast

    def device(zz, yy, cc):
        return (zz * grid_fast + yy) * CORES + cc

    targets = (
        (z > 0, device(z - 1, y, core)),
        (z < grid_slow - 1, device(z + 1, y, core)),
        (y > 0, device(z, y - 1, core)),
        (y < grid_fast - 1, device(z, y + 1, core)),
        (z >= 0, device(z, y, 1 - core)),
    )

    barrier = pltpu.get_barrier_semaphore()
    for there, target in targets:
        @pl.when(there)
        def _():
            pl.semaphore_signal(barrier, inc=1, device_id={"docs": target}, device_id_type=MESH)

    def data_of(zz, yy, cc, piece):
        where = ((zz * grid_fast + yy) * HALVES + piece // group) * CORES + cc
        return buf.at[pl.ds(pl.multiple_of((where * group + lax.rem(piece, group)) * part, part), part)]

    own_copies = [pltpu.make_async_copy(x_ref, mine, own_sem.at[PIECES])]
    for piece in range(PIECES):
        own_copies.append(
            pltpu.make_async_copy(
                x_ref.at[pl.ds(piece * part, part)], data_of(z, y, core, piece), own_sem.at[piece]
            )
        )
    own_copies.append(pltpu.make_async_copy(lab_ref, labs.at[me], own_lab_sem.at[0]))
    for copy in own_copies:
        copy.start()
    pl.semaphore_wait(barrier, sum(there.astype(jnp.int32) for there, _ in targets))

    def data_copy(direction, zz, yy, piece, own):
        data = data_of(zz, yy, core, piece)
        return pltpu.make_async_remote_copy(
            x_ref.at[pl.ds(piece * part, part)] if own else data, data,
            send_sem.at[direction, (zz * grid_fast + yy) * PIECES + piece],
            recv_sem.at[device(zz, yy, core) * PIECES + piece],
            device_id={"docs": targets[direction][1]}, device_id_type=MESH,
        )

    def lab_copy(direction, zz, yy, own):
        slot = device(zz, yy, core)
        return pltpu.make_async_remote_copy(
            lab_ref if own else labs.at[slot], labs.at[slot],
            lsend_sem.at[direction, zz * grid_fast + yy], lrecv_sem.at[slot],
            device_id={"docs": targets[direction][1]}, device_id_type=MESH,
        )

    def each(directions, wanted, zz, yy, piece, own, act):
        for direction, want in zip(directions, wanted):
            @pl.when(jnp.logical_and(targets[direction][0], want))
            def _():
                @pl.when(piece == 0)
                def _():
                    act(lab_copy(direction, zz, yy, own))
                act(data_copy(direction, zz, yy, piece, own))

    start = lambda copy: copy.start()
    finish = lambda copy: copy.wait_send()

    def arrived(zz, yy, cc, piece):
        slot = device(zz, yy, cc)
        @pl.when(piece == 0)
        def _():
            pltpu.make_async_remote_copy(
                labs.at[slot], labs.at[slot], lsend_sem.at[0, 0], lrecv_sem.at[slot],
                device_id={"docs": targets[4][1]}, device_id_type=MESH,
            ).wait_recv()
        data = data_of(zz, yy, cc, piece)
        pltpu.make_async_remote_copy(
            data, data, send_sem.at[0, 0], recv_sem.at[slot * PIECES + piece],
            device_id={"docs": targets[4][1]}, device_id_type=MESH,
        ).wait_recv()

    yes = z >= 0
    for piece in range(PIECES):
        each((2, 3, 0, 1, 4), (yes,) * 5, z, y, piece, True, start)

    row_max[...] = jnp.full_like(row_max, neg_large)
    row_total[...] = jnp.zeros_like(row_total)
    acc[...] = jnp.zeros_like(acc)
    own_copies[-1].wait()
    label_column = jnp.transpose(
        jnp.broadcast_to(labs[me].astype(jnp.float32), (rows, rows))
    )[:, :1]
    column = lax.broadcasted_iota(jnp.int32, (rows, keys), 1)
    gap = (
        column + (column // half_rows) * (rows - half_rows)
        - lax.broadcasted_iota(jnp.int32, (rows, keys), 0)
    )
    for copy in own_copies[:-1]:
        copy.wait()

    def compute(zz, yy, half):
        where = zz * grid_fast + yy
        values = buf[pl.ds(pl.multiple_of((where * HALVES + half) * keys, keys), keys), :]
        tags = []
        for cc in range(CORES):
            tag = labs[where * CORES + cc].astype(jnp.float32)
            pieces = [tag[:, h * half_rows:(h + 1) * half_rows] for h in range(HALVES)]
            picked = pieces[0]
            for h in range(1, HALVES):
                picked = jnp.where(half == h, pieces[h], picked)
            tags.append(picked)
        tags = jnp.concatenate(tags, axis=1)
        scores = lax.dot_general(
            mine[...], values, (((1,), (1,)), ((), ())), preferred_element_type=jnp.float32
        ) * (kernel_gain / math.sqrt(width))
        self_gap = jnp.where(where == chip, core * rows - half * half_rows, CORES * rows)
        absorb(scores, (label_column == tags) & (gap != self_gap), values)

    def compute_core(zz, yy, cc):
        slot = device(zz, yy, cc)
        values = buf[pl.ds(pl.multiple_of(slot * rows, rows), rows), :]
        scores = lax.dot_general(
            mine[...], values, (((1,), (1,)), ((), ())), preferred_element_type=jnp.float32
        ) * (kernel_gain / math.sqrt(width))
        absorb(scores, label_column == labs[slot].astype(jnp.float32), values)

    def absorb(scores, near, values):
        masked = jnp.where(near, scores, neg_large)
        before = row_max[...]
        peak = jnp.maximum(before, jnp.max(masked, axis=1, keepdims=True))
        weights = jnp.where(near, jnp.exp(masked - peak), 0.0)
        scale = jnp.exp(before - peak)
        row_max[...] = peak
        row_total[...] = row_total[...] * scale + jnp.sum(weights, axis=1, keepdims=True)
        acc[...] = acc[...] * scale + jnp.dot(
            weights.astype(jnp.bfloat16), values, preferred_element_type=jnp.float32
        )

    def meet(zz, yy, half):
        def one(p, carry):
            arrived(zz, yy, 1 - core, half * group + p)
            return carry
        lax.fori_loop(0, group, one, 0)
        compute(zz, yy, half)

    def visited(distance, side, reach, origin):
        place = origin + jnp.where(side == 0, -distance, distance)
        inside = (distance >= 0) & (distance < reach) & (place >= 0) & (place < reach)
        return place, inside & jnp.logical_or(distance > 0, side == 0)

    def other_columns(body):
        if grid_fast == 2:
            body(1 - y)
            return
        def one(i, carry):
            yy, valid = visited(i // 2 + 1, lax.rem(i, 2), grid_fast, y)
            @pl.when(valid)
            def _():
                body(yy)
            return carry
        lax.fori_loop(0, 2 * (grid_fast - 1), one, 0)

    def along(zz, piece, side, act):
        each((2, 3, 0, 1, 4), (yes, yes, side == 1, side == 0, yes), zz, y, piece, False, act)

    def across(zz, yy, piece, act):
        each((2, 3, 4), (yy > y, yy < y, yes), zz, yy, piece, False, act)

    def receive(zz, yy, piece):
        arrived(zz, yy, core, piece)
        across(zz, yy, piece, start)

    farthest = jnp.where(2 * z >= grid_slow, 0, grid_slow - 1)

    def event(e, carry):
        distance = e // (2 * PIECES)
        piece = lax.rem(e // 2, PIECES)
        side = lax.rem(e, 2)
        half = piece // group

        @pl.when(e == 2 * PIECES * grid_slow)
        def _():
            for p in range(PIECES):
                each((2, 3, 0, 1, 4), (yes,) * 5, z, y, p, True, finish)

        zz, valid = visited(distance, side, grid_slow, z)
        @pl.when(valid & (distance > 0))
        def _():
            arrived(zz, y, core, piece)
            along(zz, piece, side, start)

        z1, valid1 = visited(distance - 1, side, grid_slow, z)
        z2, valid2 = visited(distance - 2, side, grid_slow, z)
        @pl.when(valid2)
        def _():
            other_columns(lambda yy: receive(z2, yy, piece))
            @pl.when(distance > 2)
            def _():
                along(z2, piece, side, finish)

        z3, valid3 = visited(distance - 3, side, grid_slow, z)
        @pl.when(valid3)
        def _():
            other_columns(lambda yy: across(z3, yy, piece, finish))

        near = valid1 & (lax.rem(piece, group) == 0)
        if grid_fast == 2:
            far = valid2 & (lax.rem(piece, group) == group - 1) & (z2 != farthest)
            @pl.when(near | far)
            def _():
                def one(i, carry):
                    @pl.when(jnp.where(i == 0, near, far))
                    def _():
                        meet(jnp.where(i == 0, z1, z2), jnp.where(i == 0, y, 1 - y), half)
                    return carry
                lax.fori_loop(0, 2, one, 0)
        else:
            @pl.when(near)
            def _():
                meet(z1, y, half)
            @pl.when(valid2 & (lax.rem(piece, group) == group - 1))
            def _():
                other_columns(lambda yy: meet(z2, yy, half))
        return carry

    lax.fori_loop(0, 2 * PIECES * (grid_slow + 2), event, 0)
    if grid_fast == 2:
        def last_pair(i, carry):
            cc = jnp.where(i == 0, core, 1 - core)
            @pl.when(i == 1)
            def _():
                for p in range(PIECES):
                    arrived(farthest, 1 - y, 1 - core, p)
            compute_core(farthest, 1 - y, cc)
            return carry
        lax.fori_loop(0, CORES, last_pair, 0)

    total = row_total[...]
    density = row_max[...] + jnp.log(total)
    dens_ref[...] = jnp.transpose(jnp.broadcast_to(density, (rows, rows)))[:1, :]
    mean_ref[...] = (acc[...] / total).astype(mean_ref.dtype)

    for e in range(2 * PIECES):
        last, valid = visited(grid_slow - 1, e % 2, grid_slow, z)
        @pl.when(valid)
        def _():
            other_columns(lambda yy: across(last, yy, e // 2, finish))


def folded_kernel(
    planes, x_ref, lab_ref, dens_ref, mean_ref,
    buf, labs, meter, acc, row_max, row_total,
    send_sem, lsend_sem, recv_sem, pair_sem, own_sem, ready_sem,
):
    rows, width = x_ref.shape
    row_units = width * x_ref.dtype.itemsize // (rows * lab_ref.dtype.itemsize)
    half_rows = rows // 2
    tip = rows // 8
    FIRST, SECOND, WHOLE = (0, half_rows), (half_rows, half_rows), (0, rows)
    FIRST_BODY, FIRST_TIP = (0, half_rows - tip), (half_rows - tip, tip)
    SECOND_TIP, SECOND_BODY = (half_rows, tip), (half_rows + tip, half_rows - tip)
    TIPS = (half_rows - tip, 2 * tip)
    me = lax.axis_index("docs")
    core = lax.rem(me, CORES)
    y = lax.rem(me // CORES, 2)
    z = me // (CORES * 2)
    mirrored = 2 * z >= planes
    end = (z == 0) | (z == planes - 1)
    mid = jnp.logical_not(end)

    def device(k, column, cc):
        zz = jnp.where(mirrored, planes - 1 - k, k)
        return (zz * 2 + column) * CORES + cc

    OUT, IN, SIDE, PAIR = range(4)
    AXIS = (0, 0, 1, 2)
    home = jnp.where(end, 0, 1)
    targets = (
        device(0, y, core),
        device(home + 1, y, core),
        device(home, 1 - y, core),
        device(home, y, 1 - core),
    )
    END_ORDER = ((0, 0), (1, 0), (0, 1), (2, 0), (1, 1), (3, 0), (2, 1), (3, 1))
    MID_ORDER = ((1, 0), (2, 0), (0, 0), (3, 0), (0, 1), (1, 1), (2, 1), (3, 1))

    up = (mid & mirrored, jnp.logical_not(mirrored), y == 0, core == 0)
    down = (mid & jnp.logical_not(mirrored), mirrored, y == 1, core == 1)
    barrier = pltpu.get_barrier_semaphore()
    for target, higher in zip(targets, up):
        @pl.when(higher)
        def _():
            pl.semaphore_signal(barrier, inc=1, device_id={"docs": target}, device_id_type=MESH)

    def rows_of(slot, cc, part):
        first, size = part
        first = (slot * CORES + cc) * rows + first
        return buf.at[pl.ds(pl.multiple_of(first, tip), size)]

    lower_count = sum(lower.astype(jnp.int32) for lower in down)
    @pl.when(lower_count > 0)
    def _():
        pl.semaphore_wait(barrier, lower_count)

    def data_copy(direction, slot, there, done, part, own=False):
        return pltpu.make_async_remote_copy(
            x_ref.at[pl.ds(*part)] if own else rows_of(slot, core, part), rows_of(there, core, part),
            send_sem.at[1 if direction == PAIR else 0], done,
            device_id={"docs": targets[direction]}, device_id_type=MESH,
        )

    def lab_copy(direction, slot, there, done, own=False):
        return pltpu.make_async_remote_copy(
            lab_ref if own else labs.at[slot * CORES + core], labs.at[there * CORES + core],
            lsend_sem.at[0], done,
            device_id={"docs": targets[direction]}, device_id_type=MESH,
        )

    def take(done, data_rows, labels=0):
        amount = meter.at[pl.ds(0, data_rows * row_units + labels)]
        pltpu.make_async_remote_copy(
            amount, amount, lsend_sem.at[0], done,
            device_id={"docs": targets[PAIR]}, device_id_type=MESH,
        ).wait_recv()

    class Role:
        def __init__(self, is_end):
            self.is_end = is_end
            self.order = END_ORDER if is_end else MID_ORDER

        def slot(self, k, other):
            return self.order.index((k, other))

        def done(self, k, other, part):
            if (k, other) == (3, 1):
                if self.is_end:
                    return recv_sem.at[11 if part in (FIRST_TIP, SECOND_TIP) else 10]
                return recv_sem.at[10 if part == SECOND else 11]
            if self.is_end:
                first = {(1, 0): 0, (0, 1): 2, (2, 0): 4, (1, 1): 6, (3, 0): 7, (2, 1): 9}[k, other]
                split = (k, other) not in ((1, 1), (2, 1))
            else:
                first = {(2, 0): 0, (0, 0): 2, (3, 0): 4, (0, 1): 6, (1, 1): 8, (2, 1): 9}[k, other]
                split = (k, other) not in ((1, 1), (2, 1))
            return recv_sem.at[first + (1 if split and part == SECOND else 0)]

        def receiver(self, direction, k, other):
            if direction == SIDE:
                return self, k, 1 - other
            if direction == PAIR:
                return self, k, other
            if direction == OUT:
                return at_end, k, other
            return at_mid, k if self.is_end else planes - 1 - k, other

        def send(self, k, other, part, directions, own=False):
            for direction in directions:
                role, kk, oo = self.receiver(direction, k, other)
                slot, there = self.slot(k, other), role.slot(kk, oo)
                done = pair_sem.at[(there + 1) // 2] if direction == PAIR else role.done(kk, oo, part)
                if part in (FIRST, FIRST_BODY, WHOLE):
                    lab_copy(direction, slot, there, done, own).start()
                data_copy(direction, slot, there, done, part, own).start()

        def arrived(self, k, other, part):
            take(self.done(k, other, part), part[1], 0 if part == SECOND else 1)

        def pass_on(self, k, other, part, directions):
            self.arrived(k, other, part)
            self.send(k, other, part, directions)

        def pair(self, k, other):
            self.send(k, other, WHOLE, (PAIR,))

        def gather(self, k, other):
            self.arrived(k, other, WHOLE)
            self.pair(k, other)

    at_end, at_mid = Role(True), Role(False)

    def start_own(direction):
        def by(role):
            k = 0 if role.is_end else 1
            for part in {SIDE: (SECOND, FIRST), PAIR: (WHOLE,)}.get(direction, (FIRST, SECOND)):
                role.send(k, 0, part, (direction,), own=True)

        if direction == OUT:
            by(at_mid)
        elif direction == PAIR:
            by(at_end)
        else:
            pl.when(end)(lambda: by(at_end))
            pl.when(mid)(lambda: by(at_mid))

    for direction, lower in enumerate(down):
        @pl.when(lower)
        def _():
            start_own(direction)
    for direction, lower in enumerate(down):
        @pl.when(lower)
        def _():
            pl.semaphore_signal(
                ready_sem.at[AXIS[direction]], inc=1,
                device_id={"docs": targets[direction]}, device_id_type=MESH,
            )
    own_data = pltpu.make_async_copy(x_ref, rows_of(0, core, WHOLE), own_sem.at[0])
    own_data.start()
    own_lab = pltpu.make_async_copy(lab_ref, labs.at[core], own_sem.at[1])
    own_lab.start()
    for direction, higher in reversed(tuple(enumerate(up))):
        @pl.when(higher)
        def _():
            pl.semaphore_wait(ready_sem.at[AXIS[direction]], 1)
            start_own(direction)

    own_lab.wait()
    label_column = jnp.transpose(
        jnp.broadcast_to(labs[core].astype(jnp.float32), (rows, rows))
    )[:, :1]
    own_data.wait()

    def from_pair(group, slots):
        take(pair_sem.at[group], slots * rows, slots)

    def masked_scores(slot, count):
        keys = count * CORES * rows
        values = buf[pl.ds(pl.multiple_of(slot * CORES * rows, rows), keys), :]
        mine = buf[pl.ds(pl.multiple_of(core * rows, rows), rows), :]
        tags = jnp.concatenate(
            [labs[slot * CORES + n].astype(jnp.float32) for n in range(count * CORES)], axis=1
        )
        scores = lax.dot_general(
            mine, values, (((1,), (1,)), ((), ())), preferred_element_type=jnp.float32
        ) * (kernel_gain / math.sqrt(width))
        return scores, label_column == tags, values

    def first_block():
        scores, near, values = masked_scores(0, 1)
        gap = lax.broadcasted_iota(jnp.int32, near.shape, 1) - lax.broadcasted_iota(jnp.int32, near.shape, 0)
        masked = jnp.where(near & (gap != core * rows), scores, neg_large)
        peak = jnp.maximum(jnp.max(masked, axis=1, keepdims=True), neg_start)
        weights = jnp.exp(masked - peak)
        row_max[...] = peak
        row_total[...] = jnp.sum(weights, axis=1, keepdims=True)
        acc[...] = jnp.dot(weights.astype(jnp.bfloat16), values, preferred_element_type=jnp.float32)

    def absorb(slot, count):
        scores, near, values = masked_scores(slot, count)
        masked = jnp.where(near, scores, neg_large)
        before = row_max[...]
        peak = jnp.maximum(before, jnp.max(masked, axis=1, keepdims=True))
        weights = jnp.exp(masked - peak)
        scale = jnp.exp(before - peak)
        total = row_total[...] * scale + jnp.sum(weights, axis=1, keepdims=True)
        gained = jnp.dot(weights.astype(jnp.bfloat16), values, preferred_element_type=jnp.float32)
        return peak, total, scale, gained

    from_pair(0, 1)
    first_block()

    def step(j, carry):
        @pl.when(end & (j == 1))
        def _():
            r = at_end
            r.pass_on(1, 0, FIRST, (SIDE,))
            r.pass_on(0, 1, SECOND, (IN,))
            r.pass_on(1, 0, SECOND, (SIDE,))
            r.pair(1, 0)
            r.pass_on(0, 1, FIRST, (IN,))
            r.pair(0, 1)
            r.pass_on(2, 0, FIRST, (SIDE,))

        @pl.when(end & (j == 2))
        def _():
            r = at_end
            r.pass_on(2, 0, SECOND, (SIDE,))
            r.pair(2, 0)
            r.gather(1, 1)
            r.arrived(3, 0, FIRST)
            r.send(3, 0, FIRST_BODY, (SIDE,))
            r.send(3, 0, FIRST_TIP, (SIDE,))

        @pl.when(end & (j == 3))
        def _():
            r = at_end
            r.arrived(3, 0, SECOND)
            r.pair(3, 0)
            r.gather(2, 1)
            take(recv_sem.at[10], rows - 2 * tip, 1)
            r.send(3, 1, FIRST_BODY, (PAIR,))
            r.send(3, 1, SECOND_BODY, (PAIR,))
            take(recv_sem.at[11], 2 * tip)
            r.send(3, 1, TIPS, (PAIR,))

        @pl.when(mid & (j == 1))
        def _():
            r = at_mid
            r.pass_on(2, 0, FIRST, (OUT, SIDE))
            r.pass_on(0, 0, FIRST, (IN,))
            r.pass_on(2, 0, SECOND, (OUT, SIDE))
            r.pair(2, 0)
            r.pass_on(0, 0, SECOND, (IN,))
            r.pair(0, 0)
            r.gather(1, 1)
            r.pass_on(3, 0, FIRST, (OUT, SIDE))
            r.pass_on(0, 1, SECOND, (IN,))

        @pl.when(mid & (j == 2))
        def _():
            r = at_mid
            r.pass_on(3, 0, SECOND, (OUT,))
            r.pair(3, 0)
            r.arrived(0, 1, FIRST)
            r.pair(0, 1)
            r.gather(2, 1)

        @pl.when(mid & (j == 3))
        def _():
            r = at_mid
            r.arrived(3, 1, SECOND)
            r.send(3, 1, SECOND_BODY, (OUT,))
            r.send(3, 1, SECOND_TIP, (OUT,))
            r.send(3, 1, SECOND, (PAIR,))
            r.arrived(3, 1, FIRST)
            r.send(3, 1, FIRST, (PAIR,))

        slot = 2 * j - 1
        from_pair(j, 2)
        peak, total, scale, gained = absorb(slot, 2)
        row_max[...] = peak
        row_total[...] = total
        acc[...] = acc[...] * scale + gained
        return carry

    lax.fori_loop(1, planes, step, 0)

    from_pair(planes, 1)
    peak, total, scale, gained = absorb(2 * planes - 1, 1)
    density = peak + jnp.log(total)
    dens_ref[...] = jnp.transpose(jnp.broadcast_to(density, (rows, rows)))[:1, :]
    inverse = 1.0 / total
    mean_ref[...] = ((acc[...] * scale + gained) * inverse).astype(mean_ref.dtype)

    def sent(done, amount):
        pltpu.make_async_remote_copy(
            amount, amount, done, pair_sem.at[0],
            device_id={"docs": targets[PAIR]}, device_id_type=MESH,
        ).wait_send()

    sent(send_sem.at[1], buf.at[pl.ds(0, 16 * half_rows)])

    @pl.when(end)
    def _():
        sent(send_sem.at[0], buf.at[pl.ds(0, 11 * half_rows)])
        sent(lsend_sem.at[0], labs.at[pl.ds(0, 14)])

    @pl.when(mid)
    def _():
        sent(send_sem.at[0], buf.at[pl.ds(0, 17 * half_rows)])
        sent(lsend_sem.at[0], labs.at[pl.ds(0, 16)])


def publish_kernel(dens_ref, mean_ref, dens_out, mean_out, sem):
    copies = (
        pltpu.make_async_copy(mean_ref, mean_out, sem.at[0]),
        pltpu.make_async_copy(dens_ref, dens_out, sem.at[1]),
    )
    for copy in copies:
        copy.start()
    for copy in copies:
        copy.wait()


def publish(density, mean):
    held = [pltpu.with_memory_space_constraint(a, pltpu.VMEM) for a in (density, mean)]
    return pl.pallas_call(
        publish_kernel,
        out_shape=tuple(jax.ShapeDtypeStruct(a.shape, a.dtype) for a in (density, mean)),
        in_specs=[pl.BlockSpec(memory_space=pltpu.VMEM)] * 2,
        out_specs=(pl.BlockSpec(memory_space=pltpu.HBM),) * 2,
        scratch_shapes=[pltpu.SemaphoreType.DMA((2,))],
    )(*held)


def general_call(device_count, rows, width):
    grid_slow, grid_fast = chip_grid(device_count)
    chips = device_count // CORES
    vmem = pl.BlockSpec(memory_space=pltpu.VMEM)
    return pl.pallas_call(
        functools.partial(kernel, grid_slow, grid_fast),
        out_shape=(
            pltpu.VMEM((1, rows), jnp.float32),
            pltpu.VMEM((rows, width), jnp.bfloat16),
        ),
        in_specs=[pl.BlockSpec(memory_space=pl.ANY), pl.BlockSpec(memory_space=pl.ANY)],
        out_specs=(vmem, vmem),
        scratch_shapes=[
            pltpu.VMEM((device_count * rows, width), jnp.bfloat16),
            pltpu.VMEM((device_count, 1, rows), jnp.int32),
            pltpu.VMEM((rows, width), jnp.bfloat16),
            pltpu.VMEM((rows, width), jnp.float32),
            pltpu.VMEM((rows, 1), jnp.float32),
            pltpu.VMEM((rows, 1), jnp.float32),
            pltpu.SemaphoreType.DMA((5, chips * PIECES)),
            pltpu.SemaphoreType.DMA((device_count * PIECES,)),
            pltpu.SemaphoreType.DMA((5, chips)),
            pltpu.SemaphoreType.DMA((device_count,)),
            pltpu.SemaphoreType.DMA((PIECES + 1,)),
            pltpu.SemaphoreType.DMA((1,)),
        ],
        compiler_params=pltpu.CompilerParams(collective_id=0, has_side_effects=True),
    )


def folded_call(device_count, rows, width):
    chips = device_count // CORES
    vmem = pl.BlockSpec(memory_space=pltpu.VMEM)
    return pl.pallas_call(
        functools.partial(folded_kernel, chips // 2),
        out_shape=(
            pltpu.VMEM((1, rows), jnp.float32),
            pltpu.VMEM((rows, width), jnp.bfloat16),
        ),
        in_specs=[pl.BlockSpec(memory_space=pl.ANY), pl.BlockSpec(memory_space=pl.ANY)],
        out_specs=(vmem, vmem),
        scratch_shapes=[
            pltpu.VMEM((device_count * rows, width), jnp.bfloat16),
            pltpu.VMEM((device_count, 1, rows), jnp.int32),
            pltpu.VMEM((width + CORES, 1, rows), jnp.int32),
            pltpu.VMEM((rows, width), jnp.float32),
            pltpu.VMEM((rows, 1), jnp.float32),
            pltpu.VMEM((rows, 1), jnp.float32),
            pltpu.SemaphoreType.DMA((2,)),
            pltpu.SemaphoreType.DMA((1,)),
            pltpu.SemaphoreType.DMA((12,)),
            pltpu.SemaphoreType.DMA((chips // 2 + 1,)),
            pltpu.SemaphoreType.DMA((2,)),
            pltpu.SemaphoreType.REGULAR((3,)),
        ],
        compiler_params=pltpu.CompilerParams(collective_id=0, has_side_effects=True),
    )


def per_device(device_count, embeddings, labels, row_slot):
    rows, width = embeddings.shape
    call = folded_call if chip_grid(device_count) == FOLDED_GRID else general_call
    density, mean = call(device_count, rows, width)(embeddings, labels.reshape(1, rows))
    density, mean = publish(density, mean)
    return density.reshape(rows), mean


def solution(mesh):
    return jax.shard_map(
        functools.partial(per_device, mesh.shape["docs"]),
        mesh=mesh,
        in_specs=(P(("groups", "docs"), None), P(("groups", "docs")), P(("groups", "docs"))),
        out_specs=(P(("groups", "docs")), P(("groups", "docs"), None)),
        check_vma=False,
    )
```

```python
import functools
import math

import jax
import jax.numpy as jnp
from jax import lax
from jax.experimental import pallas as pl
from jax.experimental.pallas import tpu as pltpu
from jax.sharding import PartitionSpec as P

MESH = pl.DeviceIdType.MESH
CORES = 2
PIECES = 2
HALVES = 1
FOLDED_GRID = (4, 2)

neg_large = -1e30
neg_start = -1e29
kernel_gain = 4.0


def chip_grid(device_count):
    chips = device_count // CORES
    fast = 1
    while (2 * fast) * (2 * fast) <= chips and chips % (2 * fast) == 0:
        fast *= 2
    return chips // fast, fast


def kernel(
    grid_slow, grid_fast, x_ref, lab_ref, dens_ref, mean_ref,
    buf, labs, mine, acc, row_max, row_total,
    send_sem, recv_sem, lsend_sem, lrecv_sem, own_sem, own_lab_sem,
):
    rows, width = x_ref.shape
    part = rows // PIECES
    group = PIECES // HALVES
    half_rows = rows // HALVES
    keys = CORES * half_rows
    me = lax.axis_index("docs")
    core = lax.rem(me, CORES)
    chip = me // CORES
    y = lax.rem(chip, grid_fast)
    z = chip // grid_fast

    def device(zz, yy, cc):
        return (zz * grid_fast + yy) * CORES + cc

    targets = (
        (z > 0, device(z - 1, y, core)),
        (z < grid_slow - 1, device(z + 1, y, core)),
        (y > 0, device(z, y - 1, core)),
        (y < grid_fast - 1, device(z, y + 1, core)),
        (z >= 0, device(z, y, 1 - core)),
    )

    barrier = pltpu.get_barrier_semaphore()
    for there, target in targets:
        @pl.when(there)
        def _():
            pl.semaphore_signal(barrier, inc=1, device_id={"docs": target}, device_id_type=MESH)

    def data_of(zz, yy, cc, piece):
        where = ((zz * grid_fast + yy) * HALVES + piece // group) * CORES + cc
        return buf.at[pl.ds(pl.multiple_of((where * group + lax.rem(piece, group)) * part, part), part)]

    own_copies = [pltpu.make_async_copy(x_ref, mine, own_sem.at[PIECES])]
    for piece in range(PIECES):
        own_copies.append(
            pltpu.make_async_copy(
                x_ref.at[pl.ds(piece * part, part)], data_of(z, y, core, piece), own_sem.at[piece]
            )
        )
    own_copies.append(pltpu.make_async_copy(lab_ref, labs.at[me], own_lab_sem.at[0]))
    for copy in own_copies:
        copy.start()
    pl.semaphore_wait(barrier, sum(there.astype(jnp.int32) for there, _ in targets))

    def data_copy(direction, zz, yy, piece, own):
        data = data_of(zz, yy, core, piece)
        return pltpu.make_async_remote_copy(
            x_ref.at[pl.ds(piece * part, part)] if own else data, data,
            send_sem.at[direction, (zz * grid_fast + yy) * PIECES + piece],
            recv_sem.at[device(zz, yy, core) * PIECES + piece],
            device_id={"docs": targets[direction][1]}, device_id_type=MESH,
        )

    def lab_copy(direction, zz, yy, own):
        slot = device(zz, yy, core)
        return pltpu.make_async_remote_copy(
            lab_ref if own else labs.at[slot], labs.at[slot],
            lsend_sem.at[direction, zz * grid_fast + yy], lrecv_sem.at[slot],
            device_id={"docs": targets[direction][1]}, device_id_type=MESH,
        )

    def each(directions, wanted, zz, yy, piece, own, act):
        for direction, want in zip(directions, wanted):
            @pl.when(jnp.logical_and(targets[direction][0], want))
            def _():
                @pl.when(piece == 0)
                def _():
                    act(lab_copy(direction, zz, yy, own))
                act(data_copy(direction, zz, yy, piece, own))

    start = lambda copy: copy.start()
    finish = lambda copy: copy.wait_send()

    def arrived(zz, yy, cc, piece):
        slot = device(zz, yy, cc)
        @pl.when(piece == 0)
        def _():
            pltpu.make_async_remote_copy(
                labs.at[slot], labs.at[slot], lsend_sem.at[0, 0], lrecv_sem.at[slot],
                device_id={"docs": targets[4][1]}, device_id_type=MESH,
            ).wait_recv()
        data = data_of(zz, yy, cc, piece)
        pltpu.make_async_remote_copy(
            data, data, send_sem.at[0, 0], recv_sem.at[slot * PIECES + piece],
            device_id={"docs": targets[4][1]}, device_id_type=MESH,
        ).wait_recv()

    yes = z >= 0
    for piece in range(PIECES):
        each((2, 3, 0, 1, 4), (yes,) * 5, z, y, piece, True, start)

    row_max[...] = jnp.full_like(row_max, neg_large)
    row_total[...] = jnp.zeros_like(row_total)
    acc[...] = jnp.zeros_like(acc)
    own_copies[-1].wait()
    label_column = jnp.transpose(
        jnp.broadcast_to(labs[me].astype(jnp.float32), (rows, rows))
    )[:, :1]
    column = lax.broadcasted_iota(jnp.int32, (rows, keys), 1)
    gap = (
        column + (column // half_rows) * (rows - half_rows)
        - lax.broadcasted_iota(jnp.int32, (rows, keys), 0)
    )
    for copy in own_copies[:-1]:
        copy.wait()

    def compute(zz, yy, half):
        where = zz * grid_fast + yy
        values = buf[pl.ds(pl.multiple_of((where * HALVES + half) * keys, keys), keys), :]
        tags = []
        for cc in range(CORES):
            tag = labs[where * CORES + cc].astype(jnp.float32)
            pieces = [tag[:, h * half_rows:(h + 1) * half_rows] for h in range(HALVES)]
            picked = pieces[0]
            for h in range(1, HALVES):
                picked = jnp.where(half == h, pieces[h], picked)
            tags.append(picked)
        tags = jnp.concatenate(tags, axis=1)
        scores = lax.dot_general(
            mine[...], values, (((1,), (1,)), ((), ())), preferred_element_type=jnp.float32
        ) * (kernel_gain / math.sqrt(width))
        self_gap = jnp.where(where == chip, core * rows - half * half_rows, CORES * rows)
        absorb(scores, (label_column == tags) & (gap != self_gap), values)

    def compute_core(zz, yy, cc):
        slot = device(zz, yy, cc)
        values = buf[pl.ds(pl.multiple_of(slot * rows, rows), rows), :]
        scores = lax.dot_general(
            mine[...], values, (((1,), (1,)), ((), ())), preferred_element_type=jnp.float32
        ) * (kernel_gain / math.sqrt(width))
        absorb(scores, label_column == labs[slot].astype(jnp.float32), values)

    def absorb(scores, near, values):
        masked = jnp.where(near, scores, neg_large)
        before = row_max[...]
        peak = jnp.maximum(before, jnp.max(masked, axis=1, keepdims=True))
        weights = jnp.where(near, jnp.exp(masked - peak), 0.0)
        scale = jnp.exp(before - peak)
        row_max[...] = peak
        row_total[...] = row_total[...] * scale + jnp.sum(weights, axis=1, keepdims=True)
        acc[...] = acc[...] * scale + jnp.dot(
            weights.astype(jnp.bfloat16), values, preferred_element_type=jnp.float32
        )

    def meet(zz, yy, half):
        def one(p, carry):
            arrived(zz, yy, 1 - core, half * group + p)
            return carry
        lax.fori_loop(0, group, one, 0)
        compute(zz, yy, half)

    def visited(distance, side, reach, origin):
        place = origin + jnp.where(side == 0, -distance, distance)
        inside = (distance >= 0) & (distance < reach) & (place >= 0) & (place < reach)
        return place, inside & jnp.logical_or(distance > 0, side == 0)

    def other_columns(body):
        if grid_fast == 2:
            body(1 - y)
            return
        def one(i, carry):
            yy, valid = visited(i // 2 + 1, lax.rem(i, 2), grid_fast, y)
            @pl.when(valid)
            def _():
                body(yy)
            return carry
        lax.fori_loop(0, 2 * (grid_fast - 1), one, 0)

    def along(zz, piece, side, act):
        each((2, 3, 0, 1, 4), (yes, yes, side == 1, side == 0, yes), zz, y, piece, False, act)

    def across(zz, yy, piece, act):
        each((2, 3, 4), (yy > y, yy < y, yes), zz, yy, piece, False, act)

    def receive(zz, yy, piece):
        arrived(zz, yy, core, piece)
        across(zz, yy, piece, start)

    farthest = jnp.where(2 * z >= grid_slow, 0, grid_slow - 1)

    def event(e, carry):
        distance = e // (2 * PIECES)
        piece = lax.rem(e // 2, PIECES)
        side = lax.rem(e, 2)
        half = piece // group

        @pl.when(e == 2 * PIECES * grid_slow)
        def _():
            for p in range(PIECES):
                each((2, 3, 0, 1, 4), (yes,) * 5, z, y, p, True, finish)

        zz, valid = visited(distance, side, grid_slow, z)
        @pl.when(valid & (distance > 0))
        def _():
            arrived(zz, y, core, piece)
            along(zz, piece, side, start)

        z1, valid1 = visited(distance - 1, side, grid_slow, z)
        z2, valid2 = visited(distance - 2, side, grid_slow, z)
        @pl.when(valid2)
        def _():
            other_columns(lambda yy: receive(z2, yy, piece))
            @pl.when(distance > 2)
            def _():
                along(z2, piece, side, finish)

        z3, valid3 = visited(distance - 3, side, grid_slow, z)
        @pl.when(valid3)
        def _():
            other_columns(lambda yy: across(z3, yy, piece, finish))

        near = valid1 & (lax.rem(piece, group) == 0)
        if grid_fast == 2:
            far = valid2 & (lax.rem(piece, group) == group - 1) & (z2 != farthest)
            @pl.when(near | far)
            def _():
                def one(i, carry):
                    @pl.when(jnp.where(i == 0, near, far))
                    def _():
                        meet(jnp.where(i == 0, z1, z2), jnp.where(i == 0, y, 1 - y), half)
                    return carry
                lax.fori_loop(0, 2, one, 0)
        else:
            @pl.when(near)
            def _():
                meet(z1, y, half)
            @pl.when(valid2 & (lax.rem(piece, group) == group - 1))
            def _():
                other_columns(lambda yy: meet(z2, yy, half))
        return carry

    lax.fori_loop(0, 2 * PIECES * (grid_slow + 2), event, 0)
    if grid_fast == 2:
        def last_pair(i, carry):
            cc = jnp.where(i == 0, core, 1 - core)
            @pl.when(i == 1)
            def _():
                for p in range(PIECES):
                    arrived(farthest, 1 - y, 1 - core, p)
            compute_core(farthest, 1 - y, cc)
            return carry
        lax.fori_loop(0, CORES, last_pair, 0)

    total = row_total[...]
    density = row_max[...] + jnp.log(total)
    dens_ref[...] = jnp.transpose(jnp.broadcast_to(density, (rows, rows)))[:1, :]
    mean_ref[...] = (acc[...] / total).astype(mean_ref.dtype)

    for e in range(2 * PIECES):
        last, valid = visited(grid_slow - 1, e % 2, grid_slow, z)
        @pl.when(valid)
        def _():
            other_columns(lambda yy: across(last, yy, e // 2, finish))


def folded_kernel(
    planes, x_ref, lab_ref, dens_ref, mean_ref,
    buf, labs, meter, acc, row_max, row_total,
    send_sem, lsend_sem, recv_sem, pair_sem, own_sem, ready_sem,
):
    rows, width = x_ref.shape
    row_units = width * x_ref.dtype.itemsize // (rows * lab_ref.dtype.itemsize)
    half_rows = rows // 2
    tip = rows // 8
    FIRST, SECOND, WHOLE = (0, half_rows), (half_rows, half_rows), (0, rows)
    FIRST_A, FIRST_B = (0, half_rows // 2), (half_rows // 2, half_rows // 2 - tip)
    FIRST_TIP, SECOND_TIP = (half_rows - tip, tip), (half_rows, tip)
    SECOND_B, SECOND_A = (half_rows + tip, half_rows // 2 - tip), (rows - half_rows // 2, half_rows // 2)
    me = lax.axis_index("docs")
    core = lax.rem(me, CORES)
    y = lax.rem(me // CORES, 2)
    z = me // (CORES * 2)
    mirrored = 2 * z >= planes
    end = (z == 0) | (z == planes - 1)
    mid = jnp.logical_not(end)

    def device(k, column, cc):
        zz = jnp.where(mirrored, planes - 1 - k, k)
        return (zz * 2 + column) * CORES + cc

    OUT, IN, SIDE, PAIR, OUT_TWIN, SIDE_TWIN = range(6)
    AXIS = (0, 0, 1, 2)
    home = jnp.where(end, 0, 1)
    targets = (
        device(0, y, core),
        device(home + 1, y, core),
        device(home, 1 - y, core),
        device(home, y, 1 - core),
        device(0, y, 1 - core),
        device(home, 1 - y, 1 - core),
    )
    END_ORDER = ((0, 0), (1, 0), (0, 1), (2, 0), (1, 1), (3, 0), (2, 1), (3, 1))
    MID_ORDER = ((1, 0), (2, 0), (0, 0), (3, 0), (0, 1), (1, 1), (2, 1), (3, 1))

    up = (mid & mirrored, jnp.logical_not(mirrored), y == 0, core == 0)
    down = (mid & jnp.logical_not(mirrored), mirrored, y == 1, core == 1)
    barrier = pltpu.get_barrier_semaphore()
    for target, higher in zip(targets, up):
        @pl.when(higher)
        def _():
            pl.semaphore_signal(barrier, inc=1, device_id={"docs": target}, device_id_type=MESH)

    def rows_of(slot, cc, part):
        first, size = part
        first = (slot * CORES + cc) * rows + first
        return buf.at[pl.ds(pl.multiple_of(first, tip), size)]

    lower_count = sum(lower.astype(jnp.int32) for lower in down)
    @pl.when(lower_count > 0)
    def _():
        pl.semaphore_wait(barrier, lower_count)

    def data_copy(direction, slot, there, done, part, own=False):
        return pltpu.make_async_remote_copy(
            x_ref.at[pl.ds(*part)] if own else rows_of(slot, core, part), rows_of(there, core, part),
            send_sem.at[1 if direction == PAIR else 0], done,
            device_id={"docs": targets[direction]}, device_id_type=MESH,
        )

    def lab_copy(direction, slot, there, done, own=False):
        return pltpu.make_async_remote_copy(
            lab_ref if own else labs.at[slot * CORES + core], labs.at[there * CORES + core],
            lsend_sem.at[0], done,
            device_id={"docs": targets[direction]}, device_id_type=MESH,
        )

    def take(done, data_rows, labels=0):
        amount = meter.at[pl.ds(0, data_rows * row_units + labels)]
        pltpu.make_async_remote_copy(
            amount, amount, lsend_sem.at[0], done,
            device_id={"docs": targets[PAIR]}, device_id_type=MESH,
        ).wait_recv()

    class Role:
        def __init__(self, is_end):
            self.is_end = is_end
            self.order = END_ORDER if is_end else MID_ORDER

        def slot(self, k, other):
            return self.order.index((k, other))

        def done(self, k, other, part):
            if (k, other) == (3, 1):
                if self.is_end:
                    return recv_sem.at[10 if part in (FIRST_A, SECOND_A) else 11 if part in (FIRST_B, SECOND_B) else 12]
                return recv_sem.at[10 if part == SECOND else 11]
            if self.is_end:
                first = {(1, 0): 0, (0, 1): 2, (2, 0): 4, (1, 1): 6, (3, 0): 7, (2, 1): 9}[k, other]
                split = (k, other) not in ((1, 1), (2, 1))
            else:
                first = {(2, 0): 0, (0, 0): 2, (3, 0): 4, (0, 1): 6, (1, 1): 8, (2, 1): 9}[k, other]
                split = (k, other) not in ((1, 1), (2, 1))
            return recv_sem.at[first + (1 if split and part == SECOND else 0)]

        def receiver(self, direction, k, other):
            if direction in (SIDE, SIDE_TWIN):
                return self, k, 1 - other
            if direction == PAIR:
                return self, k, other
            if direction in (OUT, OUT_TWIN):
                return at_end, k, other
            return at_mid, k if self.is_end else planes - 1 - k, other

        def send(self, k, other, part, directions, own=False):
            for direction in directions:
                role, kk, oo = self.receiver(direction, k, other)
                slot, there = self.slot(k, other), role.slot(kk, oo)
                done = pair_sem.at[(there + 1) // 2] if direction == PAIR else role.done(kk, oo, part)
                if part in (FIRST, FIRST_A, WHOLE):
                    lab_copy(direction, slot, there, done, own).start()
                data_copy(direction, slot, there, done, part, own).start()

        def arrived(self, k, other, part):
            take(self.done(k, other, part), part[1], 0 if part == SECOND else 1)

        def pass_on(self, k, other, part, directions):
            self.arrived(k, other, part)
            self.send(k, other, part, directions)

        def pair(self, k, other):
            self.send(k, other, WHOLE, (PAIR,))

        def gather(self, k, other):
            self.arrived(k, other, WHOLE)
            self.pair(k, other)

    at_end, at_mid = Role(True), Role(False)

    def start_own(direction):
        def by(role):
            k = 0 if role.is_end else 1
            for part in {SIDE: (SECOND, FIRST), PAIR: (WHOLE,)}.get(direction, (FIRST, SECOND)):
                role.send(k, 0, part, (direction,), own=True)

        if direction == OUT:
            by(at_mid)
        elif direction == PAIR:
            by(at_end)
        else:
            pl.when(end)(lambda: by(at_end))
            pl.when(mid)(lambda: by(at_mid))

    for direction, lower in enumerate(down):
        @pl.when(lower)
        def _():
            start_own(direction)
    for direction, lower in enumerate(down):
        @pl.when(lower)
        def _():
            pl.semaphore_signal(
                ready_sem.at[AXIS[direction]], inc=1,
                device_id={"docs": targets[direction]}, device_id_type=MESH,
            )
    own_data = pltpu.make_async_copy(x_ref, rows_of(0, core, WHOLE), own_sem.at[0])
    own_data.start()
    own_lab = pltpu.make_async_copy(lab_ref, labs.at[core], own_sem.at[0])
    own_lab.start()
    for direction, higher in reversed(tuple(enumerate(up))):
        @pl.when(higher)
        def _():
            pl.semaphore_wait(ready_sem.at[AXIS[direction]], 1)
            start_own(direction)

    own_amount = meter.at[pl.ds(0, rows * row_units + 1)]
    pltpu.make_async_copy(own_amount, own_amount, own_sem.at[0]).wait()
    label_column = jnp.transpose(
        jnp.broadcast_to(labs[core].astype(jnp.float32), (rows, rows))
    )[:, :1]

    def from_pair(group, slots):
        take(pair_sem.at[group], slots * rows, slots)

    def masked_scores(slot, count):
        keys = count * CORES * rows
        values = buf[pl.ds(pl.multiple_of(slot * CORES * rows, rows), keys), :]
        mine = buf[pl.ds(pl.multiple_of(core * rows, rows), rows), :]
        tags = jnp.concatenate(
            [labs[slot * CORES + n].astype(jnp.float32) for n in range(count * CORES)], axis=1
        )
        scores = lax.dot_general(
            mine, values, (((1,), (1,)), ((), ())), preferred_element_type=jnp.float32
        ) * (kernel_gain / math.sqrt(width))
        return scores, label_column == tags, values

    def first_block():
        scores, near, values = masked_scores(0, 1)
        gap = lax.broadcasted_iota(jnp.int32, near.shape, 1) - lax.broadcasted_iota(jnp.int32, near.shape, 0)
        masked = jnp.where(near & (gap != core * rows), scores, neg_large)
        peak = jnp.maximum(jnp.max(masked, axis=1, keepdims=True), neg_start)
        weights = jnp.exp(masked - peak)
        row_max[...] = peak
        row_total[...] = jnp.sum(weights, axis=1, keepdims=True)
        acc[...] = jnp.dot(weights.astype(jnp.bfloat16), values, preferred_element_type=jnp.float32)

    def absorb(slot, count):
        scores, near, values = masked_scores(slot, count)
        masked = jnp.where(near, scores, neg_large)
        before = row_max[...]
        peak = jnp.maximum(before, jnp.max(masked, axis=1, keepdims=True))
        weights = jnp.exp(masked - peak)
        scale = jnp.exp(before - peak)
        total = row_total[...] * scale + jnp.sum(weights, axis=1, keepdims=True)
        gained = jnp.dot(weights.astype(jnp.bfloat16), values, preferred_element_type=jnp.float32)
        return peak, total, scale, gained

    from_pair(0, 1)
    first_block()

    def step(j, carry):
        @pl.when(end & (j == 1))
        def _():
            r = at_end
            r.pass_on(1, 0, FIRST, (SIDE,))
            r.pass_on(0, 1, SECOND, (IN,))
            r.pass_on(1, 0, SECOND, (SIDE,))
            r.pair(1, 0)
            r.pass_on(0, 1, FIRST, (IN,))
            r.pair(0, 1)
            r.pass_on(2, 0, FIRST, (SIDE,))

        @pl.when(end & (j == 2))
        def _():
            r = at_end
            r.pass_on(2, 0, SECOND, (SIDE,))
            r.pair(2, 0)
            r.gather(1, 1)
            r.arrived(3, 0, FIRST)
            r.send(3, 0, FIRST_A, (SIDE,))
            r.send(3, 0, FIRST_B, (SIDE,))
            r.send(3, 0, FIRST_TIP, (SIDE, SIDE_TWIN))

        @pl.when(end & (j == 3))
        def _():
            r = at_end
            r.arrived(3, 0, SECOND)
            r.pair(3, 0)
            r.gather(2, 1)
            take(recv_sem.at[10], half_rows, 1)
            r.send(3, 1, FIRST_A, (PAIR,))
            r.send(3, 1, SECOND_A, (PAIR,))
            take(recv_sem.at[11], half_rows - 2 * tip)
            r.send(3, 1, FIRST_B, (PAIR,))
            r.send(3, 1, SECOND_B, (PAIR,))

        @pl.when(mid & (j == 1))
        def _():
            r = at_mid
            r.pass_on(2, 0, FIRST, (OUT, SIDE))
            r.pass_on(0, 0, FIRST, (IN,))
            r.pass_on(2, 0, SECOND, (OUT, SIDE))
            r.pair(2, 0)
            r.pass_on(0, 0, SECOND, (IN,))
            r.pair(0, 0)
            r.gather(1, 1)
            r.pass_on(3, 0, FIRST, (OUT, SIDE))
            r.pass_on(0, 1, SECOND, (IN,))

        @pl.when(mid & (j == 2))
        def _():
            r = at_mid
            r.pass_on(3, 0, SECOND, (OUT,))
            r.pair(3, 0)
            r.arrived(0, 1, FIRST)
            r.pair(0, 1)
            r.gather(2, 1)

        @pl.when(mid & (j == 3))
        def _():
            r = at_mid
            r.arrived(3, 1, SECOND)
            r.send(3, 1, SECOND_A, (OUT,))
            r.send(3, 1, SECOND_B, (OUT,))
            r.send(3, 1, SECOND_TIP, (OUT, OUT_TWIN))
            r.send(3, 1, SECOND, (PAIR,))
            r.arrived(3, 1, FIRST)
            r.send(3, 1, FIRST, (PAIR,))

        slot = 2 * j - 1
        from_pair(j, 2)
        peak, total, scale, gained = absorb(slot, 2)
        row_max[...] = peak
        row_total[...] = total
        acc[...] = acc[...] * scale + gained
        return carry

    lax.fori_loop(1, planes, step, 0)

    @pl.when(end)
    def _():
        take(recv_sem.at[12], 4 * tip)
        take(pair_sem.at[planes], rows - 2 * tip, 1)

    @pl.when(mid)
    def _():
        from_pair(planes, 1)

    parts = []
    for cc in range(CORES):
        values = buf[pl.ds(((2 * planes - 1) * CORES + cc) * rows, rows), :]
        scores = lax.dot_general(
            buf[pl.ds(pl.multiple_of(core * rows, rows), rows), :], values,
            (((1,), (1,)), ((), ())), preferred_element_type=jnp.float32,
        ) * (kernel_gain / math.sqrt(width))
        tags = labs[(2 * planes - 1) * CORES + cc].astype(jnp.float32)
        parts.append((jnp.where(label_column == tags, scores, neg_large), values))
    before = row_max[...]
    peak = jnp.maximum(before, jnp.max(jnp.maximum(parts[0][0], parts[1][0]), axis=1, keepdims=True))
    scale = jnp.exp(before - peak)
    weights = [jnp.exp(masked - peak) for masked, _ in parts]
    total = row_total[...] * scale + jnp.sum(weights[0] + weights[1], axis=1, keepdims=True)
    inverse = 1.0 / total
    gained = sum(
        jnp.dot(w.astype(jnp.bfloat16), values, preferred_element_type=jnp.float32)
        for w, (_, values) in zip(weights, parts)
    )
    mean_ref[...] = ((acc[...] * scale + gained) * inverse).astype(mean_ref.dtype)
    density = peak + jnp.log(total)
    dens_ref[...] = jnp.transpose(jnp.broadcast_to(density, (rows, rows)))[:1, :]

    def sent(done, amount):
        pltpu.make_async_remote_copy(
            amount, amount, done, pair_sem.at[0],
            device_id={"docs": targets[PAIR]}, device_id_type=MESH,
        ).wait_send()

    @pl.when(end)
    def _():
        sent(send_sem.at[0], buf.at[pl.ds(0, 11 * half_rows + tip)])
        sent(send_sem.at[1], buf.at[pl.ds(0, 16 * half_rows - 2 * tip)])
        sent(lsend_sem.at[0], labs.at[pl.ds(0, 14)])

    @pl.when(mid)
    def _():
        sent(send_sem.at[0], buf.at[pl.ds(0, 17 * half_rows + tip)])
        sent(send_sem.at[1], buf.at[pl.ds(0, 16 * half_rows)])
        sent(lsend_sem.at[0], labs.at[pl.ds(0, 16)])


def publish_kernel(dens_ref, mean_ref, dens_out, mean_out, sem):
    copies = (
        pltpu.make_async_copy(mean_ref, mean_out, sem.at[0]),
        pltpu.make_async_copy(dens_ref, dens_out, sem.at[1]),
    )
    for copy in copies:
        copy.start()
    for copy in copies:
        copy.wait()


def publish(density, mean):
    held = [pltpu.with_memory_space_constraint(a, pltpu.VMEM) for a in (density, mean)]
    return pl.pallas_call(
        publish_kernel,
        out_shape=tuple(jax.ShapeDtypeStruct(a.shape, a.dtype) for a in (density, mean)),
        in_specs=[pl.BlockSpec(memory_space=pltpu.VMEM)] * 2,
        out_specs=(pl.BlockSpec(memory_space=pltpu.HBM),) * 2,
        scratch_shapes=[pltpu.SemaphoreType.DMA((2,))],
    )(*held)


def general_call(device_count, rows, width):
    grid_slow, grid_fast = chip_grid(device_count)
    chips = device_count // CORES
    vmem = pl.BlockSpec(memory_space=pltpu.VMEM)
    return pl.pallas_call(
        functools.partial(kernel, grid_slow, grid_fast),
        out_shape=(
            pltpu.VMEM((1, rows), jnp.float32),
            pltpu.VMEM((rows, width), jnp.bfloat16),
        ),
        in_specs=[pl.BlockSpec(memory_space=pl.ANY), pl.BlockSpec(memory_space=pl.ANY)],
        out_specs=(vmem, vmem),
        scratch_shapes=[
            pltpu.VMEM((device_count * rows, width), jnp.bfloat16),
            pltpu.VMEM((device_count, 1, rows), jnp.int32),
            pltpu.VMEM((rows, width), jnp.bfloat16),
            pltpu.VMEM((rows, width), jnp.float32),
            pltpu.VMEM((rows, 1), jnp.float32),
            pltpu.VMEM((rows, 1), jnp.float32),
            pltpu.SemaphoreType.DMA((5, chips * PIECES)),
            pltpu.SemaphoreType.DMA((device_count * PIECES,)),
            pltpu.SemaphoreType.DMA((5, chips)),
            pltpu.SemaphoreType.DMA((device_count,)),
            pltpu.SemaphoreType.DMA((PIECES + 1,)),
            pltpu.SemaphoreType.DMA((1,)),
        ],
        compiler_params=pltpu.CompilerParams(collective_id=0, has_side_effects=True),
    )


def folded_call(device_count, rows, width):
    chips = device_count // CORES
    vmem = pl.BlockSpec(memory_space=pltpu.VMEM)
    return pl.pallas_call(
        functools.partial(folded_kernel, chips // 2),
        out_shape=(
            pltpu.VMEM((1, rows), jnp.float32),
            pltpu.VMEM((rows, width), jnp.bfloat16),
        ),
        in_specs=[pl.BlockSpec(memory_space=pl.ANY), pl.BlockSpec(memory_space=pl.ANY)],
        out_specs=(vmem, vmem),
        scratch_shapes=[
            pltpu.VMEM((device_count * rows, width), jnp.bfloat16),
            pltpu.VMEM((device_count, 1, rows), jnp.int32),
            pltpu.VMEM((width + CORES, 1, rows), jnp.int32),
            pltpu.VMEM((rows, width), jnp.float32),
            pltpu.VMEM((rows, 1), jnp.float32),
            pltpu.VMEM((rows, 1), jnp.float32),
            pltpu.SemaphoreType.DMA((2,)),
            pltpu.SemaphoreType.DMA((1,)),
            pltpu.SemaphoreType.DMA((13,)),
            pltpu.SemaphoreType.DMA((chips // 2 + 1,)),
            pltpu.SemaphoreType.DMA((1,)),
            pltpu.SemaphoreType.REGULAR((3,)),
        ],
        compiler_params=pltpu.CompilerParams(collective_id=0, has_side_effects=True),
    )


def per_device(device_count, embeddings, labels, row_slot):
    rows, width = embeddings.shape
    call = folded_call if chip_grid(device_count) == FOLDED_GRID else general_call
    density, mean = call(device_count, rows, width)(embeddings, labels.reshape(1, rows))
    density, mean = publish(density, mean)
    return density.reshape(rows), mean


def solution(mesh):
    return jax.shard_map(
        functools.partial(per_device, mesh.shape["docs"]),
        mesh=mesh,
        in_specs=(P(("groups", "docs"), None), P(("groups", "docs")), P(("groups", "docs"))),
        out_specs=(P(("groups", "docs")), P(("groups", "docs"), None)),
        check_vma=False,
    )
```

```python
import functools
import math

import jax
import jax.numpy as jnp
from jax import lax
from jax.experimental import pallas as pl
from jax.experimental.pallas import tpu as pltpu
from jax.sharding import PartitionSpec as P

MESH = pl.DeviceIdType.MESH
CORES = 2
PIECES = 2
HALVES = 1
FOLDED_GRID = (4, 2)

neg_large = -1e30
neg_start = -1e29
kernel_gain = 4.0


def chip_grid(device_count):
    chips = device_count // CORES
    fast = 1
    while (2 * fast) * (2 * fast) <= chips and chips % (2 * fast) == 0:
        fast *= 2
    return chips // fast, fast


def kernel(
    grid_slow, grid_fast, x_ref, lab_ref, dens_ref, mean_ref,
    buf, labs, mine, acc, row_max, row_total,
    send_sem, recv_sem, lsend_sem, lrecv_sem, own_sem, own_lab_sem,
):
    rows, width = x_ref.shape
    part = rows // PIECES
    group = PIECES // HALVES
    half_rows = rows // HALVES
    keys = CORES * half_rows
    me = lax.axis_index("docs")
    core = lax.rem(me, CORES)
    chip = me // CORES
    y = lax.rem(chip, grid_fast)
    z = chip // grid_fast

    def device(zz, yy, cc):
        return (zz * grid_fast + yy) * CORES + cc

    targets = (
        (z > 0, device(z - 1, y, core)),
        (z < grid_slow - 1, device(z + 1, y, core)),
        (y > 0, device(z, y - 1, core)),
        (y < grid_fast - 1, device(z, y + 1, core)),
        (z >= 0, device(z, y, 1 - core)),
    )

    barrier = pltpu.get_barrier_semaphore()
    for there, target in targets:
        @pl.when(there)
        def _():
            pl.semaphore_signal(barrier, inc=1, device_id={"docs": target}, device_id_type=MESH)

    def data_of(zz, yy, cc, piece):
        where = ((zz * grid_fast + yy) * HALVES + piece // group) * CORES + cc
        return buf.at[pl.ds(pl.multiple_of((where * group + lax.rem(piece, group)) * part, part), part)]

    own_copies = [pltpu.make_async_copy(x_ref, mine, own_sem.at[PIECES])]
    for piece in range(PIECES):
        own_copies.append(
            pltpu.make_async_copy(
                x_ref.at[pl.ds(piece * part, part)], data_of(z, y, core, piece), own_sem.at[piece]
            )
        )
    own_copies.append(pltpu.make_async_copy(lab_ref, labs.at[me], own_lab_sem.at[0]))
    for copy in own_copies:
        copy.start()
    pl.semaphore_wait(barrier, sum(there.astype(jnp.int32) for there, _ in targets))

    def data_copy(direction, zz, yy, piece, own):
        data = data_of(zz, yy, core, piece)
        return pltpu.make_async_remote_copy(
            x_ref.at[pl.ds(piece * part, part)] if own else data, data,
            send_sem.at[direction, (zz * grid_fast + yy) * PIECES + piece],
            recv_sem.at[device(zz, yy, core) * PIECES + piece],
            device_id={"docs": targets[direction][1]}, device_id_type=MESH,
        )

    def lab_copy(direction, zz, yy, own):
        slot = device(zz, yy, core)
        return pltpu.make_async_remote_copy(
            lab_ref if own else labs.at[slot], labs.at[slot],
            lsend_sem.at[direction, zz * grid_fast + yy], lrecv_sem.at[slot],
            device_id={"docs": targets[direction][1]}, device_id_type=MESH,
        )

    def each(directions, wanted, zz, yy, piece, own, act):
        for direction, want in zip(directions, wanted):
            @pl.when(jnp.logical_and(targets[direction][0], want))
            def _():
                @pl.when(piece == 0)
                def _():
                    act(lab_copy(direction, zz, yy, own))
                act(data_copy(direction, zz, yy, piece, own))

    start = lambda copy: copy.start()
    finish = lambda copy: copy.wait_send()

    def arrived(zz, yy, cc, piece):
        slot = device(zz, yy, cc)
        @pl.when(piece == 0)
        def _():
            pltpu.make_async_remote_copy(
                labs.at[slot], labs.at[slot], lsend_sem.at[0, 0], lrecv_sem.at[slot],
                device_id={"docs": targets[4][1]}, device_id_type=MESH,
            ).wait_recv()
        data = data_of(zz, yy, cc, piece)
        pltpu.make_async_remote_copy(
            data, data, send_sem.at[0, 0], recv_sem.at[slot * PIECES + piece],
            device_id={"docs": targets[4][1]}, device_id_type=MESH,
        ).wait_recv()

    yes = z >= 0
    for piece in range(PIECES):
        each((2, 3, 0, 1, 4), (yes,) * 5, z, y, piece, True, start)

    row_max[...] = jnp.full_like(row_max, neg_large)
    row_total[...] = jnp.zeros_like(row_total)
    acc[...] = jnp.zeros_like(acc)
    own_copies[-1].wait()
    label_column = jnp.transpose(
        jnp.broadcast_to(labs[me].astype(jnp.float32), (rows, rows))
    )[:, :1]
    column = lax.broadcasted_iota(jnp.int32, (rows, keys), 1)
    gap = (
        column + (column // half_rows) * (rows - half_rows)
        - lax.broadcasted_iota(jnp.int32, (rows, keys), 0)
    )
    for copy in own_copies[:-1]:
        copy.wait()

    def compute(zz, yy, half):
        where = zz * grid_fast + yy
        values = buf[pl.ds(pl.multiple_of((where * HALVES + half) * keys, keys), keys), :]
        tags = []
        for cc in range(CORES):
            tag = labs[where * CORES + cc].astype(jnp.float32)
            pieces = [tag[:, h * half_rows:(h + 1) * half_rows] for h in range(HALVES)]
            picked = pieces[0]
            for h in range(1, HALVES):
                picked = jnp.where(half == h, pieces[h], picked)
            tags.append(picked)
        tags = jnp.concatenate(tags, axis=1)
        scores = lax.dot_general(
            mine[...], values, (((1,), (1,)), ((), ())), preferred_element_type=jnp.float32
        ) * (kernel_gain / math.sqrt(width))
        self_gap = jnp.where(where == chip, core * rows - half * half_rows, CORES * rows)
        absorb(scores, (label_column == tags) & (gap != self_gap), values)

    def compute_core(zz, yy, cc):
        slot = device(zz, yy, cc)
        values = buf[pl.ds(pl.multiple_of(slot * rows, rows), rows), :]
        scores = lax.dot_general(
            mine[...], values, (((1,), (1,)), ((), ())), preferred_element_type=jnp.float32
        ) * (kernel_gain / math.sqrt(width))
        absorb(scores, label_column == labs[slot].astype(jnp.float32), values)

    def absorb(scores, near, values):
        masked = jnp.where(near, scores, neg_large)
        before = row_max[...]
        peak = jnp.maximum(before, jnp.max(masked, axis=1, keepdims=True))
        weights = jnp.where(near, jnp.exp(masked - peak), 0.0)
        scale = jnp.exp(before - peak)
        row_max[...] = peak
        row_total[...] = row_total[...] * scale + jnp.sum(weights, axis=1, keepdims=True)
        acc[...] = acc[...] * scale + jnp.dot(
            weights.astype(jnp.bfloat16), values, preferred_element_type=jnp.float32
        )

    def meet(zz, yy, half):
        def one(p, carry):
            arrived(zz, yy, 1 - core, half * group + p)
            return carry
        lax.fori_loop(0, group, one, 0)
        compute(zz, yy, half)

    def visited(distance, side, reach, origin):
        place = origin + jnp.where(side == 0, -distance, distance)
        inside = (distance >= 0) & (distance < reach) & (place >= 0) & (place < reach)
        return place, inside & jnp.logical_or(distance > 0, side == 0)

    def other_columns(body):
        if grid_fast == 2:
            body(1 - y)
            return
        def one(i, carry):
            yy, valid = visited(i // 2 + 1, lax.rem(i, 2), grid_fast, y)
            @pl.when(valid)
            def _():
                body(yy)
            return carry
        lax.fori_loop(0, 2 * (grid_fast - 1), one, 0)

    def along(zz, piece, side, act):
        each((2, 3, 0, 1, 4), (yes, yes, side == 1, side == 0, yes), zz, y, piece, False, act)

    def across(zz, yy, piece, act):
        each((2, 3, 4), (yy > y, yy < y, yes), zz, yy, piece, False, act)

    def receive(zz, yy, piece):
        arrived(zz, yy, core, piece)
        across(zz, yy, piece, start)

    farthest = jnp.where(2 * z >= grid_slow, 0, grid_slow - 1)

    def event(e, carry):
        distance = e // (2 * PIECES)
        piece = lax.rem(e // 2, PIECES)
        side = lax.rem(e, 2)
        half = piece // group

        @pl.when(e == 2 * PIECES * grid_slow)
        def _():
            for p in range(PIECES):
                each((2, 3, 0, 1, 4), (yes,) * 5, z, y, p, True, finish)

        zz, valid = visited(distance, side, grid_slow, z)
        @pl.when(valid & (distance > 0))
        def _():
            arrived(zz, y, core, piece)
            along(zz, piece, side, start)

        z1, valid1 = visited(distance - 1, side, grid_slow, z)
        z2, valid2 = visited(distance - 2, side, grid_slow, z)
        @pl.when(valid2)
        def _():
            other_columns(lambda yy: receive(z2, yy, piece))
            @pl.when(distance > 2)
            def _():
                along(z2, piece, side, finish)

        z3, valid3 = visited(distance - 3, side, grid_slow, z)
        @pl.when(valid3)
        def _():
            other_columns(lambda yy: across(z3, yy, piece, finish))

        near = valid1 & (lax.rem(piece, group) == 0)
        if grid_fast == 2:
            far = valid2 & (lax.rem(piece, group) == group - 1) & (z2 != farthest)
            @pl.when(near | far)
            def _():
                def one(i, carry):
                    @pl.when(jnp.where(i == 0, near, far))
                    def _():
                        meet(jnp.where(i == 0, z1, z2), jnp.where(i == 0, y, 1 - y), half)
                    return carry
                lax.fori_loop(0, 2, one, 0)
        else:
            @pl.when(near)
            def _():
                meet(z1, y, half)
            @pl.when(valid2 & (lax.rem(piece, group) == group - 1))
            def _():
                other_columns(lambda yy: meet(z2, yy, half))
        return carry

    lax.fori_loop(0, 2 * PIECES * (grid_slow + 2), event, 0)
    if grid_fast == 2:
        def last_pair(i, carry):
            cc = jnp.where(i == 0, core, 1 - core)
            @pl.when(i == 1)
            def _():
                for p in range(PIECES):
                    arrived(farthest, 1 - y, 1 - core, p)
            compute_core(farthest, 1 - y, cc)
            return carry
        lax.fori_loop(0, CORES, last_pair, 0)

    total = row_total[...]
    density = row_max[...] + jnp.log(total)
    dens_ref[...] = jnp.transpose(jnp.broadcast_to(density, (rows, rows)))[:1, :]
    mean_ref[...] = (acc[...] / total).astype(mean_ref.dtype)

    for e in range(2 * PIECES):
        last, valid = visited(grid_slow - 1, e % 2, grid_slow, z)
        @pl.when(valid)
        def _():
            other_columns(lambda yy: across(last, yy, e // 2, finish))


def folded_kernel(
    planes, x_ref, lab_ref, dens_ref, mean_ref,
    buf, labs, meter, acc, row_max, row_total,
    send_sem, lsend_sem, recv_sem, pair_sem, own_sem, ready_sem,
):
    rows, width = x_ref.shape
    row_units = width * x_ref.dtype.itemsize // (rows * lab_ref.dtype.itemsize)
    half_rows = rows // 2
    tip = rows // 8
    FIRST, SECOND, WHOLE = (0, half_rows), (half_rows, half_rows), (0, rows)
    FIRST_A, FIRST_B = (0, half_rows // 2), (half_rows // 2, half_rows // 2 - tip)
    FIRST_TIP, SECOND_TIP = (half_rows - tip, tip), (half_rows, tip)
    SECOND_B, SECOND_A = (half_rows + tip, half_rows // 2 - tip), (rows - half_rows // 2, half_rows // 2)
    SECOND_C = (half_rows, half_rows // 2)
    me = lax.axis_index("docs")
    core = lax.rem(me, CORES)
    y = lax.rem(me // CORES, 2)
    z = me // (CORES * 2)
    mirrored = 2 * z >= planes
    end = (z == 0) | (z == planes - 1)
    mid = jnp.logical_not(end)

    def device(k, column, cc):
        zz = jnp.where(mirrored, planes - 1 - k, k)
        return (zz * 2 + column) * CORES + cc

    OUT, IN, SIDE, PAIR, OUT_TWIN, SIDE_TWIN = range(6)
    AXIS = (0, 0, 1, 2)
    home = jnp.where(end, 0, 1)
    targets = (
        device(0, y, core),
        device(home + 1, y, core),
        device(home, 1 - y, core),
        device(home, y, 1 - core),
        device(0, y, 1 - core),
        device(home, 1 - y, 1 - core),
    )
    END_ORDER = ((0, 0), (1, 0), (0, 1), (2, 0), (1, 1), (3, 0), (2, 1), (3, 1))
    MID_ORDER = ((1, 0), (2, 0), (0, 0), (3, 0), (0, 1), (1, 1), (2, 1), (3, 1))

    up = (mid & mirrored, jnp.logical_not(mirrored), y == 0, core == 0)
    down = (mid & jnp.logical_not(mirrored), mirrored, y == 1, core == 1)
    barrier = pltpu.get_barrier_semaphore()
    for target, higher in zip(targets, up):
        @pl.when(higher)
        def _():
            pl.semaphore_signal(barrier, inc=1, device_id={"docs": target}, device_id_type=MESH)

    def rows_of(slot, cc, part):
        first, size = part
        first = (slot * CORES + cc) * rows + first
        return buf.at[pl.ds(pl.multiple_of(first, tip), size)]

    lower_count = sum(lower.astype(jnp.int32) for lower in down)
    @pl.when(lower_count > 0)
    def _():
        pl.semaphore_wait(barrier, lower_count)

    def data_copy(direction, slot, there, done, part, own=False):
        return pltpu.make_async_remote_copy(
            x_ref.at[pl.ds(*part)] if own else rows_of(slot, core, part), rows_of(there, core, part),
            send_sem.at[1 if direction == PAIR else 0], done,
            device_id={"docs": targets[direction]}, device_id_type=MESH,
        )

    def lab_copy(direction, slot, there, done, own=False):
        return pltpu.make_async_remote_copy(
            lab_ref if own else labs.at[slot * CORES + core], labs.at[there * CORES + core],
            lsend_sem.at[0], done,
            device_id={"docs": targets[direction]}, device_id_type=MESH,
        )

    def take(done, data_rows, labels=0):
        amount = meter.at[pl.ds(0, data_rows * row_units + labels)]
        pltpu.make_async_remote_copy(
            amount, amount, lsend_sem.at[0], done,
            device_id={"docs": targets[PAIR]}, device_id_type=MESH,
        ).wait_recv()

    class Role:
        def __init__(self, is_end):
            self.is_end = is_end
            self.order = END_ORDER if is_end else MID_ORDER

        def slot(self, k, other):
            return self.order.index((k, other))

        def done(self, k, other, part):
            if (k, other) == (3, 1):
                if self.is_end:
                    return recv_sem.at[11 if part in (FIRST_A, SECOND_A) else 12 if part in (FIRST_B, SECOND_B) else 13]
                return recv_sem.at[11 if part == SECOND_A else 12 if part == SECOND_C else 13]
            if self.is_end:
                first = {(1, 0): 0, (0, 1): 2, (2, 0): 5, (1, 1): 7, (3, 0): 8, (2, 1): 10}[k, other]
            else:
                first = {(2, 0): 0, (0, 0): 2, (3, 0): 4, (0, 1): 6, (1, 1): 9, (2, 1): 10}[k, other]
            if (k, other) in ((1, 1), (2, 1)):
                return recv_sem.at[first]
            if (k, other) == (0, 1):
                return recv_sem.at[first + (0 if part == FIRST else 1 if part == SECOND_A else 2)]
            return recv_sem.at[first + (1 if part == SECOND else 0)]

        def receiver(self, direction, k, other):
            if direction in (SIDE, SIDE_TWIN):
                return self, k, 1 - other
            if direction == PAIR:
                return self, k, other
            if direction in (OUT, OUT_TWIN):
                return at_end, k, other
            return at_mid, k if self.is_end else planes - 1 - k, other

        def send(self, k, other, part, directions, own=False):
            for direction in directions:
                role, kk, oo = self.receiver(direction, k, other)
                slot, there = self.slot(k, other), role.slot(kk, oo)
                done = pair_sem.at[(there + 1) // 2] if direction == PAIR else role.done(kk, oo, part)
                if part in (FIRST, FIRST_A, WHOLE):
                    lab_copy(direction, slot, there, done, own).start()
                data_copy(direction, slot, there, done, part, own).start()

        def arrived(self, k, other, part):
            take(self.done(k, other, part), part[1], 1 if part[0] == 0 else 0)

        def pass_on(self, k, other, part, directions):
            self.arrived(k, other, part)
            self.send(k, other, part, directions)

        def pair(self, k, other):
            self.send(k, other, WHOLE, (PAIR,))

        def gather(self, k, other):
            self.arrived(k, other, WHOLE)
            self.pair(k, other)

    at_end, at_mid = Role(True), Role(False)

    def start_own(direction):
        def by(role):
            k = 0 if role.is_end else 1
            for part in {SIDE: (SECOND_A, SECOND_C, FIRST), PAIR: (WHOLE,)}.get(direction, (FIRST, SECOND)):
                role.send(k, 0, part, (direction,), own=True)

        if direction == OUT:
            by(at_mid)
        elif direction == PAIR:
            by(at_end)
        else:
            pl.when(end)(lambda: by(at_end))
            pl.when(mid)(lambda: by(at_mid))

    for direction, lower in enumerate(down):
        @pl.when(lower)
        def _():
            start_own(direction)
    for direction, lower in enumerate(down):
        @pl.when(lower)
        def _():
            pl.semaphore_signal(
                ready_sem.at[AXIS[direction]], inc=1,
                device_id={"docs": targets[direction]}, device_id_type=MESH,
            )
    own_data = pltpu.make_async_copy(x_ref, rows_of(0, core, WHOLE), own_sem.at[0])
    own_data.start()
    own_lab = pltpu.make_async_copy(lab_ref, labs.at[core], own_sem.at[0])
    own_lab.start()
    for direction, higher in reversed(tuple(enumerate(up))):
        @pl.when(higher)
        def _():
            pl.semaphore_wait(ready_sem.at[AXIS[direction]], 1)
            start_own(direction)

    own_amount = meter.at[pl.ds(0, rows * row_units + 1)]
    pltpu.make_async_copy(own_amount, own_amount, own_sem.at[0]).wait()
    label_column = jnp.transpose(
        jnp.broadcast_to(labs[core].astype(jnp.float32), (rows, rows))
    )[:, :1]

    def from_pair(group, slots):
        take(pair_sem.at[group], slots * rows, slots)

    def masked_scores(slot, count):
        keys = count * CORES * rows
        values = buf[pl.ds(pl.multiple_of(slot * CORES * rows, rows), keys), :]
        mine = buf[pl.ds(pl.multiple_of(core * rows, rows), rows), :]
        tags = jnp.concatenate(
            [labs[slot * CORES + n].astype(jnp.float32) for n in range(count * CORES)], axis=1
        )
        scores = lax.dot_general(
            mine, values, (((1,), (1,)), ((), ())), preferred_element_type=jnp.float32
        ) * (kernel_gain / math.sqrt(width))
        return scores, label_column == tags, values

    def first_block():
        scores, near, values = masked_scores(0, 1)
        gap = lax.broadcasted_iota(jnp.int32, near.shape, 1) - lax.broadcasted_iota(jnp.int32, near.shape, 0)
        masked = jnp.where(near & (gap != core * rows), scores, neg_large)
        peak = jnp.maximum(jnp.max(masked, axis=1, keepdims=True), neg_start)
        weights = jnp.exp(masked - peak)
        row_max[...] = peak
        row_total[...] = jnp.sum(weights, axis=1, keepdims=True)
        acc[...] = jnp.dot(weights.astype(jnp.bfloat16), values, preferred_element_type=jnp.float32)

    def absorb(slot, count):
        scores, near, values = masked_scores(slot, count)
        masked = jnp.where(near, scores, neg_large)
        before = row_max[...]
        peak = jnp.maximum(before, jnp.max(masked, axis=1, keepdims=True))
        weights = jnp.exp(masked - peak)
        scale = jnp.exp(before - peak)
        total = row_total[...] * scale + jnp.sum(weights, axis=1, keepdims=True)
        gained = jnp.dot(weights.astype(jnp.bfloat16), values, preferred_element_type=jnp.float32)
        return peak, total, scale, gained

    from_pair(0, 1)
    first_block()

    def step(j, carry):
        @pl.when(end & (j == 1))
        def _():
            r = at_end
            r.pass_on(1, 0, FIRST, (SIDE,))
            r.pass_on(0, 1, SECOND_A, (IN,))
            r.pass_on(0, 1, SECOND_C, (IN,))
            r.pass_on(1, 0, SECOND, (SIDE,))
            r.pair(1, 0)
            r.pass_on(0, 1, FIRST, (IN,))
            r.pair(0, 1)
            r.pass_on(2, 0, FIRST, (SIDE,))

        @pl.when(end & (j == 2))
        def _():
            r = at_end
            r.pass_on(2, 0, SECOND, (SIDE,))
            r.pair(2, 0)
            r.gather(1, 1)
            r.arrived(3, 0, FIRST)
            r.send(3, 0, FIRST_A, (SIDE,))
            r.send(3, 0, FIRST_B, (SIDE,))
            r.send(3, 0, FIRST_TIP, (SIDE, SIDE_TWIN))

        @pl.when(end & (j == 3))
        def _():
            r = at_end
            r.arrived(3, 0, SECOND)
            r.pair(3, 0)
            r.gather(2, 1)
            take(recv_sem.at[11], half_rows, 1)
            r.send(3, 1, FIRST_A, (PAIR,))
            r.send(3, 1, SECOND_A, (PAIR,))
            take(recv_sem.at[12], half_rows - 2 * tip)
            r.send(3, 1, FIRST_B, (PAIR,))
            r.send(3, 1, SECOND_B, (PAIR,))

        @pl.when(mid & (j == 1))
        def _():
            r = at_mid
            r.pass_on(2, 0, FIRST, (OUT, SIDE))
            r.pass_on(0, 0, FIRST, (IN,))
            r.pass_on(2, 0, SECOND, (OUT, SIDE))
            r.pair(2, 0)
            r.pass_on(0, 0, SECOND, (IN,))
            r.pair(0, 0)
            r.gather(1, 1)
            r.pass_on(3, 0, FIRST, (OUT, SIDE))
            r.pass_on(0, 1, SECOND_A, (IN,))
            r.pass_on(0, 1, SECOND_C, (IN,))

        @pl.when(mid & (j == 2))
        def _():
            r = at_mid
            r.pass_on(3, 0, SECOND, (OUT,))
            r.pair(3, 0)
            r.arrived(0, 1, FIRST)
            r.pair(0, 1)
            r.gather(2, 1)

        @pl.when(mid & (j == 3))
        def _():
            r = at_mid
            r.arrived(3, 1, SECOND_A)
            r.send(3, 1, SECOND_A, (OUT,))
            r.arrived(3, 1, SECOND_C)
            r.send(3, 1, SECOND_B, (OUT,))
            r.send(3, 1, SECOND_TIP, (OUT, OUT_TWIN))
            r.send(3, 1, SECOND, (PAIR,))
            r.arrived(3, 1, FIRST)
            r.send(3, 1, FIRST, (PAIR,))

        slot = 2 * j - 1
        from_pair(j, 2)
        peak, total, scale, gained = absorb(slot, 2)
        row_max[...] = peak
        row_total[...] = total
        acc[...] = acc[...] * scale + gained
        return carry

    lax.fori_loop(1, planes, step, 0)

    @pl.when(end)
    def _():
        take(recv_sem.at[13], 4 * tip)
        take(pair_sem.at[planes], rows - 2 * tip, 1)

    @pl.when(mid)
    def _():
        from_pair(planes, 1)

    parts = []
    for cc in range(CORES):
        values = buf[pl.ds(((2 * planes - 1) * CORES + cc) * rows, rows), :]
        scores = lax.dot_general(
            buf[pl.ds(pl.multiple_of(core * rows, rows), rows), :], values,
            (((1,), (1,)), ((), ())), preferred_element_type=jnp.float32,
        ) * (kernel_gain / math.sqrt(width))
        tags = labs[(2 * planes - 1) * CORES + cc].astype(jnp.float32)
        parts.append((jnp.where(label_column == tags, scores, neg_large), values))
    before = row_max[...]
    peak = jnp.maximum(before, jnp.max(jnp.maximum(parts[0][0], parts[1][0]), axis=1, keepdims=True))
    scale = jnp.exp(before - peak)
    weights = [jnp.exp(masked - peak) for masked, _ in parts]
    total = row_total[...] * scale + jnp.sum(weights[0] + weights[1], axis=1, keepdims=True)
    inverse = 1.0 / total
    gained = sum(
        jnp.dot(w.astype(jnp.bfloat16), values, preferred_element_type=jnp.float32)
        for w, (_, values) in zip(weights, parts)
    )
    mean_ref[...] = ((acc[...] * scale + gained) * inverse).astype(mean_ref.dtype)
    density = peak + jnp.log(total)
    dens_ref[...] = jnp.transpose(jnp.broadcast_to(density, (rows, rows)))[:1, :]

    def sent(done, amount):
        pltpu.make_async_remote_copy(
            amount, amount, done, pair_sem.at[0],
            device_id={"docs": targets[PAIR]}, device_id_type=MESH,
        ).wait_send()

    @pl.when(end)
    def _():
        sent(send_sem.at[0], buf.at[pl.ds(0, 11 * half_rows + tip)])
        sent(send_sem.at[1], buf.at[pl.ds(0, 16 * half_rows - 2 * tip)])
        sent(lsend_sem.at[0], labs.at[pl.ds(0, 14)])

    @pl.when(mid)
    def _():
        sent(send_sem.at[0], buf.at[pl.ds(0, 17 * half_rows + tip)])
        sent(send_sem.at[1], buf.at[pl.ds(0, 16 * half_rows)])
        sent(lsend_sem.at[0], labs.at[pl.ds(0, 16)])


def publish_kernel(dens_ref, mean_ref, dens_out, mean_out, sem):
    copies = (
        pltpu.make_async_copy(mean_ref, mean_out, sem.at[0]),
        pltpu.make_async_copy(dens_ref, dens_out, sem.at[1]),
    )
    for copy in copies:
        copy.start()
    for copy in copies:
        copy.wait()


def publish(density, mean):
    held = [pltpu.with_memory_space_constraint(a, pltpu.VMEM) for a in (density, mean)]
    return pl.pallas_call(
        publish_kernel,
        out_shape=tuple(jax.ShapeDtypeStruct(a.shape, a.dtype) for a in (density, mean)),
        in_specs=[pl.BlockSpec(memory_space=pltpu.VMEM)] * 2,
        out_specs=(pl.BlockSpec(memory_space=pltpu.HBM),) * 2,
        scratch_shapes=[pltpu.SemaphoreType.DMA((2,))],
    )(*held)


def general_call(device_count, rows, width):
    grid_slow, grid_fast = chip_grid(device_count)
    chips = device_count // CORES
    vmem = pl.BlockSpec(memory_space=pltpu.VMEM)
    return pl.pallas_call(
        functools.partial(kernel, grid_slow, grid_fast),
        out_shape=(
            pltpu.VMEM((1, rows), jnp.float32),
            pltpu.VMEM((rows, width), jnp.bfloat16),
        ),
        in_specs=[pl.BlockSpec(memory_space=pl.ANY), pl.BlockSpec(memory_space=pl.ANY)],
        out_specs=(vmem, vmem),
        scratch_shapes=[
            pltpu.VMEM((device_count * rows, width), jnp.bfloat16),
            pltpu.VMEM((device_count, 1, rows), jnp.int32),
            pltpu.VMEM((rows, width), jnp.bfloat16),
            pltpu.VMEM((rows, width), jnp.float32),
            pltpu.VMEM((rows, 1), jnp.float32),
            pltpu.VMEM((rows, 1), jnp.float32),
            pltpu.SemaphoreType.DMA((5, chips * PIECES)),
            pltpu.SemaphoreType.DMA((device_count * PIECES,)),
            pltpu.SemaphoreType.DMA((5, chips)),
            pltpu.SemaphoreType.DMA((device_count,)),
            pltpu.SemaphoreType.DMA((PIECES + 1,)),
            pltpu.SemaphoreType.DMA((1,)),
        ],
        compiler_params=pltpu.CompilerParams(collective_id=0, has_side_effects=True),
    )


def folded_call(device_count, rows, width):
    chips = device_count // CORES
    vmem = pl.BlockSpec(memory_space=pltpu.VMEM)
    return pl.pallas_call(
        functools.partial(folded_kernel, chips // 2),
        out_shape=(
            pltpu.VMEM((1, rows), jnp.float32),
            pltpu.VMEM((rows, width), jnp.bfloat16),
        ),
        in_specs=[pl.BlockSpec(memory_space=pl.ANY), pl.BlockSpec(memory_space=pl.ANY)],
        out_specs=(vmem, vmem),
        scratch_shapes=[
            pltpu.VMEM((device_count * rows, width), jnp.bfloat16),
            pltpu.VMEM((device_count, 1, rows), jnp.int32),
            pltpu.VMEM((width + CORES, 1, rows), jnp.int32),
            pltpu.VMEM((rows, width), jnp.float32),
            pltpu.VMEM((rows, 1), jnp.float32),
            pltpu.VMEM((rows, 1), jnp.float32),
            pltpu.SemaphoreType.DMA((2,)),
            pltpu.SemaphoreType.DMA((1,)),
            pltpu.SemaphoreType.DMA((14,)),
            pltpu.SemaphoreType.DMA((chips // 2 + 1,)),
            pltpu.SemaphoreType.DMA((1,)),
            pltpu.SemaphoreType.REGULAR((3,)),
        ],
        compiler_params=pltpu.CompilerParams(collective_id=0, has_side_effects=True),
    )


def per_device(device_count, embeddings, labels, row_slot):
    rows, width = embeddings.shape
    call = folded_call if chip_grid(device_count) == FOLDED_GRID else general_call
    density, mean = call(device_count, rows, width)(embeddings, labels.reshape(1, rows))
    density, mean = publish(density, mean)
    return density.reshape(rows), mean


def solution(mesh):
    return jax.shard_map(
        functools.partial(per_device, mesh.shape["docs"]),
        mesh=mesh,
        in_specs=(P(("groups", "docs"), None), P(("groups", "docs")), P(("groups", "docs"))),
        out_specs=(P(("groups", "docs")), P(("groups", "docs"), None)),
        check_vma=False,
    )
```

```python
import functools
import math

import jax
import jax.numpy as jnp
from jax import lax
from jax.experimental import pallas as pl
from jax.experimental.pallas import tpu as pltpu
from jax.sharding import PartitionSpec as P

MESH = pl.DeviceIdType.MESH
CORES = 2
PIECES = 2
HALVES = 1
FOLDED_GRID = (4, 2)

neg_large = -1e30
neg_start = -1e29
kernel_gain = 4.0


def chip_grid(device_count):
    chips = device_count // CORES
    fast = 1
    while (2 * fast) * (2 * fast) <= chips and chips % (2 * fast) == 0:
        fast *= 2
    return chips // fast, fast


def kernel(
    grid_slow, grid_fast, x_ref, lab_ref, dens_ref, mean_ref,
    buf, labs, mine, acc, row_max, row_total,
    send_sem, recv_sem, lsend_sem, lrecv_sem, own_sem, own_lab_sem,
):
    rows, width = x_ref.shape
    part = rows // PIECES
    group = PIECES // HALVES
    half_rows = rows // HALVES
    keys = CORES * half_rows
    me = lax.axis_index("docs")
    core = lax.rem(me, CORES)
    chip = me // CORES
    y = lax.rem(chip, grid_fast)
    z = chip // grid_fast

    def device(zz, yy, cc):
        return (zz * grid_fast + yy) * CORES + cc

    targets = (
        (z > 0, device(z - 1, y, core)),
        (z < grid_slow - 1, device(z + 1, y, core)),
        (y > 0, device(z, y - 1, core)),
        (y < grid_fast - 1, device(z, y + 1, core)),
        (z >= 0, device(z, y, 1 - core)),
    )

    barrier = pltpu.get_barrier_semaphore()
    for there, target in targets:
        @pl.when(there)
        def _():
            pl.semaphore_signal(barrier, inc=1, device_id={"docs": target}, device_id_type=MESH)

    def data_of(zz, yy, cc, piece):
        where = ((zz * grid_fast + yy) * HALVES + piece // group) * CORES + cc
        return buf.at[pl.ds(pl.multiple_of((where * group + lax.rem(piece, group)) * part, part), part)]

    own_copies = [pltpu.make_async_copy(x_ref, mine, own_sem.at[PIECES])]
    for piece in range(PIECES):
        own_copies.append(
            pltpu.make_async_copy(
                x_ref.at[pl.ds(piece * part, part)], data_of(z, y, core, piece), own_sem.at[piece]
            )
        )
    own_copies.append(pltpu.make_async_copy(lab_ref, labs.at[me], own_lab_sem.at[0]))
    for copy in own_copies:
        copy.start()
    pl.semaphore_wait(barrier, sum(there.astype(jnp.int32) for there, _ in targets))

    def data_copy(direction, zz, yy, piece, own):
        data = data_of(zz, yy, core, piece)
        return pltpu.make_async_remote_copy(
            x_ref.at[pl.ds(piece * part, part)] if own else data, data,
            send_sem.at[direction, (zz * grid_fast + yy) * PIECES + piece],
            recv_sem.at[device(zz, yy, core) * PIECES + piece],
            device_id={"docs": targets[direction][1]}, device_id_type=MESH,
        )

    def lab_copy(direction, zz, yy, own):
        slot = device(zz, yy, core)
        return pltpu.make_async_remote_copy(
            lab_ref if own else labs.at[slot], labs.at[slot],
            lsend_sem.at[direction, zz * grid_fast + yy], lrecv_sem.at[slot],
            device_id={"docs": targets[direction][1]}, device_id_type=MESH,
        )

    def each(directions, wanted, zz, yy, piece, own, act):
        for direction, want in zip(directions, wanted):
            @pl.when(jnp.logical_and(targets[direction][0], want))
            def _():
                @pl.when(piece == 0)
                def _():
                    act(lab_copy(direction, zz, yy, own))
                act(data_copy(direction, zz, yy, piece, own))

    start = lambda copy: copy.start()
    finish = lambda copy: copy.wait_send()

    def arrived(zz, yy, cc, piece):
        slot = device(zz, yy, cc)
        @pl.when(piece == 0)
        def _():
            pltpu.make_async_remote_copy(
                labs.at[slot], labs.at[slot], lsend_sem.at[0, 0], lrecv_sem.at[slot],
                device_id={"docs": targets[4][1]}, device_id_type=MESH,
            ).wait_recv()
        data = data_of(zz, yy, cc, piece)
        pltpu.make_async_remote_copy(
            data, data, send_sem.at[0, 0], recv_sem.at[slot * PIECES + piece],
            device_id={"docs": targets[4][1]}, device_id_type=MESH,
        ).wait_recv()

    yes = z >= 0
    for piece in range(PIECES):
        each((2, 3, 0, 1, 4), (yes,) * 5, z, y, piece, True, start)

    row_max[...] = jnp.full_like(row_max, neg_large)
    row_total[...] = jnp.zeros_like(row_total)
    acc[...] = jnp.zeros_like(acc)
    own_copies[-1].wait()
    label_column = jnp.transpose(
        jnp.broadcast_to(labs[me].astype(jnp.float32), (rows, rows))
    )[:, :1]
    column = lax.broadcasted_iota(jnp.int32, (rows, keys), 1)
    gap = (
        column + (column // half_rows) * (rows - half_rows)
        - lax.broadcasted_iota(jnp.int32, (rows, keys), 0)
    )
    for copy in own_copies[:-1]:
        copy.wait()

    def compute(zz, yy, half):
        where = zz * grid_fast + yy
        values = buf[pl.ds(pl.multiple_of((where * HALVES + half) * keys, keys), keys), :]
        tags = []
        for cc in range(CORES):
            tag = labs[where * CORES + cc].astype(jnp.float32)
            pieces = [tag[:, h * half_rows:(h + 1) * half_rows] for h in range(HALVES)]
            picked = pieces[0]
            for h in range(1, HALVES):
                picked = jnp.where(half == h, pieces[h], picked)
            tags.append(picked)
        tags = jnp.concatenate(tags, axis=1)
        scores = lax.dot_general(
            mine[...], values, (((1,), (1,)), ((), ())), preferred_element_type=jnp.float32
        ) * (kernel_gain / math.sqrt(width))
        self_gap = jnp.where(where == chip, core * rows - half * half_rows, CORES * rows)
        absorb(scores, (label_column == tags) & (gap != self_gap), values)

    def compute_core(zz, yy, cc):
        slot = device(zz, yy, cc)
        values = buf[pl.ds(pl.multiple_of(slot * rows, rows), rows), :]
        scores = lax.dot_general(
            mine[...], values, (((1,), (1,)), ((), ())), preferred_element_type=jnp.float32
        ) * (kernel_gain / math.sqrt(width))
        absorb(scores, label_column == labs[slot].astype(jnp.float32), values)

    def absorb(scores, near, values):
        masked = jnp.where(near, scores, neg_large)
        before = row_max[...]
        peak = jnp.maximum(before, jnp.max(masked, axis=1, keepdims=True))
        weights = jnp.where(near, jnp.exp(masked - peak), 0.0)
        scale = jnp.exp(before - peak)
        row_max[...] = peak
        row_total[...] = row_total[...] * scale + jnp.sum(weights, axis=1, keepdims=True)
        acc[...] = acc[...] * scale + jnp.dot(
            weights.astype(jnp.bfloat16), values, preferred_element_type=jnp.float32
        )

    def meet(zz, yy, half):
        def one(p, carry):
            arrived(zz, yy, 1 - core, half * group + p)
            return carry
        lax.fori_loop(0, group, one, 0)
        compute(zz, yy, half)

    def visited(distance, side, reach, origin):
        place = origin + jnp.where(side == 0, -distance, distance)
        inside = (distance >= 0) & (distance < reach) & (place >= 0) & (place < reach)
        return place, inside & jnp.logical_or(distance > 0, side == 0)

    def other_columns(body):
        if grid_fast == 2:
            body(1 - y)
            return
        def one(i, carry):
            yy, valid = visited(i // 2 + 1, lax.rem(i, 2), grid_fast, y)
            @pl.when(valid)
            def _():
                body(yy)
            return carry
        lax.fori_loop(0, 2 * (grid_fast - 1), one, 0)

    def along(zz, piece, side, act):
        each((2, 3, 0, 1, 4), (yes, yes, side == 1, side == 0, yes), zz, y, piece, False, act)

    def across(zz, yy, piece, act):
        each((2, 3, 4), (yy > y, yy < y, yes), zz, yy, piece, False, act)

    def receive(zz, yy, piece):
        arrived(zz, yy, core, piece)
        across(zz, yy, piece, start)

    farthest = jnp.where(2 * z >= grid_slow, 0, grid_slow - 1)

    def event(e, carry):
        distance = e // (2 * PIECES)
        piece = lax.rem(e // 2, PIECES)
        side = lax.rem(e, 2)
        half = piece // group

        @pl.when(e == 2 * PIECES * grid_slow)
        def _():
            for p in range(PIECES):
                each((2, 3, 0, 1, 4), (yes,) * 5, z, y, p, True, finish)

        zz, valid = visited(distance, side, grid_slow, z)
        @pl.when(valid & (distance > 0))
        def _():
            arrived(zz, y, core, piece)
            along(zz, piece, side, start)

        z1, valid1 = visited(distance - 1, side, grid_slow, z)
        z2, valid2 = visited(distance - 2, side, grid_slow, z)
        @pl.when(valid2)
        def _():
            other_columns(lambda yy: receive(z2, yy, piece))
            @pl.when(distance > 2)
            def _():
                along(z2, piece, side, finish)

        z3, valid3 = visited(distance - 3, side, grid_slow, z)
        @pl.when(valid3)
        def _():
            other_columns(lambda yy: across(z3, yy, piece, finish))

        near = valid1 & (lax.rem(piece, group) == 0)
        if grid_fast == 2:
            far = valid2 & (lax.rem(piece, group) == group - 1) & (z2 != farthest)
            @pl.when(near | far)
            def _():
                def one(i, carry):
                    @pl.when(jnp.where(i == 0, near, far))
                    def _():
                        meet(jnp.where(i == 0, z1, z2), jnp.where(i == 0, y, 1 - y), half)
                    return carry
                lax.fori_loop(0, 2, one, 0)
        else:
            @pl.when(near)
            def _():
                meet(z1, y, half)
            @pl.when(valid2 & (lax.rem(piece, group) == group - 1))
            def _():
                other_columns(lambda yy: meet(z2, yy, half))
        return carry

    lax.fori_loop(0, 2 * PIECES * (grid_slow + 2), event, 0)
    if grid_fast == 2:
        def last_pair(i, carry):
            cc = jnp.where(i == 0, core, 1 - core)
            @pl.when(i == 1)
            def _():
                for p in range(PIECES):
                    arrived(farthest, 1 - y, 1 - core, p)
            compute_core(farthest, 1 - y, cc)
            return carry
        lax.fori_loop(0, CORES, last_pair, 0)

    total = row_total[...]
    density = row_max[...] + jnp.log(total)
    dens_ref[...] = jnp.transpose(jnp.broadcast_to(density, (rows, rows)))[:1, :]
    mean_ref[...] = (acc[...] / total).astype(mean_ref.dtype)

    for e in range(2 * PIECES):
        last, valid = visited(grid_slow - 1, e % 2, grid_slow, z)
        @pl.when(valid)
        def _():
            other_columns(lambda yy: across(last, yy, e // 2, finish))


def folded_kernel(
    planes, x_ref, lab_ref, dens_ref, mean_ref,
    buf, labs, meter, acc, row_max, row_total,
    send_sem, recv_sem, pair_sem, own_sem, ready_sem,
):
    rows, width = x_ref.shape
    row_units = width * x_ref.dtype.itemsize // (rows * lab_ref.dtype.itemsize)
    half_rows = rows // 2
    tip = rows // 8
    FIRST, SECOND, WHOLE = (0, half_rows), (half_rows, half_rows), (0, rows)
    FIRST_A, FIRST_B = (0, half_rows // 2), (half_rows // 2, half_rows // 2 - tip)
    FIRST_TIP, SECOND_TIP = (half_rows - tip, tip), (half_rows, tip)
    SECOND_B, SECOND_A = (half_rows + tip, half_rows // 2 - tip), (rows - half_rows // 2, half_rows // 2)
    SECOND_C = (half_rows, half_rows // 2)
    me = lax.axis_index("docs")
    core = lax.rem(me, CORES)
    y = lax.rem(me // CORES, 2)
    z = me // (CORES * 2)
    mirrored = 2 * z >= planes
    end = (z == 0) | (z == planes - 1)
    mid = jnp.logical_not(end)

    def device(k, column, cc):
        zz = jnp.where(mirrored, planes - 1 - k, k)
        return (zz * 2 + column) * CORES + cc

    OUT, IN, SIDE, PAIR, OUT_TWIN, SIDE_TWIN = range(6)
    AXIS = (0, 0, 0, 1)
    home = jnp.where(end, 0, 1)
    inward = jnp.where(mirrored, -2 * CORES, 2 * CORES)
    across, beside = CORES - 2 * CORES * y, 1 - 2 * core
    targets = (me - inward, me + inward, me + across, me + beside, me - inward + beside, me + across + beside)
    END_ORDER = ((0, 0), (1, 0), (0, 1), (2, 0), (1, 1), (3, 0), (2, 1), (3, 1))
    MID_ORDER = ((1, 0), (2, 0), (0, 0), (3, 0), (0, 1), (1, 1), (2, 1), (3, 1))

    up = (mid & mirrored, jnp.logical_not(mirrored), y == 0, core == 0)
    down = (mid & jnp.logical_not(mirrored), mirrored, y == 1, core == 1)
    barrier = pltpu.get_barrier_semaphore()
    for target, higher in zip(targets, up):
        @pl.when(higher)
        def _():
            pl.semaphore_signal(barrier, inc=1, device_id={"docs": target}, device_id_type=MESH)

    def rows_of(slot, cc, part):
        first, size = part
        first = (slot * CORES + cc) * rows + first
        return buf.at[pl.ds(pl.multiple_of(first, tip), size)]

    lower_count = sum(lower.astype(jnp.int32) for lower in down)
    @pl.when(lower_count > 0)
    def _():
        pl.semaphore_wait(barrier, lower_count)

    def data_copy(direction, slot, there, done, part, own=False):
        return pltpu.make_async_remote_copy(
            x_ref.at[pl.ds(*part)] if own else rows_of(slot, core, part), rows_of(there, core, part),
            send_sem.at[0], done,
            device_id={"docs": targets[direction]}, device_id_type=MESH,
        )

    def lab_copy(direction, slot, there, done, own=False):
        return pltpu.make_async_remote_copy(
            lab_ref if own else labs.at[slot * CORES + core], labs.at[there * CORES + core],
            send_sem.at[0], done,
            device_id={"docs": targets[direction]}, device_id_type=MESH,
        )

    def take(done, data_rows, labels=0):
        amount = meter.at[pl.ds(0, data_rows * row_units + labels)]
        pltpu.make_async_remote_copy(
            amount, amount, send_sem.at[0], done,
            device_id={"docs": targets[PAIR]}, device_id_type=MESH,
        ).wait_recv()

    class Role:
        def __init__(self, is_end):
            self.is_end = is_end
            self.order = END_ORDER if is_end else MID_ORDER

        def slot(self, k, other):
            return self.order.index((k, other))

        def done(self, k, other, part):
            second = 1 if part == SECOND else 0
            if self.is_end:
                if (k, other) == (3, 1):
                    index = 8 if part in (FIRST_A, SECOND_A) else 9 if part in (FIRST_B, SECOND_B) else 10
                elif (k, other) == (0, 1):
                    index = {FIRST: 1, SECOND_A: 2, SECOND_C: 3}[part]
                else:
                    index = {(1, 0): second, (2, 0): 4 + second, (1, 1): 5, (3, 0): 6 + second, (2, 1): 7}[k, other]
            elif (k, other) == (3, 1):
                index = 9 if part == SECOND_A else 10 if part == SECOND_C else 11
            elif (k, other) == (0, 1):
                index = {FIRST: 8, SECOND_A: 6, SECOND_C: 7}[part]
            else:
                index = {(2, 0): second, (0, 0): 2 + second, (1, 1): 3, (3, 0): 4 + second, (2, 1): 8}[k, other]
            return recv_sem.at[index]

        def receiver(self, direction, k, other):
            if direction in (SIDE, SIDE_TWIN):
                return self, k, 1 - other
            if direction == PAIR:
                return self, k, other
            if direction in (OUT, OUT_TWIN):
                return at_end, k, other
            return at_mid, k if self.is_end else planes - 1 - k, other

        def send(self, k, other, part, directions, own=False):
            for direction in directions:
                role, kk, oo = self.receiver(direction, k, other)
                slot, there = self.slot(k, other), role.slot(kk, oo)
                done = pair_sem.at[(there + 1) // 2] if direction == PAIR else role.done(kk, oo, part)
                if part in (FIRST, FIRST_A, WHOLE):
                    lab_copy(direction, slot, there, done, own).start()
                data_copy(direction, slot, there, done, part, own).start()

        def arrived(self, k, other, part):
            take(self.done(k, other, part), part[1], 1 if part[0] == 0 else 0)

        def pass_on(self, k, other, part, directions):
            self.arrived(k, other, part)
            self.send(k, other, part, directions)

        def pair(self, k, other):
            self.send(k, other, WHOLE, (PAIR,))

    at_end, at_mid = Role(True), Role(False)

    def start_own(direction):
        def by(role):
            k = 0 if role.is_end else 1
            for part in {SIDE: (SECOND_A, SECOND_C, FIRST), PAIR: (WHOLE,)}.get(direction, (FIRST, SECOND)):
                role.send(k, 0, part, (direction,), own=True)

        if direction == OUT:
            by(at_mid)
        elif direction == PAIR:
            by(at_end)
        else:
            pl.when(end)(lambda: by(at_end))
            pl.when(mid)(lambda: by(at_mid))

    for direction, lower in enumerate(down):
        @pl.when(lower)
        def _():
            start_own(direction)
    for direction, lower in enumerate(down):
        @pl.when(lower)
        def _():
            pl.semaphore_signal(
                ready_sem.at[AXIS[direction]], inc=1,
                device_id={"docs": targets[direction]}, device_id_type=MESH,
            )
    own_data = pltpu.make_async_copy(x_ref, rows_of(0, core, WHOLE), own_sem.at[0])
    own_data.start()
    own_lab = pltpu.make_async_copy(lab_ref, labs.at[core], own_sem.at[0])
    own_lab.start()
    @pl.when(up[PAIR])
    def _():
        pl.semaphore_wait(ready_sem.at[1], 1)
        start_own(PAIR)

    higher_count = sum(higher.astype(jnp.int32) for higher in up[:PAIR])
    @pl.when(higher_count > 0)
    def _():
        pl.semaphore_wait(ready_sem.at[0], higher_count)
    for direction in (SIDE, IN, OUT):
        @pl.when(up[direction])
        def _():
            start_own(direction)

    own_amount = meter.at[pl.ds(0, rows * row_units + 1)]
    pltpu.make_async_copy(own_amount, own_amount, own_sem.at[0]).wait()
    label_column = jnp.transpose(
        jnp.broadcast_to(labs[core].astype(jnp.float32), (rows, rows))
    )[:, :1]

    def from_pair(group, slots):
        take(pair_sem.at[group], slots * rows, slots)

    def masked_scores(slot, count):
        keys = count * CORES * rows
        values = buf[pl.ds(pl.multiple_of(slot * CORES * rows, rows), keys), :]
        mine = buf[pl.ds(pl.multiple_of(core * rows, rows), rows), :]
        tags = jnp.concatenate(
            [labs[slot * CORES + n].astype(jnp.float32) for n in range(count * CORES)], axis=1
        )
        scores = lax.dot_general(
            mine, values, (((1,), (1,)), ((), ())), preferred_element_type=jnp.float32
        ) * (kernel_gain / math.sqrt(width))
        return scores, label_column == tags, values

    def first_block():
        scores, near, values = masked_scores(0, 1)
        gap = lax.broadcasted_iota(jnp.int32, near.shape, 1) - lax.broadcasted_iota(jnp.int32, near.shape, 0)
        masked = jnp.where(near & (gap != core * rows), scores, neg_large)
        peak = jnp.maximum(jnp.max(masked, axis=1, keepdims=True), neg_start)
        weights = jnp.exp(masked - peak)
        row_max[...] = peak
        row_total[...] = jnp.sum(weights, axis=1, keepdims=True)
        acc[...] = jnp.dot(weights.astype(jnp.bfloat16), values, preferred_element_type=jnp.float32)

    def absorb(slot, count):
        scores, near, values = masked_scores(slot, count)
        masked = jnp.where(near, scores, neg_large)
        before = row_max[...]
        peak = jnp.maximum(before, jnp.max(masked, axis=1, keepdims=True))
        weights = jnp.exp(masked - peak)
        scale = jnp.exp(before - peak)
        total = row_total[...] * scale + jnp.sum(weights, axis=1, keepdims=True)
        gained = jnp.dot(weights.astype(jnp.bfloat16), values, preferred_element_type=jnp.float32)
        return peak, total, scale, gained

    from_pair(0, 1)
    first_block()

    def step(j, carry):
        @pl.when(end & (j == 1))
        def _():
            r = at_end
            r.pass_on(1, 0, FIRST, (SIDE,))
            r.pass_on(0, 1, SECOND_A, (IN,))
            r.pass_on(0, 1, SECOND_C, (IN,))
            take(r.done(1, 0, SECOND), rows, 1)
            r.send(1, 0, SECOND, (SIDE,))
            r.send(0, 1, FIRST, (IN,))
            r.pair(1, 0)
            r.pair(0, 1)
            r.pass_on(2, 0, FIRST, (SIDE,))

        @pl.when(end & (j == 2))
        def _():
            r = at_end
            take(r.done(2, 0, SECOND), rows + half_rows, 1)
            r.send(2, 0, SECOND, (SIDE,))
            r.pair(2, 0)
            r.pair(1, 1)
            r.arrived(3, 0, FIRST)
            r.send(3, 0, FIRST_A, (SIDE,))
            r.send(3, 0, FIRST_B, (SIDE,))
            r.send(3, 0, FIRST_TIP, (SIDE, SIDE_TWIN))

        @pl.when(end & (j == 3))
        def _():
            r = at_end
            take(r.done(3, 0, SECOND), rows + half_rows, 1)
            r.pair(3, 0)
            r.pair(2, 1)
            take(r.done(3, 1, FIRST_A), half_rows, 1)
            r.send(3, 1, FIRST_A, (PAIR,))
            r.send(3, 1, SECOND_A, (PAIR,))
            take(r.done(3, 1, FIRST_B), half_rows - 2 * tip)
            r.send(3, 1, FIRST_B, (PAIR,))
            r.send(3, 1, SECOND_B, (PAIR,))

        @pl.when(mid & (j == 1))
        def _():
            r = at_mid
            r.pass_on(2, 0, FIRST, (OUT, SIDE))
            r.pass_on(0, 0, FIRST, (IN,))
            r.pass_on(2, 0, SECOND, (OUT, SIDE))
            r.pair(2, 0)
            take(r.done(0, 0, SECOND), rows + half_rows, 1)
            r.send(0, 0, SECOND, (IN,))
            r.pair(0, 0)
            r.pair(1, 1)
            r.pass_on(3, 0, FIRST, (OUT, SIDE))
            r.pass_on(0, 1, SECOND_A, (IN,))
            r.pass_on(0, 1, SECOND_C, (IN,))

        @pl.when(mid & (j == 2))
        def _():
            r = at_mid
            r.pass_on(3, 0, SECOND, (OUT,))
            r.pair(3, 0)
            take(r.done(0, 1, FIRST), rows + half_rows, 2)
            r.pair(0, 1)
            r.pair(2, 1)

        @pl.when(mid & (j == 3))
        def _():
            r = at_mid
            r.arrived(3, 1, SECOND_A)
            r.send(3, 1, SECOND_A, (OUT,))
            r.arrived(3, 1, SECOND_C)
            r.send(3, 1, SECOND_B, (OUT,))
            r.send(3, 1, SECOND_TIP, (OUT, OUT_TWIN))
            r.send(3, 1, SECOND, (PAIR,))
            r.arrived(3, 1, FIRST)
            r.send(3, 1, FIRST, (PAIR,))

        slot = 2 * j - 1
        from_pair(j, 2)
        peak, total, scale, gained = absorb(slot, 2)
        row_max[...] = peak
        row_total[...] = total
        acc[...] = acc[...] * scale + gained
        return carry

    lax.fori_loop(1, planes, step, 0)

    @pl.when(end)
    def _():
        take(at_end.done(3, 1, FIRST_TIP), 4 * tip)
        take(pair_sem.at[planes], rows - 2 * tip, 1)

    @pl.when(mid)
    def _():
        from_pair(planes, 1)

    parts = []
    for cc in range(CORES):
        values = buf[pl.ds(((2 * planes - 1) * CORES + cc) * rows, rows), :]
        scores = lax.dot_general(
            buf[pl.ds(pl.multiple_of(core * rows, rows), rows), :], values,
            (((1,), (1,)), ((), ())), preferred_element_type=jnp.float32,
        ) * (kernel_gain / math.sqrt(width))
        tags = labs[(2 * planes - 1) * CORES + cc].astype(jnp.float32)
        parts.append((jnp.where(label_column == tags, scores, neg_large), values))
    before = row_max[...]
    peak = jnp.maximum(before, jnp.max(jnp.maximum(parts[0][0], parts[1][0]), axis=1, keepdims=True))
    scale = jnp.exp(before - peak)
    weights = [jnp.exp(masked - peak) for masked, _ in parts]
    total = row_total[...] * scale + jnp.sum(weights[0] + weights[1], axis=1, keepdims=True)
    inverse = 1.0 / total
    gained = sum(
        jnp.dot(w.astype(jnp.bfloat16), values, preferred_element_type=jnp.float32)
        for w, (_, values) in zip(weights, parts)
    )
    mean_ref[...] = ((acc[...] * scale + gained) * inverse).astype(mean_ref.dtype)
    density = peak + jnp.log(total)
    dens_ref[...] = jnp.transpose(jnp.broadcast_to(density, (rows, rows)))[:1, :]

    def sent(data_rows, labels):
        amount = meter.at[pl.ds(0, data_rows * row_units + labels)]
        pltpu.make_async_remote_copy(
            amount, amount, send_sem.at[0], pair_sem.at[0],
            device_id={"docs": targets[PAIR]}, device_id_type=MESH,
        ).wait_send()

    @pl.when(end)
    def _():
        sent(27 * half_rows - tip, 14)

    @pl.when(mid)
    def _():
        sent(33 * half_rows + tip, 16)


def publish_kernel(dens_ref, mean_ref, dens_out, mean_out, sem):
    copies = (
        pltpu.make_async_copy(mean_ref, mean_out, sem.at[0]),
        pltpu.make_async_copy(dens_ref, dens_out, sem.at[1]),
    )
    for copy in copies:
        copy.start()
    for copy in copies:
        copy.wait()


def publish(density, mean):
    held = [pltpu.with_memory_space_constraint(a, pltpu.VMEM) for a in (density, mean)]
    return pl.pallas_call(
        publish_kernel,
        out_shape=tuple(jax.ShapeDtypeStruct(a.shape, a.dtype) for a in (density, mean)),
        in_specs=[pl.BlockSpec(memory_space=pltpu.VMEM)] * 2,
        out_specs=(pl.BlockSpec(memory_space=pltpu.HBM),) * 2,
        scratch_shapes=[pltpu.SemaphoreType.DMA((2,))],
    )(*held)


def general_call(device_count, rows, width):
    grid_slow, grid_fast = chip_grid(device_count)
    chips = device_count // CORES
    vmem = pl.BlockSpec(memory_space=pltpu.VMEM)
    return pl.pallas_call(
        functools.partial(kernel, grid_slow, grid_fast),
        out_shape=(
            pltpu.VMEM((1, rows), jnp.float32),
            pltpu.VMEM((rows, width), jnp.bfloat16),
        ),
        in_specs=[pl.BlockSpec(memory_space=pl.ANY), pl.BlockSpec(memory_space=pl.ANY)],
        out_specs=(vmem, vmem),
        scratch_shapes=[
            pltpu.VMEM((device_count * rows, width), jnp.bfloat16),
            pltpu.VMEM((device_count, 1, rows), jnp.int32),
            pltpu.VMEM((rows, width), jnp.bfloat16),
            pltpu.VMEM((rows, width), jnp.float32),
            pltpu.VMEM((rows, 1), jnp.float32),
            pltpu.VMEM((rows, 1), jnp.float32),
            pltpu.SemaphoreType.DMA((5, chips * PIECES)),
            pltpu.SemaphoreType.DMA((device_count * PIECES,)),
            pltpu.SemaphoreType.DMA((5, chips)),
            pltpu.SemaphoreType.DMA((device_count,)),
            pltpu.SemaphoreType.DMA((PIECES + 1,)),
            pltpu.SemaphoreType.DMA((1,)),
        ],
        compiler_params=pltpu.CompilerParams(collective_id=0, has_side_effects=True),
    )


def folded_call(device_count, rows, width):
    chips = device_count // CORES
    vmem = pl.BlockSpec(memory_space=pltpu.VMEM)
    return pl.pallas_call(
        functools.partial(folded_kernel, chips // 2),
        out_shape=(
            pltpu.VMEM((1, rows), jnp.float32),
            pltpu.VMEM((rows, width), jnp.bfloat16),
        ),
        in_specs=[pl.BlockSpec(memory_space=pl.ANY), pl.BlockSpec(memory_space=pl.ANY)],
        out_specs=(vmem, vmem),
        scratch_shapes=[
            pltpu.VMEM((device_count * rows, width), jnp.bfloat16),
            pltpu.VMEM((device_count, 1, rows), jnp.int32),
            pltpu.VMEM(((33 * rows // 2 + rows // 8) * width // (2 * rows) + 2 * chips, 1, rows), jnp.int32),
            pltpu.VMEM((rows, width), jnp.float32),
            pltpu.VMEM((rows, 1), jnp.float32),
            pltpu.VMEM((rows, 1), jnp.float32),
            pltpu.SemaphoreType.DMA((1,)),
            pltpu.SemaphoreType.DMA((12,)),
            pltpu.SemaphoreType.DMA((chips // 2 + 1,)),
            pltpu.SemaphoreType.DMA((1,)),
            pltpu.SemaphoreType.REGULAR((2,)),
        ],
        compiler_params=pltpu.CompilerParams(collective_id=0, has_side_effects=True),
    )


def per_device(device_count, embeddings, labels, row_slot):
    rows, width = embeddings.shape
    call = folded_call if chip_grid(device_count) == FOLDED_GRID else general_call
    density, mean = call(device_count, rows, width)(embeddings, labels.reshape(1, rows))
    density, mean = publish(density, mean)
    return density.reshape(rows), mean


def solution(mesh):
    return jax.shard_map(
        functools.partial(per_device, mesh.shape["docs"]),
        mesh=mesh,
        in_specs=(P(("groups", "docs"), None), P(("groups", "docs")), P(("groups", "docs"))),
        out_specs=(P(("groups", "docs")), P(("groups", "docs"), None)),
        check_vma=False,
    )
```

```python
import functools
import math

import jax
import jax.numpy as jnp
from jax import lax
from jax.experimental import pallas as pl
from jax.experimental.pallas import tpu as pltpu
from jax.sharding import PartitionSpec as P

MESH = pl.DeviceIdType.MESH
CORES = 2
PIECES = 2
HALVES = 1
FOLDED_GRID = (4, 2)

neg_large = -1e30
neg_start = -1e29
kernel_gain = 4.0


def chip_grid(device_count):
    chips = device_count // CORES
    fast = 1
    while (2 * fast) * (2 * fast) <= chips and chips % (2 * fast) == 0:
        fast *= 2
    return chips // fast, fast


def kernel(
    grid_slow, grid_fast, x_ref, lab_ref, dens_ref, mean_ref,
    buf, labs, mine, acc, row_max, row_total,
    send_sem, recv_sem, lsend_sem, lrecv_sem, own_sem, own_lab_sem,
):
    rows, width = x_ref.shape
    part = rows // PIECES
    group = PIECES // HALVES
    half_rows = rows // HALVES
    keys = CORES * half_rows
    me = lax.axis_index("docs")
    core = lax.rem(me, CORES)
    chip = me // CORES
    y = lax.rem(chip, grid_fast)
    z = chip // grid_fast

    def device(zz, yy, cc):
        return (zz * grid_fast + yy) * CORES + cc

    targets = (
        (z > 0, device(z - 1, y, core)),
        (z < grid_slow - 1, device(z + 1, y, core)),
        (y > 0, device(z, y - 1, core)),
        (y < grid_fast - 1, device(z, y + 1, core)),
        (z >= 0, device(z, y, 1 - core)),
    )

    barrier = pltpu.get_barrier_semaphore()
    for there, target in targets:
        @pl.when(there)
        def _():
            pl.semaphore_signal(barrier, inc=1, device_id={"docs": target}, device_id_type=MESH)

    def data_of(zz, yy, cc, piece):
        where = ((zz * grid_fast + yy) * HALVES + piece // group) * CORES + cc
        return buf.at[pl.ds(pl.multiple_of((where * group + lax.rem(piece, group)) * part, part), part)]

    own_copies = [pltpu.make_async_copy(x_ref, mine, own_sem.at[PIECES])]
    for piece in range(PIECES):
        own_copies.append(
            pltpu.make_async_copy(
                x_ref.at[pl.ds(piece * part, part)], data_of(z, y, core, piece), own_sem.at[piece]
            )
        )
    own_copies.append(pltpu.make_async_copy(lab_ref, labs.at[me], own_lab_sem.at[0]))
    for copy in own_copies:
        copy.start()
    pl.semaphore_wait(barrier, sum(there.astype(jnp.int32) for there, _ in targets))

    def data_copy(direction, zz, yy, piece, own):
        data = data_of(zz, yy, core, piece)
        return pltpu.make_async_remote_copy(
            x_ref.at[pl.ds(piece * part, part)] if own else data, data,
            send_sem.at[direction, (zz * grid_fast + yy) * PIECES + piece],
            recv_sem.at[device(zz, yy, core) * PIECES + piece],
            device_id={"docs": targets[direction][1]}, device_id_type=MESH,
        )

    def lab_copy(direction, zz, yy, own):
        slot = device(zz, yy, core)
        return pltpu.make_async_remote_copy(
            lab_ref if own else labs.at[slot], labs.at[slot],
            lsend_sem.at[direction, zz * grid_fast + yy], lrecv_sem.at[slot],
            device_id={"docs": targets[direction][1]}, device_id_type=MESH,
        )

    def each(directions, wanted, zz, yy, piece, own, act):
        for direction, want in zip(directions, wanted):
            @pl.when(jnp.logical_and(targets[direction][0], want))
            def _():
                @pl.when(piece == 0)
                def _():
                    act(lab_copy(direction, zz, yy, own))
                act(data_copy(direction, zz, yy, piece, own))

    start = lambda copy: copy.start()
    finish = lambda copy: copy.wait_send()

    def arrived(zz, yy, cc, piece):
        slot = device(zz, yy, cc)
        @pl.when(piece == 0)
        def _():
            pltpu.make_async_remote_copy(
                labs.at[slot], labs.at[slot], lsend_sem.at[0, 0], lrecv_sem.at[slot],
                device_id={"docs": targets[4][1]}, device_id_type=MESH,
            ).wait_recv()
        data = data_of(zz, yy, cc, piece)
        pltpu.make_async_remote_copy(
            data, data, send_sem.at[0, 0], recv_sem.at[slot * PIECES + piece],
            device_id={"docs": targets[4][1]}, device_id_type=MESH,
        ).wait_recv()

    yes = z >= 0
    for piece in range(PIECES):
        each((2, 3, 0, 1, 4), (yes,) * 5, z, y, piece, True, start)

    row_max[...] = jnp.full_like(row_max, neg_large)
    row_total[...] = jnp.zeros_like(row_total)
    acc[...] = jnp.zeros_like(acc)
    own_copies[-1].wait()
    label_column = jnp.transpose(
        jnp.broadcast_to(labs[me].astype(jnp.float32), (rows, rows))
    )[:, :1]
    column = lax.broadcasted_iota(jnp.int32, (rows, keys), 1)
    gap = (
        column + (column // half_rows) * (rows - half_rows)
        - lax.broadcasted_iota(jnp.int32, (rows, keys), 0)
    )
    for copy in own_copies[:-1]:
        copy.wait()

    def compute(zz, yy, half):
        where = zz * grid_fast + yy
        values = buf[pl.ds(pl.multiple_of((where * HALVES + half) * keys, keys), keys), :]
        tags = []
        for cc in range(CORES):
            tag = labs[where * CORES + cc].astype(jnp.float32)
            pieces = [tag[:, h * half_rows:(h + 1) * half_rows] for h in range(HALVES)]
            picked = pieces[0]
            for h in range(1, HALVES):
                picked = jnp.where(half == h, pieces[h], picked)
            tags.append(picked)
        tags = jnp.concatenate(tags, axis=1)
        scores = lax.dot_general(
            mine[...], values, (((1,), (1,)), ((), ())), preferred_element_type=jnp.float32
        ) * (kernel_gain / math.sqrt(width))
        self_gap = jnp.where(where == chip, core * rows - half * half_rows, CORES * rows)
        absorb(scores, (label_column == tags) & (gap != self_gap), values)

    def compute_core(zz, yy, cc):
        slot = device(zz, yy, cc)
        values = buf[pl.ds(pl.multiple_of(slot * rows, rows), rows), :]
        scores = lax.dot_general(
            mine[...], values, (((1,), (1,)), ((), ())), preferred_element_type=jnp.float32
        ) * (kernel_gain / math.sqrt(width))
        absorb(scores, label_column == labs[slot].astype(jnp.float32), values)

    def absorb(scores, near, values):
        masked = jnp.where(near, scores, neg_large)
        before = row_max[...]
        peak = jnp.maximum(before, jnp.max(masked, axis=1, keepdims=True))
        weights = jnp.where(near, jnp.exp(masked - peak), 0.0)
        scale = jnp.exp(before - peak)
        row_max[...] = peak
        row_total[...] = row_total[...] * scale + jnp.sum(weights, axis=1, keepdims=True)
        acc[...] = acc[...] * scale + jnp.dot(
            weights.astype(jnp.bfloat16), values, preferred_element_type=jnp.float32
        )

    def meet(zz, yy, half):
        def one(p, carry):
            arrived(zz, yy, 1 - core, half * group + p)
            return carry
        lax.fori_loop(0, group, one, 0)
        compute(zz, yy, half)

    def visited(distance, side, reach, origin):
        place = origin + jnp.where(side == 0, -distance, distance)
        inside = (distance >= 0) & (distance < reach) & (place >= 0) & (place < reach)
        return place, inside & jnp.logical_or(distance > 0, side == 0)

    def other_columns(body):
        if grid_fast == 2:
            body(1 - y)
            return
        def one(i, carry):
            yy, valid = visited(i // 2 + 1, lax.rem(i, 2), grid_fast, y)
            @pl.when(valid)
            def _():
                body(yy)
            return carry
        lax.fori_loop(0, 2 * (grid_fast - 1), one, 0)

    def along(zz, piece, side, act):
        each((2, 3, 0, 1, 4), (yes, yes, side == 1, side == 0, yes), zz, y, piece, False, act)

    def across(zz, yy, piece, act):
        each((2, 3, 4), (yy > y, yy < y, yes), zz, yy, piece, False, act)

    def receive(zz, yy, piece):
        arrived(zz, yy, core, piece)
        across(zz, yy, piece, start)

    farthest = jnp.where(2 * z >= grid_slow, 0, grid_slow - 1)

    def event(e, carry):
        distance = e // (2 * PIECES)
        piece = lax.rem(e // 2, PIECES)
        side = lax.rem(e, 2)
        half = piece // group

        @pl.when(e == 2 * PIECES * grid_slow)
        def _():
            for p in range(PIECES):
                each((2, 3, 0, 1, 4), (yes,) * 5, z, y, p, True, finish)

        zz, valid = visited(distance, side, grid_slow, z)
        @pl.when(valid & (distance > 0))
        def _():
            arrived(zz, y, core, piece)
            along(zz, piece, side, start)

        z1, valid1 = visited(distance - 1, side, grid_slow, z)
        z2, valid2 = visited(distance - 2, side, grid_slow, z)
        @pl.when(valid2)
        def _():
            other_columns(lambda yy: receive(z2, yy, piece))
            @pl.when(distance > 2)
            def _():
                along(z2, piece, side, finish)

        z3, valid3 = visited(distance - 3, side, grid_slow, z)
        @pl.when(valid3)
        def _():
            other_columns(lambda yy: across(z3, yy, piece, finish))

        near = valid1 & (lax.rem(piece, group) == 0)
        if grid_fast == 2:
            far = valid2 & (lax.rem(piece, group) == group - 1) & (z2 != farthest)
            @pl.when(near | far)
            def _():
                def one(i, carry):
                    @pl.when(jnp.where(i == 0, near, far))
                    def _():
                        meet(jnp.where(i == 0, z1, z2), jnp.where(i == 0, y, 1 - y), half)
                    return carry
                lax.fori_loop(0, 2, one, 0)
        else:
            @pl.when(near)
            def _():
                meet(z1, y, half)
            @pl.when(valid2 & (lax.rem(piece, group) == group - 1))
            def _():
                other_columns(lambda yy: meet(z2, yy, half))
        return carry

    lax.fori_loop(0, 2 * PIECES * (grid_slow + 2), event, 0)
    if grid_fast == 2:
        def last_pair(i, carry):
            cc = jnp.where(i == 0, core, 1 - core)
            @pl.when(i == 1)
            def _():
                for p in range(PIECES):
                    arrived(farthest, 1 - y, 1 - core, p)
            compute_core(farthest, 1 - y, cc)
            return carry
        lax.fori_loop(0, CORES, last_pair, 0)

    total = row_total[...]
    density = row_max[...] + jnp.log(total)
    dens_ref[...] = jnp.transpose(jnp.broadcast_to(density, (rows, rows)))[:1, :]
    mean_ref[...] = (acc[...] / total).astype(mean_ref.dtype)

    for e in range(2 * PIECES):
        last, valid = visited(grid_slow - 1, e % 2, grid_slow, z)
        @pl.when(valid)
        def _():
            other_columns(lambda yy: across(last, yy, e // 2, finish))


def folded_kernel(
    planes, x_ref, lab_ref, dens_ref, mean_ref,
    buf, labs, meter, acc, row_max, row_total,
    send_sem, recv_sem, pair_sem, own_sem, ready_sem,
):
    rows, width = x_ref.shape
    row_units = width * x_ref.dtype.itemsize // (rows * lab_ref.dtype.itemsize)
    half_rows = rows // 2
    tip = rows // 8
    FIRST, SECOND, WHOLE = (0, half_rows), (half_rows, half_rows), (0, rows)
    FIRST_A, FIRST_B = (0, half_rows // 2), (half_rows // 2, half_rows // 2 - tip)
    FIRST_TIP, SECOND_TIP = (half_rows - tip, tip), (half_rows, tip)
    SECOND_B, SECOND_A = (half_rows + tip, half_rows // 2 - tip), (rows - half_rows // 2, half_rows // 2)
    SECOND_C = (half_rows, half_rows // 2)
    me = lax.axis_index("docs")
    core = lax.rem(me, CORES)
    y = lax.rem(me // CORES, 2)
    z = me // (CORES * 2)
    barrier = pltpu.get_barrier_semaphore()
    for higher, stride in ((z < planes - 1, 2 * CORES), (y == 0, CORES), (core == 0, 1)):
        @pl.when(higher)
        def _():
            pl.semaphore_signal(barrier, inc=1, device_id={"docs": me + stride}, device_id_type=MESH)

    mirrored = 2 * z >= planes
    end = (z == 0) | (z == planes - 1)
    mid = jnp.logical_not(end)

    def device(k, column, cc):
        zz = jnp.where(mirrored, planes - 1 - k, k)
        return (zz * 2 + column) * CORES + cc

    OUT, IN, SIDE, PAIR, OUT_TWIN, SIDE_TWIN = range(6)
    home = jnp.where(end, 0, 1)
    inward = jnp.where(mirrored, -2 * CORES, 2 * CORES)
    across, beside = CORES - 2 * CORES * y, 1 - 2 * core
    targets = (me - inward, me + inward, me + across, me + beside, me - inward + beside, me + across + beside)
    END_ORDER = ((0, 0), (1, 0), (0, 1), (2, 0), (1, 1), (3, 0), (2, 1), (3, 1))
    MID_ORDER = ((1, 0), (2, 0), (0, 0), (3, 0), (0, 1), (1, 1), (2, 1), (3, 1))

    up = (mid & mirrored, jnp.logical_not(mirrored), y == 0, core == 0)
    down = (mid & jnp.logical_not(mirrored), mirrored, y == 1, core == 1)

    def rows_of(slot, cc, part):
        first, size = part
        first = (slot * CORES + cc) * rows + first
        return buf.at[pl.ds(pl.multiple_of(first, tip), size)]

    lower_count = (z > 0).astype(jnp.int32) + y + core
    @pl.when(lower_count > 0)
    def _():
        pl.semaphore_wait(barrier, lower_count)

    def data_copy(direction, slot, there, done, part, own=False):
        return pltpu.make_async_remote_copy(
            x_ref.at[pl.ds(*part)] if own else rows_of(slot, core, part), rows_of(there, core, part),
            send_sem.at[0], done,
            device_id={"docs": targets[direction]}, device_id_type=MESH,
        )

    def lab_copy(direction, slot, there, done, own=False):
        return pltpu.make_async_remote_copy(
            lab_ref if own else labs.at[slot * CORES + core], labs.at[there * CORES + core],
            send_sem.at[0], done,
            device_id={"docs": targets[direction]}, device_id_type=MESH,
        )

    def take(done, data_rows, labels=0):
        amount = meter.at[pl.ds(0, data_rows * row_units + labels)]
        pltpu.make_async_remote_copy(
            amount, amount, send_sem.at[0], done,
            device_id={"docs": targets[PAIR]}, device_id_type=MESH,
        ).wait_recv()

    class Role:
        def __init__(self, is_end):
            self.is_end = is_end
            self.order = END_ORDER if is_end else MID_ORDER

        def slot(self, k, other):
            return self.order.index((k, other))

        def done(self, k, other, part):
            second = 1 if part == SECOND else 0
            if self.is_end:
                if (k, other) == (3, 1):
                    index = 8 if part in (FIRST_A, SECOND_A) else 9 if part in (FIRST_B, SECOND_B) else 10
                elif (k, other) == (0, 1):
                    index = {FIRST: 1, SECOND_A: 2, SECOND_C: 3}[part]
                else:
                    index = {(1, 0): second, (2, 0): 4 + second, (1, 1): 5, (3, 0): 6 + second, (2, 1): 7}[k, other]
            elif (k, other) == (3, 1):
                index = 9 if part == SECOND_A else 10 if part == SECOND_C else 11
            elif (k, other) == (0, 1):
                index = {FIRST: 8, SECOND_A: 6, SECOND_C: 7}[part]
            else:
                index = {(2, 0): second, (0, 0): 2 + second, (1, 1): 3, (3, 0): 4 + second, (2, 1): 8}[k, other]
            return recv_sem.at[index]

        def receiver(self, direction, k, other):
            if direction in (SIDE, SIDE_TWIN):
                return self, k, 1 - other
            if direction == PAIR:
                return self, k, other
            if direction in (OUT, OUT_TWIN):
                return at_end, k, other
            return at_mid, k if self.is_end else planes - 1 - k, other

        def send(self, k, other, part, directions, own=False):
            for direction in directions:
                role, kk, oo = self.receiver(direction, k, other)
                slot, there = self.slot(k, other), role.slot(kk, oo)
                done = pair_sem.at[(there + 1) // 2] if direction == PAIR else role.done(kk, oo, part)
                if part in (FIRST, FIRST_A, WHOLE):
                    lab_copy(direction, slot, there, done, own).start()
                data_copy(direction, slot, there, done, part, own).start()

        def arrived(self, k, other, part):
            take(self.done(k, other, part), part[1], 1 if part[0] == 0 else 0)

        def pass_on(self, k, other, part, directions):
            self.arrived(k, other, part)
            self.send(k, other, part, directions)

        def pair(self, k, other):
            self.send(k, other, WHOLE, (PAIR,))

    at_end, at_mid = Role(True), Role(False)

    def start_own(direction):
        def by(role):
            k = 0 if role.is_end else 1
            for part in {SIDE: (SECOND_A, SECOND_C, FIRST), PAIR: (WHOLE,)}.get(direction, (FIRST, SECOND)):
                role.send(k, 0, part, (direction,), own=True)

        if direction == OUT:
            by(at_mid)
        elif direction == PAIR:
            by(at_end)
        else:
            pl.when(end)(lambda: by(at_end))
            pl.when(mid)(lambda: by(at_mid))

    for direction, lower in enumerate(down):
        @pl.when(lower)
        def _():
            start_own(direction)
    for lower, stride, axis in ((z > 0, 2 * CORES, 0), (y == 1, CORES, 0), (core == 1, 1, 1)):
        @pl.when(lower)
        def _():
            pl.semaphore_signal(
                ready_sem.at[axis], inc=1, device_id={"docs": me - stride}, device_id_type=MESH,
            )

    own_data = pltpu.make_async_copy(x_ref, rows_of(0, core, WHOLE), own_sem.at[0])
    own_data.start()
    own_lab = pltpu.make_async_copy(lab_ref, labs.at[core], own_sem.at[0])
    own_lab.start()
    @pl.when(up[PAIR])
    def _():
        pl.semaphore_wait(ready_sem.at[1], 1)
        start_own(PAIR)

    higher_count = sum(higher.astype(jnp.int32) for higher in up[:PAIR])
    @pl.when(higher_count > 0)
    def _():
        pl.semaphore_wait(ready_sem.at[0], higher_count)
    for direction in (SIDE, IN, OUT):
        @pl.when(up[direction])
        def _():
            start_own(direction)

    own_amount = meter.at[pl.ds(0, rows * row_units + 1)]
    pltpu.make_async_copy(own_amount, own_amount, own_sem.at[0]).wait()
    label_column = jnp.transpose(
        jnp.broadcast_to(labs[core].astype(jnp.float32), (rows, rows))
    )[:, :1]

    def from_pair(group, slots):
        take(pair_sem.at[group], slots * rows, slots)

    def masked_scores(slot, count):
        keys = count * CORES * rows
        values = buf[pl.ds(pl.multiple_of(slot * CORES * rows, rows), keys), :]
        mine = buf[pl.ds(pl.multiple_of(core * rows, rows), rows), :]
        tags = jnp.concatenate(
            [labs[slot * CORES + n].astype(jnp.float32) for n in range(count * CORES)], axis=1
        )
        scores = lax.dot_general(
            mine, values, (((1,), (1,)), ((), ())), preferred_element_type=jnp.float32
        ) * (kernel_gain / math.sqrt(width))
        return scores, label_column == tags, values

    def first_block():
        scores, near, values = masked_scores(0, 1)
        gap = lax.broadcasted_iota(jnp.int32, near.shape, 1) - lax.broadcasted_iota(jnp.int32, near.shape, 0)
        masked = jnp.where(near & (gap != core * rows), scores, neg_large)
        peak = jnp.maximum(jnp.max(masked, axis=1, keepdims=True), neg_start)
        weights = jnp.exp(masked - peak)
        row_max[...] = peak
        row_total[...] = jnp.sum(weights, axis=1, keepdims=True)
        acc[...] = jnp.dot(weights.astype(jnp.bfloat16), values, preferred_element_type=jnp.float32)

    def absorb(slot, count):
        scores, near, values = masked_scores(slot, count)
        masked = jnp.where(near, scores, neg_large)
        before = row_max[...]
        peak = jnp.maximum(before, jnp.max(masked, axis=1, keepdims=True))
        weights = jnp.exp(masked - peak)
        scale = jnp.exp(before - peak)
        total = row_total[...] * scale + jnp.sum(weights, axis=1, keepdims=True)
        gained = jnp.dot(weights.astype(jnp.bfloat16), values, preferred_element_type=jnp.float32)
        return peak, total, scale, gained

    from_pair(0, 1)
    first_block()

    def step(j, carry):
        @pl.when(end & (j == 1))
        def _():
            r = at_end
            r.pass_on(1, 0, FIRST, (SIDE,))
            r.pass_on(0, 1, SECOND_A, (IN,))
            r.pass_on(0, 1, SECOND_C, (IN,))
            take(r.done(1, 0, SECOND), rows, 1)
            r.send(1, 0, SECOND, (SIDE,))
            r.send(0, 1, FIRST, (IN,))
            r.pair(1, 0)
            r.pair(0, 1)
            r.pass_on(2, 0, FIRST, (SIDE,))

        @pl.when(end & (j == 2))
        def _():
            r = at_end
            take(r.done(2, 0, SECOND), rows + half_rows, 1)
            r.send(2, 0, SECOND, (SIDE,))
            r.pair(2, 0)
            r.pair(1, 1)
            r.arrived(3, 0, FIRST)
            r.send(3, 0, FIRST_A, (SIDE,))
            r.send(3, 0, FIRST_B, (SIDE,))
            r.send(3, 0, FIRST_TIP, (SIDE, SIDE_TWIN))

        @pl.when(end & (j == 3))
        def _():
            r = at_end
            take(r.done(3, 0, SECOND), rows + half_rows, 1)
            r.pair(3, 0)
            r.pair(2, 1)
            take(r.done(3, 1, FIRST_A), half_rows, 1)
            r.send(3, 1, FIRST_A, (PAIR,))
            r.send(3, 1, SECOND_A, (PAIR,))
            take(r.done(3, 1, FIRST_B), half_rows - 2 * tip)
            r.send(3, 1, FIRST_B, (PAIR,))
            r.send(3, 1, SECOND_B, (PAIR,))

        @pl.when(mid & (j == 1))
        def _():
            r = at_mid
            r.pass_on(2, 0, FIRST, (OUT, SIDE))
            r.pass_on(0, 0, FIRST, (IN,))
            r.pass_on(2, 0, SECOND, (OUT, SIDE))
            r.pair(2, 0)
            take(r.done(0, 0, SECOND), rows + half_rows, 1)
            r.send(0, 0, SECOND, (IN,))
            r.pair(0, 0)
            r.pair(1, 1)
            r.pass_on(3, 0, FIRST, (OUT, SIDE))
            r.pass_on(0, 1, SECOND_A, (IN,))
            r.pass_on(0, 1, SECOND_C, (IN,))

        @pl.when(mid & (j == 2))
        def _():
            r = at_mid
            r.pass_on(3, 0, SECOND, (OUT,))
            r.pair(3, 0)
            take(r.done(0, 1, FIRST), rows + half_rows, 2)
            r.pair(0, 1)
            r.pair(2, 1)

        @pl.when(mid & (j == 3))
        def _():
            r = at_mid
            r.arrived(3, 1, SECOND_A)
            r.send(3, 1, SECOND_A, (OUT,))
            r.arrived(3, 1, SECOND_C)
            r.send(3, 1, SECOND_B, (OUT,))
            r.send(3, 1, SECOND_TIP, (OUT, OUT_TWIN))
            r.send(3, 1, SECOND, (PAIR,))
            r.arrived(3, 1, FIRST)
            r.send(3, 1, FIRST, (PAIR,))

        slot = 2 * j - 1
        from_pair(j, 2)
        peak, total, scale, gained = absorb(slot, 2)
        row_max[...] = peak
        row_total[...] = total
        acc[...] = acc[...] * scale + gained
        return carry

    lax.fori_loop(1, planes, step, 0)

    @pl.when(end)
    def _():
        take(at_end.done(3, 1, FIRST_TIP), 4 * tip)
        take(pair_sem.at[planes], rows - 2 * tip, 1)

    @pl.when(mid)
    def _():
        from_pair(planes, 1)

    parts = []
    for cc in range(CORES):
        values = buf[pl.ds(((2 * planes - 1) * CORES + cc) * rows, rows), :]
        scores = lax.dot_general(
            buf[pl.ds(pl.multiple_of(core * rows, rows), rows), :], values,
            (((1,), (1,)), ((), ())), preferred_element_type=jnp.float32,
        ) * (kernel_gain / math.sqrt(width))
        tags = labs[(2 * planes - 1) * CORES + cc].astype(jnp.float32)
        parts.append((jnp.where(label_column == tags, scores, neg_large), values))
    before = row_max[...]
    peak = jnp.maximum(before, jnp.max(jnp.maximum(parts[0][0], parts[1][0]), axis=1, keepdims=True))
    scale = jnp.exp(before - peak)
    weights = [jnp.exp(masked - peak) for masked, _ in parts]
    total = row_total[...] * scale + jnp.sum(weights[0] + weights[1], axis=1, keepdims=True)
    inverse = 1.0 / total
    gained = jnp.dot(
        jnp.concatenate([w.astype(jnp.bfloat16) for w in weights], axis=1),
        buf[pl.ds((2 * planes - 1) * CORES * rows, CORES * rows), :], preferred_element_type=jnp.float32,
    )
    mean_ref[...] = ((acc[...] * scale + gained) * inverse).astype(mean_ref.dtype)
    density = peak + jnp.log(total)
    dens_ref[...] = jnp.transpose(jnp.broadcast_to(density, (rows, rows)))[:1, :]

    def sent(data_rows, labels):
        amount = meter.at[pl.ds(0, data_rows * row_units + labels)]
        pltpu.make_async_remote_copy(
            amount, amount, send_sem.at[0], pair_sem.at[0],
            device_id={"docs": targets[PAIR]}, device_id_type=MESH,
        ).wait_send()

    @pl.when(end)
    def _():
        sent(27 * half_rows - tip, 14)

    @pl.when(mid)
    def _():
        sent(33 * half_rows + tip, 16)


def publish_kernel(dens_ref, mean_ref, dens_out, mean_out, sem):
    copies = (
        pltpu.make_async_copy(mean_ref, mean_out, sem.at[0]),
        pltpu.make_async_copy(dens_ref, dens_out, sem.at[1]),
    )
    for copy in copies:
        copy.start()
    for copy in copies:
        copy.wait()


def publish(density, mean):
    held = [pltpu.with_memory_space_constraint(a, pltpu.VMEM) for a in (density, mean)]
    return pl.pallas_call(
        publish_kernel,
        out_shape=tuple(jax.ShapeDtypeStruct(a.shape, a.dtype) for a in (density, mean)),
        in_specs=[pl.BlockSpec(memory_space=pltpu.VMEM)] * 2,
        out_specs=(pl.BlockSpec(memory_space=pltpu.HBM),) * 2,
        scratch_shapes=[pltpu.SemaphoreType.DMA((2,))],
    )(*held)


def general_call(device_count, rows, width):
    grid_slow, grid_fast = chip_grid(device_count)
    chips = device_count // CORES
    vmem = pl.BlockSpec(memory_space=pltpu.VMEM)
    return pl.pallas_call(
        functools.partial(kernel, grid_slow, grid_fast),
        out_shape=(
            pltpu.VMEM((1, rows), jnp.float32),
            pltpu.VMEM((rows, width), jnp.bfloat16),
        ),
        in_specs=[pl.BlockSpec(memory_space=pl.ANY), pl.BlockSpec(memory_space=pl.ANY)],
        out_specs=(vmem, vmem),
        scratch_shapes=[
            pltpu.VMEM((device_count * rows, width), jnp.bfloat16),
            pltpu.VMEM((device_count, 1, rows), jnp.int32),
            pltpu.VMEM((rows, width), jnp.bfloat16),
            pltpu.VMEM((rows, width), jnp.float32),
            pltpu.VMEM((rows, 1), jnp.float32),
            pltpu.VMEM((rows, 1), jnp.float32),
            pltpu.SemaphoreType.DMA((5, chips * PIECES)),
            pltpu.SemaphoreType.DMA((device_count * PIECES,)),
            pltpu.SemaphoreType.DMA((5, chips)),
            pltpu.SemaphoreType.DMA((device_count,)),
            pltpu.SemaphoreType.DMA((PIECES + 1,)),
            pltpu.SemaphoreType.DMA((1,)),
        ],
        compiler_params=pltpu.CompilerParams(collective_id=0, has_side_effects=True),
    )


def folded_call(device_count, rows, width):
    chips = device_count // CORES
    vmem = pl.BlockSpec(memory_space=pltpu.VMEM)
    return pl.pallas_call(
        functools.partial(folded_kernel, chips // 2),
        out_shape=(
            pltpu.VMEM((1, rows), jnp.float32),
            pltpu.VMEM((rows, width), jnp.bfloat16),
        ),
        in_specs=[pl.BlockSpec(memory_space=pl.ANY), pl.BlockSpec(memory_space=pl.ANY)],
        out_specs=(vmem, vmem),
        scratch_shapes=[
            pltpu.VMEM((device_count * rows, width), jnp.bfloat16),
            pltpu.VMEM((device_count, 1, rows), jnp.int32),
            pltpu.VMEM(((33 * rows // 2 + rows // 8) * width // (2 * rows) + 2 * chips, 1, rows), jnp.int32),
            pltpu.VMEM((rows, width), jnp.float32),
            pltpu.VMEM((rows, 1), jnp.float32),
            pltpu.VMEM((rows, 1), jnp.float32),
            pltpu.SemaphoreType.DMA((1,)),
            pltpu.SemaphoreType.DMA((12,)),
            pltpu.SemaphoreType.DMA((chips // 2 + 1,)),
            pltpu.SemaphoreType.DMA((1,)),
            pltpu.SemaphoreType.REGULAR((2,)),
        ],
        compiler_params=pltpu.CompilerParams(collective_id=0, has_side_effects=True),
    )


def per_device(device_count, embeddings, labels, row_slot):
    rows, width = embeddings.shape
    call = folded_call if chip_grid(device_count) == FOLDED_GRID else general_call
    density, mean = call(device_count, rows, width)(embeddings, labels.reshape(1, rows))
    density, mean = publish(density, mean)
    return density.reshape(rows), mean


def solution(mesh):
    return jax.shard_map(
        functools.partial(per_device, mesh.shape["docs"]),
        mesh=mesh,
        in_specs=(P(("groups", "docs"), None), P(("groups", "docs")), P(("groups", "docs"))),
        out_specs=(P(("groups", "docs")), P(("groups", "docs"), None)),
        check_vma=False,
    )
```

```python
import functools
import math

import jax
import jax.numpy as jnp
from jax import lax
from jax.experimental import pallas as pl
from jax.experimental.pallas import tpu as pltpu
from jax.sharding import PartitionSpec as P

MESH = pl.DeviceIdType.MESH
CORES = 2
PIECES = 2
HALVES = 1
FOLDED_GRID = (4, 2)

neg_large = -1e30
neg_start = -1e29
kernel_gain = 4.0


def chip_grid(device_count):
    chips = device_count // CORES
    fast = 1
    while (2 * fast) * (2 * fast) <= chips and chips % (2 * fast) == 0:
        fast *= 2
    return chips // fast, fast


def kernel(
    grid_slow, grid_fast, x_ref, lab_ref, dens_ref, mean_ref,
    buf, labs, mine, acc, row_max, row_total,
    send_sem, recv_sem, lsend_sem, lrecv_sem, own_sem, own_lab_sem,
):
    rows, width = x_ref.shape
    part = rows // PIECES
    group = PIECES // HALVES
    half_rows = rows // HALVES
    keys = CORES * half_rows
    me = lax.axis_index("docs")
    core = lax.rem(me, CORES)
    chip = me // CORES
    y = lax.rem(chip, grid_fast)
    z = chip // grid_fast

    def device(zz, yy, cc):
        return (zz * grid_fast + yy) * CORES + cc

    targets = (
        (z > 0, device(z - 1, y, core)),
        (z < grid_slow - 1, device(z + 1, y, core)),
        (y > 0, device(z, y - 1, core)),
        (y < grid_fast - 1, device(z, y + 1, core)),
        (z >= 0, device(z, y, 1 - core)),
    )

    barrier = pltpu.get_barrier_semaphore()
    for there, target in targets:
        @pl.when(there)
        def _():
            pl.semaphore_signal(barrier, inc=1, device_id={"docs": target}, device_id_type=MESH)

    def data_of(zz, yy, cc, piece):
        where = ((zz * grid_fast + yy) * HALVES + piece // group) * CORES + cc
        return buf.at[pl.ds(pl.multiple_of((where * group + lax.rem(piece, group)) * part, part), part)]

    own_copies = [pltpu.make_async_copy(x_ref, mine, own_sem.at[PIECES])]
    for piece in range(PIECES):
        own_copies.append(
            pltpu.make_async_copy(
                x_ref.at[pl.ds(piece * part, part)], data_of(z, y, core, piece), own_sem.at[piece]
            )
        )
    own_copies.append(pltpu.make_async_copy(lab_ref, labs.at[me], own_lab_sem.at[0]))
    for copy in own_copies:
        copy.start()
    pl.semaphore_wait(barrier, sum(there.astype(jnp.int32) for there, _ in targets))

    def data_copy(direction, zz, yy, piece, own):
        data = data_of(zz, yy, core, piece)
        return pltpu.make_async_remote_copy(
            x_ref.at[pl.ds(piece * part, part)] if own else data, data,
            send_sem.at[direction, (zz * grid_fast + yy) * PIECES + piece],
            recv_sem.at[device(zz, yy, core) * PIECES + piece],
            device_id={"docs": targets[direction][1]}, device_id_type=MESH,
        )

    def lab_copy(direction, zz, yy, own):
        slot = device(zz, yy, core)
        return pltpu.make_async_remote_copy(
            lab_ref if own else labs.at[slot], labs.at[slot],
            lsend_sem.at[direction, zz * grid_fast + yy], lrecv_sem.at[slot],
            device_id={"docs": targets[direction][1]}, device_id_type=MESH,
        )

    def each(directions, wanted, zz, yy, piece, own, act):
        for direction, want in zip(directions, wanted):
            @pl.when(jnp.logical_and(targets[direction][0], want))
            def _():
                @pl.when(piece == 0)
                def _():
                    act(lab_copy(direction, zz, yy, own))
                act(data_copy(direction, zz, yy, piece, own))

    start = lambda copy: copy.start()
    finish = lambda copy: copy.wait_send()

    def arrived(zz, yy, cc, piece):
        slot = device(zz, yy, cc)
        @pl.when(piece == 0)
        def _():
            pltpu.make_async_remote_copy(
                labs.at[slot], labs.at[slot], lsend_sem.at[0, 0], lrecv_sem.at[slot],
                device_id={"docs": targets[4][1]}, device_id_type=MESH,
            ).wait_recv()
        data = data_of(zz, yy, cc, piece)
        pltpu.make_async_remote_copy(
            data, data, send_sem.at[0, 0], recv_sem.at[slot * PIECES + piece],
            device_id={"docs": targets[4][1]}, device_id_type=MESH,
        ).wait_recv()

    yes = z >= 0
    for piece in range(PIECES):
        each((2, 3, 0, 1, 4), (yes,) * 5, z, y, piece, True, start)

    row_max[...] = jnp.full_like(row_max, neg_large)
    row_total[...] = jnp.zeros_like(row_total)
    acc[...] = jnp.zeros_like(acc)
    own_copies[-1].wait()
    label_column = jnp.transpose(
        jnp.broadcast_to(labs[me].astype(jnp.float32), (rows, rows))
    )[:, :1]
    column = lax.broadcasted_iota(jnp.int32, (rows, keys), 1)
    gap = (
        column + (column // half_rows) * (rows - half_rows)
        - lax.broadcasted_iota(jnp.int32, (rows, keys), 0)
    )
    for copy in own_copies[:-1]:
        copy.wait()

    def compute(zz, yy, half):
        where = zz * grid_fast + yy
        values = buf[pl.ds(pl.multiple_of((where * HALVES + half) * keys, keys), keys), :]
        tags = []
        for cc in range(CORES):
            tag = labs[where * CORES + cc].astype(jnp.float32)
            pieces = [tag[:, h * half_rows:(h + 1) * half_rows] for h in range(HALVES)]
            picked = pieces[0]
            for h in range(1, HALVES):
                picked = jnp.where(half == h, pieces[h], picked)
            tags.append(picked)
        tags = jnp.concatenate(tags, axis=1)
        scores = lax.dot_general(
            mine[...], values, (((1,), (1,)), ((), ())), preferred_element_type=jnp.float32
        ) * (kernel_gain / math.sqrt(width))
        self_gap = jnp.where(where == chip, core * rows - half * half_rows, CORES * rows)
        absorb(scores, (label_column == tags) & (gap != self_gap), values)

    def compute_core(zz, yy, cc):
        slot = device(zz, yy, cc)
        values = buf[pl.ds(pl.multiple_of(slot * rows, rows), rows), :]
        scores = lax.dot_general(
            mine[...], values, (((1,), (1,)), ((), ())), preferred_element_type=jnp.float32
        ) * (kernel_gain / math.sqrt(width))
        absorb(scores, label_column == labs[slot].astype(jnp.float32), values)

    def absorb(scores, near, values):
        masked = jnp.where(near, scores, neg_large)
        before = row_max[...]
        peak = jnp.maximum(before, jnp.max(masked, axis=1, keepdims=True))
        weights = jnp.where(near, jnp.exp(masked - peak), 0.0)
        scale = jnp.exp(before - peak)
        row_max[...] = peak
        row_total[...] = row_total[...] * scale + jnp.sum(weights, axis=1, keepdims=True)
        acc[...] = acc[...] * scale + jnp.dot(
            weights.astype(jnp.bfloat16), values, preferred_element_type=jnp.float32
        )

    def meet(zz, yy, half):
        def one(p, carry):
            arrived(zz, yy, 1 - core, half * group + p)
            return carry
        lax.fori_loop(0, group, one, 0)
        compute(zz, yy, half)

    def visited(distance, side, reach, origin):
        place = origin + jnp.where(side == 0, -distance, distance)
        inside = (distance >= 0) & (distance < reach) & (place >= 0) & (place < reach)
        return place, inside & jnp.logical_or(distance > 0, side == 0)

    def other_columns(body):
        if grid_fast == 2:
            body(1 - y)
            return
        def one(i, carry):
            yy, valid = visited(i // 2 + 1, lax.rem(i, 2), grid_fast, y)
            @pl.when(valid)
            def _():
                body(yy)
            return carry
        lax.fori_loop(0, 2 * (grid_fast - 1), one, 0)

    def along(zz, piece, side, act):
        each((2, 3, 0, 1, 4), (yes, yes, side == 1, side == 0, yes), zz, y, piece, False, act)

    def across(zz, yy, piece, act):
        each((2, 3, 4), (yy > y, yy < y, yes), zz, yy, piece, False, act)

    def receive(zz, yy, piece):
        arrived(zz, yy, core, piece)
        across(zz, yy, piece, start)

    farthest = jnp.where(2 * z >= grid_slow, 0, grid_slow - 1)

    def event(e, carry):
        distance = e // (2 * PIECES)
        piece = lax.rem(e // 2, PIECES)
        side = lax.rem(e, 2)
        half = piece // group

        @pl.when(e == 2 * PIECES * grid_slow)
        def _():
            for p in range(PIECES):
                each((2, 3, 0, 1, 4), (yes,) * 5, z, y, p, True, finish)

        zz, valid = visited(distance, side, grid_slow, z)
        @pl.when(valid & (distance > 0))
        def _():
            arrived(zz, y, core, piece)
            along(zz, piece, side, start)

        z1, valid1 = visited(distance - 1, side, grid_slow, z)
        z2, valid2 = visited(distance - 2, side, grid_slow, z)
        @pl.when(valid2)
        def _():
            other_columns(lambda yy: receive(z2, yy, piece))
            @pl.when(distance > 2)
            def _():
                along(z2, piece, side, finish)

        z3, valid3 = visited(distance - 3, side, grid_slow, z)
        @pl.when(valid3)
        def _():
            other_columns(lambda yy: across(z3, yy, piece, finish))

        near = valid1 & (lax.rem(piece, group) == 0)
        if grid_fast == 2:
            far = valid2 & (lax.rem(piece, group) == group - 1) & (z2 != farthest)
            @pl.when(near | far)
            def _():
                def one(i, carry):
                    @pl.when(jnp.where(i == 0, near, far))
                    def _():
                        meet(jnp.where(i == 0, z1, z2), jnp.where(i == 0, y, 1 - y), half)
                    return carry
                lax.fori_loop(0, 2, one, 0)
        else:
            @pl.when(near)
            def _():
                meet(z1, y, half)
            @pl.when(valid2 & (lax.rem(piece, group) == group - 1))
            def _():
                other_columns(lambda yy: meet(z2, yy, half))
        return carry

    lax.fori_loop(0, 2 * PIECES * (grid_slow + 2), event, 0)
    if grid_fast == 2:
        def last_pair(i, carry):
            cc = jnp.where(i == 0, core, 1 - core)
            @pl.when(i == 1)
            def _():
                for p in range(PIECES):
                    arrived(farthest, 1 - y, 1 - core, p)
            compute_core(farthest, 1 - y, cc)
            return carry
        lax.fori_loop(0, CORES, last_pair, 0)

    total = row_total[...]
    density = row_max[...] + jnp.log(total)
    dens_ref[...] = jnp.transpose(jnp.broadcast_to(density, (rows, rows)))[:1, :]
    mean_ref[...] = (acc[...] / total).astype(mean_ref.dtype)

    for e in range(2 * PIECES):
        last, valid = visited(grid_slow - 1, e % 2, grid_slow, z)
        @pl.when(valid)
        def _():
            other_columns(lambda yy: across(last, yy, e // 2, finish))


def folded_kernel(
    planes, x_ref, lab_ref, dens_ref, mean_ref,
    buf, labs, meter, acc, row_max, row_total,
    send_sem, recv_sem, pair_sem, own_sem, ready_sem,
):
    rows, width = x_ref.shape
    row_units = width * x_ref.dtype.itemsize // (rows * lab_ref.dtype.itemsize)
    half_rows = rows // 2
    tip = rows // 8
    FIRST, SECOND, WHOLE = (0, half_rows), (half_rows, half_rows), (0, rows)
    FIRST_A, FIRST_B = (0, half_rows // 2), (half_rows // 2, half_rows // 2 - tip)
    FIRST_TIP, SECOND_TIP = (half_rows - tip, tip), (half_rows, tip)
    SECOND_B, SECOND_A = (half_rows + tip, half_rows // 2 - tip), (rows - half_rows // 2, half_rows // 2)
    SECOND_C = (half_rows, half_rows // 2)
    me = lax.axis_index("docs")
    core = lax.rem(me, CORES)
    y = lax.rem(me // CORES, 2)
    z = me // (CORES * 2)
    barrier = pltpu.get_barrier_semaphore()
    for higher, stride in ((z < planes - 1, 2 * CORES), (y == 0, CORES), (core == 0, 1)):
        @pl.when(higher)
        def _():
            pl.semaphore_signal(barrier, inc=1, device_id={"docs": me + stride}, device_id_type=MESH)

    mirrored = 2 * z >= planes
    end = (z == 0) | (z == planes - 1)
    mid = jnp.logical_not(end)

    def device(k, column, cc):
        zz = jnp.where(mirrored, planes - 1 - k, k)
        return (zz * 2 + column) * CORES + cc

    OUT, IN, SIDE, PAIR, OUT_TWIN, SIDE_TWIN = range(6)
    home = jnp.where(end, 0, 1)
    inward = jnp.where(mirrored, -2 * CORES, 2 * CORES)
    across, beside = CORES - 2 * CORES * y, 1 - 2 * core
    targets = (me - inward, me + inward, me + across, me + beside, me - inward + beside, me + across + beside)
    END_ORDER = ((0, 0), (1, 0), (0, 1), (2, 0), (1, 1), (3, 0), (2, 1), (3, 1))
    MID_ORDER = ((1, 0), (2, 0), (0, 0), (3, 0), (0, 1), (1, 1), (2, 1), (3, 1))

    up = (mid & mirrored, jnp.logical_not(mirrored), y == 0, core == 0)
    down = (mid & jnp.logical_not(mirrored), mirrored, y == 1, core == 1)

    def rows_of(slot, cc, part):
        first, size = part
        first = (slot * CORES + cc) * rows + first
        return buf.at[pl.ds(pl.multiple_of(first, tip), size)]

    lower_count = (z > 0).astype(jnp.int32) + y + core
    @pl.when(lower_count > 0)
    def _():
        pl.semaphore_wait(barrier, lower_count)

    def data_copy(direction, slot, there, done, part, own=False):
        return pltpu.make_async_remote_copy(
            x_ref.at[pl.ds(*part)] if own else rows_of(slot, core, part), rows_of(there, core, part),
            send_sem.at[0], done,
            device_id={"docs": targets[direction]}, device_id_type=MESH,
        )

    def lab_copy(direction, slot, there, done, own=False):
        return pltpu.make_async_remote_copy(
            lab_ref if own else labs.at[slot * CORES + core], labs.at[there * CORES + core],
            send_sem.at[0], done,
            device_id={"docs": targets[direction]}, device_id_type=MESH,
        )

    def take(done, data_rows, labels=0):
        amount = meter.at[pl.ds(0, data_rows * row_units + labels)]
        pltpu.make_async_remote_copy(
            amount, amount, send_sem.at[0], done,
            device_id={"docs": targets[PAIR]}, device_id_type=MESH,
        ).wait_recv()

    class Role:
        def __init__(self, is_end):
            self.is_end = is_end
            self.order = END_ORDER if is_end else MID_ORDER

        def slot(self, k, other):
            return self.order.index((k, other))

        def done(self, k, other, part):
            second = 1 if part == SECOND else 0
            if self.is_end:
                if (k, other) == (3, 1):
                    index = 8 if part in (FIRST_A, SECOND_A) else 9 if part in (FIRST_B, SECOND_B) else 10
                elif (k, other) == (0, 1):
                    index = {FIRST: 1, SECOND_A: 2, SECOND_C: 3}[part]
                else:
                    index = {(1, 0): second, (2, 0): 4 + second, (1, 1): 5, (3, 0): 6 + second, (2, 1): 7}[k, other]
            elif (k, other) == (3, 1):
                index = 9 if part == SECOND_A else 10 if part == SECOND_C else 11
            elif (k, other) == (0, 1):
                index = {FIRST: 8, SECOND_A: 6, SECOND_C: 7}[part]
            else:
                index = {(2, 0): second, (0, 0): 2 + second, (1, 1): 3, (3, 0): 4 + second, (2, 1): 8}[k, other]
            return recv_sem.at[index]

        def receiver(self, direction, k, other):
            if direction in (SIDE, SIDE_TWIN):
                return self, k, 1 - other
            if direction == PAIR:
                return self, k, other
            if direction in (OUT, OUT_TWIN):
                return at_end, k, other
            return at_mid, k if self.is_end else planes - 1 - k, other

        def send(self, k, other, part, directions, own=False):
            for direction in directions:
                role, kk, oo = self.receiver(direction, k, other)
                slot, there = self.slot(k, other), role.slot(kk, oo)
                done = pair_sem.at[(there + 1) // 2] if direction == PAIR else role.done(kk, oo, part)
                if part in (FIRST, FIRST_A, WHOLE):
                    lab_copy(direction, slot, there, done, own).start()
                data_copy(direction, slot, there, done, part, own).start()

        def arrived(self, k, other, part):
            take(self.done(k, other, part), part[1], 1 if part[0] == 0 else 0)

        def pass_on(self, k, other, part, directions):
            self.arrived(k, other, part)
            self.send(k, other, part, directions)

        def pair(self, k, other):
            self.send(k, other, WHOLE, (PAIR,))

    at_end, at_mid = Role(True), Role(False)

    def start_own(direction):
        def by(role):
            k = 0 if role.is_end else 1
            for part in {SIDE: (SECOND_A, SECOND_C, FIRST), PAIR: (WHOLE,)}.get(direction, (FIRST, SECOND)):
                role.send(k, 0, part, (direction,), own=True)

        if direction == OUT:
            by(at_mid)
        elif direction == PAIR:
            by(at_end)
        else:
            pl.when(end)(lambda: by(at_end))
            pl.when(mid)(lambda: by(at_mid))

    for direction, lower in enumerate(down):
        @pl.when(lower)
        def _():
            start_own(direction)
    for lower, stride, axis in ((z > 0, 2 * CORES, 0), (y == 1, CORES, 0), (core == 1, 1, 1)):
        @pl.when(lower)
        def _():
            pl.semaphore_signal(
                ready_sem.at[axis], inc=1, device_id={"docs": me - stride}, device_id_type=MESH,
            )

    own_data = pltpu.make_async_copy(x_ref, rows_of(0, core, WHOLE), own_sem.at[0])
    own_data.start()
    own_lab = pltpu.make_async_copy(lab_ref, labs.at[core], own_sem.at[0])
    own_lab.start()
    @pl.when(up[PAIR])
    def _():
        pl.semaphore_wait(ready_sem.at[1], 1)
        start_own(PAIR)

    higher_count = sum(higher.astype(jnp.int32) for higher in up[:PAIR])
    @pl.when(higher_count > 0)
    def _():
        pl.semaphore_wait(ready_sem.at[0], higher_count)
    for direction in (SIDE, IN, OUT):
        @pl.when(up[direction])
        def _():
            start_own(direction)

    own_amount = meter.at[pl.ds(0, rows * row_units + 1)]
    pltpu.make_async_copy(own_amount, own_amount, own_sem.at[0]).wait()
    label_column = jnp.transpose(
        jnp.broadcast_to(labs[core].astype(jnp.float32), (rows, rows))
    )[:, :1]

    def from_pair(group, slots):
        take(pair_sem.at[group], slots * rows, slots)

    def masked_scores(slot, count):
        keys = count * CORES * rows
        values = buf[pl.ds(pl.multiple_of(slot * CORES * rows, rows), keys), :]
        mine = buf[pl.ds(pl.multiple_of(core * rows, rows), rows), :]
        tags = jnp.concatenate(
            [labs[slot * CORES + n].astype(jnp.float32) for n in range(count * CORES)], axis=1
        )
        scores = lax.dot_general(
            mine, values, (((1,), (1,)), ((), ())), preferred_element_type=jnp.float32
        ) * (kernel_gain / math.sqrt(width))
        return scores, label_column == tags, values

    def first_block():
        scores, near, values = masked_scores(0, 1)
        gap = lax.broadcasted_iota(jnp.int32, near.shape, 1) - lax.broadcasted_iota(jnp.int32, near.shape, 0)
        masked = jnp.where(near & (gap != core * rows), scores, neg_large)
        peak = jnp.maximum(jnp.max(masked, axis=1, keepdims=True), neg_start)
        weights = jnp.exp(masked - peak)
        row_max[...] = peak
        row_total[...] = jnp.sum(weights, axis=1, keepdims=True)
        acc[...] = jnp.dot(weights.astype(jnp.bfloat16), values, preferred_element_type=jnp.float32)

    def absorb(slot, count):
        parts = []
        for n in range(count):
            scores, near, values = masked_scores(slot + n, 1)
            parts.append((jnp.where(near, scores, neg_large), values))
        before = row_max[...]
        peak = before
        for masked, _ in parts:
            peak = jnp.maximum(peak, jnp.max(masked, axis=1, keepdims=True))
        weights = [jnp.exp(masked - peak) for masked, _ in parts]
        scale = jnp.exp(before - peak)
        total = row_total[...] * scale + jnp.sum(sum(weights), axis=1, keepdims=True)
        gained = sum(
            jnp.dot(w.astype(jnp.bfloat16), values, preferred_element_type=jnp.float32)
            for w, (_, values) in zip(weights, parts)
        )
        return peak, total, scale, gained

    from_pair(0, 1)
    first_block()

    def step(j, carry):
        @pl.when(end & (j == 1))
        def _():
            r = at_end
            r.pass_on(1, 0, FIRST, (SIDE,))
            r.pass_on(0, 1, SECOND_A, (IN,))
            r.pass_on(0, 1, SECOND_C, (IN,))
            take(r.done(1, 0, SECOND), rows, 1)
            r.send(1, 0, SECOND, (SIDE,))
            r.send(0, 1, FIRST, (IN,))
            r.pair(1, 0)
            r.pair(0, 1)
            r.pass_on(2, 0, FIRST, (SIDE,))

        @pl.when(end & (j == 2))
        def _():
            r = at_end
            take(r.done(2, 0, SECOND), rows + half_rows, 1)
            r.send(2, 0, SECOND, (SIDE,))
            r.pair(2, 0)
            r.pair(1, 1)
            r.arrived(3, 0, FIRST)
            r.send(3, 0, FIRST_A, (SIDE,))
            r.send(3, 0, FIRST_B, (SIDE,))
            r.send(3, 0, FIRST_TIP, (SIDE, SIDE_TWIN))

        @pl.when(end & (j == 3))
        def _():
            r = at_end
            take(r.done(3, 0, SECOND), rows + half_rows, 1)
            r.pair(3, 0)
            r.pair(2, 1)
            take(r.done(3, 1, FIRST_A), half_rows, 1)
            r.send(3, 1, FIRST_A, (PAIR,))
            r.send(3, 1, SECOND_A, (PAIR,))
            take(r.done(3, 1, FIRST_B), half_rows - 2 * tip)
            r.send(3, 1, FIRST_B, (PAIR,))
            r.send(3, 1, SECOND_B, (PAIR,))

        @pl.when(mid & (j == 1))
        def _():
            r = at_mid
            r.pass_on(2, 0, FIRST, (OUT, SIDE))
            r.pass_on(0, 0, FIRST, (IN,))
            r.pass_on(2, 0, SECOND, (OUT, SIDE))
            r.pair(2, 0)
            take(r.done(0, 0, SECOND), rows + half_rows, 1)
            r.send(0, 0, SECOND, (IN,))
            r.pair(0, 0)
            r.pair(1, 1)
            r.pass_on(3, 0, FIRST, (OUT, SIDE))
            r.pass_on(0, 1, SECOND_A, (IN,))
            r.pass_on(0, 1, SECOND_C, (IN,))

        @pl.when(mid & (j == 2))
        def _():
            r = at_mid
            r.pass_on(3, 0, SECOND, (OUT,))
            r.pair(3, 0)
            take(r.done(0, 1, FIRST), rows + half_rows, 2)
            r.pair(0, 1)
            r.pair(2, 1)

        @pl.when(mid & (j == 3))
        def _():
            r = at_mid
            r.arrived(3, 1, SECOND_A)
            r.send(3, 1, SECOND_A, (OUT,))
            r.arrived(3, 1, SECOND_C)
            r.send(3, 1, SECOND_B, (OUT,))
            r.send(3, 1, SECOND_TIP, (OUT, OUT_TWIN))
            r.send(3, 1, SECOND, (PAIR,))
            r.arrived(3, 1, FIRST)
            r.send(3, 1, FIRST, (PAIR,))

        slot = 2 * j - 1
        from_pair(j, 2)
        peak, total, scale, gained = absorb(slot, 2)
        row_max[...] = peak
        row_total[...] = total
        acc[...] = acc[...] * scale + gained
        return carry

    lax.fori_loop(1, planes, step, 0)

    @pl.when(end)
    def _():
        take(at_end.done(3, 1, FIRST_TIP), 4 * tip)
        take(pair_sem.at[planes], rows - 2 * tip, 1)

    @pl.when(mid)
    def _():
        from_pair(planes, 1)

    parts = []
    for cc in range(CORES):
        values = buf[pl.ds(((2 * planes - 1) * CORES + cc) * rows, rows), :]
        scores = lax.dot_general(
            buf[pl.ds(pl.multiple_of(core * rows, rows), rows), :], values,
            (((1,), (1,)), ((), ())), preferred_element_type=jnp.float32,
        ) * (kernel_gain / math.sqrt(width))
        tags = labs[(2 * planes - 1) * CORES + cc].astype(jnp.float32)
        parts.append((jnp.where(label_column == tags, scores, neg_large), values))
    before = row_max[...]
    peak = jnp.maximum(before, jnp.max(jnp.maximum(parts[0][0], parts[1][0]), axis=1, keepdims=True))
    scale = jnp.exp(before - peak)
    weights = [jnp.exp(masked - peak) for masked, _ in parts]
    total = row_total[...] * scale + jnp.sum(weights[0] + weights[1], axis=1, keepdims=True)
    inverse = 1.0 / total
    gained = jnp.dot(
        jnp.concatenate([w.astype(jnp.bfloat16) for w in weights], axis=1),
        buf[pl.ds((2 * planes - 1) * CORES * rows, CORES * rows), :], preferred_element_type=jnp.float32,
    )
    mean_ref[...] = ((acc[...] * scale + gained) * inverse).astype(mean_ref.dtype)
    density = peak + jnp.log(total)
    dens_ref[...] = jnp.transpose(jnp.broadcast_to(density, (rows, rows)))[:1, :]

    def sent(data_rows, labels):
        amount = meter.at[pl.ds(0, data_rows * row_units + labels)]
        pltpu.make_async_remote_copy(
            amount, amount, send_sem.at[0], pair_sem.at[0],
            device_id={"docs": targets[PAIR]}, device_id_type=MESH,
        ).wait_send()

    @pl.when(end)
    def _():
        sent(27 * half_rows - tip, 14)

    @pl.when(mid)
    def _():
        sent(33 * half_rows + tip, 16)


def publish_kernel(dens_ref, mean_ref, dens_out, mean_out, sem):
    copies = (
        pltpu.make_async_copy(mean_ref, mean_out, sem.at[0]),
        pltpu.make_async_copy(dens_ref, dens_out, sem.at[1]),
    )
    for copy in copies:
        copy.start()
    for copy in copies:
        copy.wait()


def publish(density, mean):
    held = [pltpu.with_memory_space_constraint(a, pltpu.VMEM) for a in (density, mean)]
    return pl.pallas_call(
        publish_kernel,
        out_shape=tuple(jax.ShapeDtypeStruct(a.shape, a.dtype) for a in (density, mean)),
        in_specs=[pl.BlockSpec(memory_space=pltpu.VMEM)] * 2,
        out_specs=(pl.BlockSpec(memory_space=pltpu.HBM),) * 2,
        scratch_shapes=[pltpu.SemaphoreType.DMA((2,))],
    )(*held)


def general_call(device_count, rows, width):
    grid_slow, grid_fast = chip_grid(device_count)
    chips = device_count // CORES
    vmem = pl.BlockSpec(memory_space=pltpu.VMEM)
    return pl.pallas_call(
        functools.partial(kernel, grid_slow, grid_fast),
        out_shape=(
            pltpu.VMEM((1, rows), jnp.float32),
            pltpu.VMEM((rows, width), jnp.bfloat16),
        ),
        in_specs=[pl.BlockSpec(memory_space=pl.ANY), pl.BlockSpec(memory_space=pl.ANY)],
        out_specs=(vmem, vmem),
        scratch_shapes=[
            pltpu.VMEM((device_count * rows, width), jnp.bfloat16),
            pltpu.VMEM((device_count, 1, rows), jnp.int32),
            pltpu.VMEM((rows, width), jnp.bfloat16),
            pltpu.VMEM((rows, width), jnp.float32),
            pltpu.VMEM((rows, 1), jnp.float32),
            pltpu.VMEM((rows, 1), jnp.float32),
            pltpu.SemaphoreType.DMA((5, chips * PIECES)),
            pltpu.SemaphoreType.DMA((device_count * PIECES,)),
            pltpu.SemaphoreType.DMA((5, chips)),
            pltpu.SemaphoreType.DMA((device_count,)),
            pltpu.SemaphoreType.DMA((PIECES + 1,)),
            pltpu.SemaphoreType.DMA((1,)),
        ],
        compiler_params=pltpu.CompilerParams(collective_id=0, has_side_effects=True),
    )


def folded_call(device_count, rows, width):
    chips = device_count // CORES
    vmem = pl.BlockSpec(memory_space=pltpu.VMEM)
    return pl.pallas_call(
        functools.partial(folded_kernel, chips // 2),
        out_shape=(
            pltpu.VMEM((1, rows), jnp.float32),
            pltpu.VMEM((rows, width), jnp.bfloat16),
        ),
        in_specs=[pl.BlockSpec(memory_space=pl.ANY), pl.BlockSpec(memory_space=pl.ANY)],
        out_specs=(vmem, vmem),
        scratch_shapes=[
            pltpu.VMEM((device_count * rows, width), jnp.bfloat16),
            pltpu.VMEM((device_count, 1, rows), jnp.int32),
            pltpu.VMEM(((33 * rows // 2 + rows // 8) * width // (2 * rows) + 2 * chips, 1, rows), jnp.int32),
            pltpu.VMEM((rows, width), jnp.float32),
            pltpu.VMEM((rows, 1), jnp.float32),
            pltpu.VMEM((rows, 1), jnp.float32),
            pltpu.SemaphoreType.DMA((1,)),
            pltpu.SemaphoreType.DMA((12,)),
            pltpu.SemaphoreType.DMA((chips // 2 + 1,)),
            pltpu.SemaphoreType.DMA((1,)),
            pltpu.SemaphoreType.REGULAR((2,)),
        ],
        compiler_params=pltpu.CompilerParams(collective_id=0, has_side_effects=True),
    )


def per_device(device_count, embeddings, labels, row_slot):
    rows, width = embeddings.shape
    call = folded_call if chip_grid(device_count) == FOLDED_GRID else general_call
    density, mean = call(device_count, rows, width)(embeddings, labels.reshape(1, rows))
    density, mean = publish(density, mean)
    return density.reshape(rows), mean


def solution(mesh):
    return jax.shard_map(
        functools.partial(per_device, mesh.shape["docs"]),
        mesh=mesh,
        in_specs=(P(("groups", "docs"), None), P(("groups", "docs")), P(("groups", "docs"))),
        out_specs=(P(("groups", "docs")), P(("groups", "docs"), None)),
        check_vma=False,
    )
```

```python
import functools
import math

import jax
import jax.numpy as jnp
from jax import lax
from jax.experimental import pallas as pl
from jax.experimental.pallas import tpu as pltpu
from jax.sharding import PartitionSpec as P

MESH = pl.DeviceIdType.MESH
CORES = 2
PIECES = 2
HALVES = 1
FOLDED_GRID = (4, 2)

neg_large = -1e30
neg_start = -1e29
kernel_gain = 4.0


def chip_grid(device_count):
    chips = device_count // CORES
    fast = 1
    while (2 * fast) * (2 * fast) <= chips and chips % (2 * fast) == 0:
        fast *= 2
    return chips // fast, fast


def kernel(
    grid_slow, grid_fast, x_ref, lab_ref, dens_ref, mean_ref,
    buf, labs, mine, acc, row_max, row_total,
    send_sem, recv_sem, lsend_sem, lrecv_sem, own_sem, own_lab_sem,
):
    rows, width = x_ref.shape
    part = rows // PIECES
    group = PIECES // HALVES
    half_rows = rows // HALVES
    keys = CORES * half_rows
    me = lax.axis_index("docs")
    core = lax.rem(me, CORES)
    chip = me // CORES
    y = lax.rem(chip, grid_fast)
    z = chip // grid_fast

    def device(zz, yy, cc):
        return (zz * grid_fast + yy) * CORES + cc

    targets = (
        (z > 0, device(z - 1, y, core)),
        (z < grid_slow - 1, device(z + 1, y, core)),
        (y > 0, device(z, y - 1, core)),
        (y < grid_fast - 1, device(z, y + 1, core)),
        (z >= 0, device(z, y, 1 - core)),
    )

    barrier = pltpu.get_barrier_semaphore()
    for there, target in targets:
        @pl.when(there)
        def _():
            pl.semaphore_signal(barrier, inc=1, device_id={"docs": target}, device_id_type=MESH)

    def data_of(zz, yy, cc, piece):
        where = ((zz * grid_fast + yy) * HALVES + piece // group) * CORES + cc
        return buf.at[pl.ds(pl.multiple_of((where * group + lax.rem(piece, group)) * part, part), part)]

    own_copies = [pltpu.make_async_copy(x_ref, mine, own_sem.at[PIECES])]
    for piece in range(PIECES):
        own_copies.append(
            pltpu.make_async_copy(
                x_ref.at[pl.ds(piece * part, part)], data_of(z, y, core, piece), own_sem.at[piece]
            )
        )
    own_copies.append(pltpu.make_async_copy(lab_ref, labs.at[me], own_lab_sem.at[0]))
    for copy in own_copies:
        copy.start()
    pl.semaphore_wait(barrier, sum(there.astype(jnp.int32) for there, _ in targets))

    def data_copy(direction, zz, yy, piece, own):
        data = data_of(zz, yy, core, piece)
        return pltpu.make_async_remote_copy(
            x_ref.at[pl.ds(piece * part, part)] if own else data, data,
            send_sem.at[direction, (zz * grid_fast + yy) * PIECES + piece],
            recv_sem.at[device(zz, yy, core) * PIECES + piece],
            device_id={"docs": targets[direction][1]}, device_id_type=MESH,
        )

    def lab_copy(direction, zz, yy, own):
        slot = device(zz, yy, core)
        return pltpu.make_async_remote_copy(
            lab_ref if own else labs.at[slot], labs.at[slot],
            lsend_sem.at[direction, zz * grid_fast + yy], lrecv_sem.at[slot],
            device_id={"docs": targets[direction][1]}, device_id_type=MESH,
        )

    def each(directions, wanted, zz, yy, piece, own, act):
        for direction, want in zip(directions, wanted):
            @pl.when(jnp.logical_and(targets[direction][0], want))
            def _():
                @pl.when(piece == 0)
                def _():
                    act(lab_copy(direction, zz, yy, own))
                act(data_copy(direction, zz, yy, piece, own))

    start = lambda copy: copy.start()
    finish = lambda copy: copy.wait_send()

    def arrived(zz, yy, cc, piece):
        slot = device(zz, yy, cc)
        @pl.when(piece == 0)
        def _():
            pltpu.make_async_remote_copy(
                labs.at[slot], labs.at[slot], lsend_sem.at[0, 0], lrecv_sem.at[slot],
                device_id={"docs": targets[4][1]}, device_id_type=MESH,
            ).wait_recv()
        data = data_of(zz, yy, cc, piece)
        pltpu.make_async_remote_copy(
            data, data, send_sem.at[0, 0], recv_sem.at[slot * PIECES + piece],
            device_id={"docs": targets[4][1]}, device_id_type=MESH,
        ).wait_recv()

    yes = z >= 0
    for piece in range(PIECES):
        each((2, 3, 0, 1, 4), (yes,) * 5, z, y, piece, True, start)

    row_max[...] = jnp.full_like(row_max, neg_large)
    row_total[...] = jnp.zeros_like(row_total)
    acc[...] = jnp.zeros_like(acc)
    own_copies[-1].wait()
    label_column = jnp.transpose(
        jnp.broadcast_to(labs[me].astype(jnp.float32), (rows, rows))
    )[:, :1]
    column = lax.broadcasted_iota(jnp.int32, (rows, keys), 1)
    gap = (
        column + (column // half_rows) * (rows - half_rows)
        - lax.broadcasted_iota(jnp.int32, (rows, keys), 0)
    )
    for copy in own_copies[:-1]:
        copy.wait()

    def compute(zz, yy, half):
        where = zz * grid_fast + yy
        values = buf[pl.ds(pl.multiple_of((where * HALVES + half) * keys, keys), keys), :]
        tags = []
        for cc in range(CORES):
            tag = labs[where * CORES + cc].astype(jnp.float32)
            pieces = [tag[:, h * half_rows:(h + 1) * half_rows] for h in range(HALVES)]
            picked = pieces[0]
            for h in range(1, HALVES):
                picked = jnp.where(half == h, pieces[h], picked)
            tags.append(picked)
        tags = jnp.concatenate(tags, axis=1)
        scores = lax.dot_general(
            mine[...], values, (((1,), (1,)), ((), ())), preferred_element_type=jnp.float32
        ) * (kernel_gain / math.sqrt(width))
        self_gap = jnp.where(where == chip, core * rows - half * half_rows, CORES * rows)
        absorb(scores, (label_column == tags) & (gap != self_gap), values)

    def compute_core(zz, yy, cc):
        slot = device(zz, yy, cc)
        values = buf[pl.ds(pl.multiple_of(slot * rows, rows), rows), :]
        scores = lax.dot_general(
            mine[...], values, (((1,), (1,)), ((), ())), preferred_element_type=jnp.float32
        ) * (kernel_gain / math.sqrt(width))
        absorb(scores, label_column == labs[slot].astype(jnp.float32), values)

    def absorb(scores, near, values):
        masked = jnp.where(near, scores, neg_large)
        before = row_max[...]
        peak = jnp.maximum(before, jnp.max(masked, axis=1, keepdims=True))
        weights = jnp.where(near, jnp.exp(masked - peak), 0.0)
        scale = jnp.exp(before - peak)
        row_max[...] = peak
        row_total[...] = row_total[...] * scale + jnp.sum(weights, axis=1, keepdims=True)
        acc[...] = acc[...] * scale + jnp.dot(
            weights.astype(jnp.bfloat16), values, preferred_element_type=jnp.float32
        )

    def meet(zz, yy, half):
        def one(p, carry):
            arrived(zz, yy, 1 - core, half * group + p)
            return carry
        lax.fori_loop(0, group, one, 0)
        compute(zz, yy, half)

    def visited(distance, side, reach, origin):
        place = origin + jnp.where(side == 0, -distance, distance)
        inside = (distance >= 0) & (distance < reach) & (place >= 0) & (place < reach)
        return place, inside & jnp.logical_or(distance > 0, side == 0)

    def other_columns(body):
        if grid_fast == 2:
            body(1 - y)
            return
        def one(i, carry):
            yy, valid = visited(i // 2 + 1, lax.rem(i, 2), grid_fast, y)
            @pl.when(valid)
            def _():
                body(yy)
            return carry
        lax.fori_loop(0, 2 * (grid_fast - 1), one, 0)

    def along(zz, piece, side, act):
        each((2, 3, 0, 1, 4), (yes, yes, side == 1, side == 0, yes), zz, y, piece, False, act)

    def across(zz, yy, piece, act):
        each((2, 3, 4), (yy > y, yy < y, yes), zz, yy, piece, False, act)

    def receive(zz, yy, piece):
        arrived(zz, yy, core, piece)
        across(zz, yy, piece, start)

    farthest = jnp.where(2 * z >= grid_slow, 0, grid_slow - 1)

    def event(e, carry):
        distance = e // (2 * PIECES)
        piece = lax.rem(e // 2, PIECES)
        side = lax.rem(e, 2)
        half = piece // group

        @pl.when(e == 2 * PIECES * grid_slow)
        def _():
            for p in range(PIECES):
                each((2, 3, 0, 1, 4), (yes,) * 5, z, y, p, True, finish)

        zz, valid = visited(distance, side, grid_slow, z)
        @pl.when(valid & (distance > 0))
        def _():
            arrived(zz, y, core, piece)
            along(zz, piece, side, start)

        z1, valid1 = visited(distance - 1, side, grid_slow, z)
        z2, valid2 = visited(distance - 2, side, grid_slow, z)
        @pl.when(valid2)
        def _():
            other_columns(lambda yy: receive(z2, yy, piece))
            @pl.when(distance > 2)
            def _():
                along(z2, piece, side, finish)

        z3, valid3 = visited(distance - 3, side, grid_slow, z)
        @pl.when(valid3)
        def _():
            other_columns(lambda yy: across(z3, yy, piece, finish))

        near = valid1 & (lax.rem(piece, group) == 0)
        if grid_fast == 2:
            far = valid2 & (lax.rem(piece, group) == group - 1) & (z2 != farthest)
            @pl.when(near | far)
            def _():
                def one(i, carry):
                    @pl.when(jnp.where(i == 0, near, far))
                    def _():
                        meet(jnp.where(i == 0, z1, z2), jnp.where(i == 0, y, 1 - y), half)
                    return carry
                lax.fori_loop(0, 2, one, 0)
        else:
            @pl.when(near)
            def _():
                meet(z1, y, half)
            @pl.when(valid2 & (lax.rem(piece, group) == group - 1))
            def _():
                other_columns(lambda yy: meet(z2, yy, half))
        return carry

    lax.fori_loop(0, 2 * PIECES * (grid_slow + 2), event, 0)
    if grid_fast == 2:
        def last_pair(i, carry):
            cc = jnp.where(i == 0, core, 1 - core)
            @pl.when(i == 1)
            def _():
                for p in range(PIECES):
                    arrived(farthest, 1 - y, 1 - core, p)
            compute_core(farthest, 1 - y, cc)
            return carry
        lax.fori_loop(0, CORES, last_pair, 0)

    total = row_total[...]
    density = row_max[...] + jnp.log(total)
    dens_ref[...] = jnp.transpose(jnp.broadcast_to(density, (rows, rows)))[:1, :]
    mean_ref[...] = (acc[...] / total).astype(mean_ref.dtype)

    for e in range(2 * PIECES):
        last, valid = visited(grid_slow - 1, e % 2, grid_slow, z)
        @pl.when(valid)
        def _():
            other_columns(lambda yy: across(last, yy, e // 2, finish))


def folded_kernel(
    planes, x_ref, lab_ref, dens_ref, mean_ref,
    buf, labs, meter, acc, row_max, row_total,
    send_sem, recv_sem, pair_sem, ready_sem,
):
    rows, width = x_ref.shape
    row_units = width * x_ref.dtype.itemsize // (rows * lab_ref.dtype.itemsize)
    half_rows = rows // 2
    tip = rows // 8
    FIRST, SECOND, WHOLE = (0, half_rows), (half_rows, half_rows), (0, rows)
    FIRST_A, FIRST_B = (0, half_rows // 2), (half_rows // 2, half_rows // 2 - tip)
    FIRST_TIP, SECOND_TIP = (half_rows - tip, tip), (half_rows, tip)
    SECOND_B, SECOND_A = (half_rows + tip, half_rows // 2 - tip), (rows - half_rows // 2, half_rows // 2)
    SECOND_C = (half_rows, half_rows // 2)
    me = lax.axis_index("docs")
    core = lax.rem(me, CORES)
    y = lax.rem(me // CORES, 2)
    z = me // (CORES * 2)
    barrier = pltpu.get_barrier_semaphore()
    for higher, stride in ((z < planes - 1, 2 * CORES), (y == 0, CORES), (core == 0, 1)):
        @pl.when(higher)
        def _():
            pl.semaphore_signal(barrier, inc=1, device_id={"docs": me + stride}, device_id_type=MESH)

    mirrored = 2 * z >= planes
    end = (z == 0) | (z == planes - 1)
    mid = jnp.logical_not(end)

    def device(k, column, cc):
        zz = jnp.where(mirrored, planes - 1 - k, k)
        return (zz * 2 + column) * CORES + cc

    OUT, IN, SIDE, PAIR, OUT_TWIN, SIDE_TWIN = range(6)
    home = jnp.where(end, 0, 1)
    inward = jnp.where(mirrored, -2 * CORES, 2 * CORES)
    across, beside = CORES - 2 * CORES * y, 1 - 2 * core
    targets = (me - inward, me + inward, me + across, me + beside, me - inward + beside, me + across + beside)
    END_ORDER = ((0, 0), (1, 0), (0, 1), (2, 0), (1, 1), (3, 0), (2, 1), (3, 1))
    MID_ORDER = ((1, 0), (2, 0), (0, 0), (3, 0), (0, 1), (1, 1), (2, 1), (3, 1))

    up = (mid & mirrored, jnp.logical_not(mirrored), y == 0, core == 0)
    down = (mid & jnp.logical_not(mirrored), mirrored, y == 1, core == 1)

    def rows_of(slot, cc, part):
        first, size = part
        first = (slot * CORES + cc) * rows + first
        return buf.at[pl.ds(pl.multiple_of(first, tip), size)]

    lower_count = (z > 0).astype(jnp.int32) + y + core
    @pl.when(lower_count > 0)
    def _():
        pl.semaphore_wait(barrier, lower_count)

    def data_copy(direction, slot, there, done, part, own=False):
        return pltpu.make_async_remote_copy(
            x_ref.at[pl.ds(*part)] if own else rows_of(slot, core, part), rows_of(there, core, part),
            send_sem.at[0], done,
            device_id={"docs": targets[direction]}, device_id_type=MESH,
        )

    def lab_copy(direction, slot, there, done, own=False):
        return pltpu.make_async_remote_copy(
            lab_ref if own else labs.at[slot * CORES + core], labs.at[there * CORES + core],
            send_sem.at[0], done,
            device_id={"docs": targets[direction]}, device_id_type=MESH,
        )

    def take(done, data_rows, labels=0):
        amount = meter.at[pl.ds(0, data_rows * row_units + labels)]
        pltpu.make_async_remote_copy(
            amount, amount, send_sem.at[0], done,
            device_id={"docs": targets[PAIR]}, device_id_type=MESH,
        ).wait_recv()

    class Role:
        def __init__(self, is_end):
            self.is_end = is_end
            self.order = END_ORDER if is_end else MID_ORDER

        def slot(self, k, other):
            return self.order.index((k, other))

        def done(self, k, other, part):
            second = 1 if part == SECOND else 0
            if self.is_end:
                if (k, other) == (3, 1):
                    index = 8 if part in (FIRST_A, SECOND_A) else 9 if part in (FIRST_B, SECOND_B) else 10
                elif (k, other) == (0, 1):
                    index = {FIRST: 1, SECOND_A: 2, SECOND_C: 3}[part]
                else:
                    index = {(1, 0): second, (2, 0): 4 + second, (1, 1): 5, (3, 0): 6 + second, (2, 1): 7}[k, other]
            elif (k, other) == (3, 1):
                index = 9 if part == SECOND_A else 10 if part == SECOND_C else 11
            elif (k, other) == (0, 1):
                index = {FIRST: 8, SECOND_A: 6, SECOND_C: 7}[part]
            else:
                index = {(2, 0): second, (0, 0): 2 + second, (1, 1): 3, (3, 0): 4 + second, (2, 1): 8}[k, other]
            return recv_sem.at[index]

        def receiver(self, direction, k, other):
            if direction in (SIDE, SIDE_TWIN):
                return self, k, 1 - other
            if direction == PAIR:
                return self, k, other
            if direction in (OUT, OUT_TWIN):
                return at_end, k, other
            return at_mid, k if self.is_end else planes - 1 - k, other

        def send(self, k, other, part, directions, own=False):
            for direction in directions:
                role, kk, oo = self.receiver(direction, k, other)
                slot, there = self.slot(k, other), role.slot(kk, oo)
                done = pair_sem.at[(there + 1) // 2] if direction == PAIR else role.done(kk, oo, part)
                if part in (FIRST, FIRST_A, WHOLE):
                    lab_copy(direction, slot, there, done, own).start()
                data_copy(direction, slot, there, done, part, own).start()

        def arrived(self, k, other, part):
            take(self.done(k, other, part), part[1], 1 if part[0] == 0 else 0)

        def pass_on(self, k, other, part, directions):
            self.arrived(k, other, part)
            self.send(k, other, part, directions)

        def pair(self, k, other):
            self.send(k, other, WHOLE, (PAIR,))

    at_end, at_mid = Role(True), Role(False)

    def start_own(direction):
        def by(role):
            k = 0 if role.is_end else 1
            for part in {SIDE: (SECOND_A, SECOND_C, FIRST), PAIR: (WHOLE,)}.get(direction, (FIRST, SECOND)):
                role.send(k, 0, part, (direction,), own=True)

        if direction == OUT:
            by(at_mid)
        elif direction == PAIR:
            by(at_end)
        else:
            pl.when(end)(lambda: by(at_end))
            pl.when(mid)(lambda: by(at_mid))

    for direction, lower in enumerate(down):
        @pl.when(lower)
        def _():
            start_own(direction)
    for lower, stride, axis in ((z > 0, 2 * CORES, 0), (y == 1, CORES, 0), (core == 1, 1, 1)):
        @pl.when(lower)
        def _():
            pl.semaphore_signal(
                ready_sem.at[axis], inc=1, device_id={"docs": me - stride}, device_id_type=MESH,
            )

    own_data = pltpu.make_async_copy(x_ref, rows_of(0, core, WHOLE), pair_sem.at[0])
    own_data.start()
    own_lab = pltpu.make_async_copy(lab_ref, labs.at[core], pair_sem.at[0])
    own_lab.start()
    @pl.when(up[PAIR])
    def _():
        pl.semaphore_wait(ready_sem.at[1], 1)
        start_own(PAIR)

    higher_count = sum(higher.astype(jnp.int32) for higher in up[:PAIR])
    @pl.when(higher_count > 0)
    def _():
        pl.semaphore_wait(ready_sem.at[0], higher_count)
    for direction in (SIDE, IN, OUT):
        @pl.when(up[direction])
        def _():
            start_own(direction)

    take(pair_sem.at[0], 2 * rows, 2)
    label_column = jnp.transpose(
        jnp.broadcast_to(labs[core].astype(jnp.float32), (rows, rows))
    )[:, :1]

    def from_pair(group, slots):
        take(pair_sem.at[group], slots * rows, slots)

    def masked_scores(slot, count):
        keys = count * CORES * rows
        values = buf[pl.ds(pl.multiple_of(slot * CORES * rows, rows), keys), :]
        mine = buf[pl.ds(pl.multiple_of(core * rows, rows), rows), :]
        tags = jnp.concatenate(
            [labs[slot * CORES + n].astype(jnp.float32) for n in range(count * CORES)], axis=1
        )
        scores = lax.dot_general(
            mine, values, (((1,), (1,)), ((), ())), preferred_element_type=jnp.float32
        ) * (kernel_gain / math.sqrt(width))
        return scores, label_column == tags, values

    def first_block():
        scores, near, values = masked_scores(0, 1)
        gap = lax.broadcasted_iota(jnp.int32, near.shape, 1) - lax.broadcasted_iota(jnp.int32, near.shape, 0)
        masked = jnp.where(near & (gap != core * rows), scores, neg_large)
        peak = jnp.maximum(jnp.max(masked, axis=1, keepdims=True), neg_start)
        weights = jnp.exp(masked - peak)
        row_max[...] = peak
        row_total[...] = jnp.sum(weights, axis=1, keepdims=True)
        acc[...] = jnp.dot(weights.astype(jnp.bfloat16), values, preferred_element_type=jnp.float32)

    def absorb(slot, count):
        parts = []
        for n in range(count):
            scores, near, values = masked_scores(slot + n, 1)
            parts.append((jnp.where(near, scores, neg_large), values))
        before = row_max[...]
        peak = before
        for masked, _ in parts:
            peak = jnp.maximum(peak, jnp.max(masked, axis=1, keepdims=True))
        weights = [jnp.exp(masked - peak) for masked, _ in parts]
        scale = jnp.exp(before - peak)
        total = row_total[...] * scale + jnp.sum(sum(weights), axis=1, keepdims=True)
        gained = sum(
            jnp.dot(w.astype(jnp.bfloat16), values, preferred_element_type=jnp.float32)
            for w, (_, values) in zip(weights, parts)
        )
        return peak, total, scale, gained

    first_block()

    def step(j, carry):
        @pl.when(end & (j == 1))
        def _():
            r = at_end
            r.pass_on(1, 0, FIRST, (SIDE,))
            r.pass_on(0, 1, SECOND_A, (IN,))
            r.pass_on(0, 1, SECOND_C, (IN,))
            take(r.done(1, 0, SECOND), rows, 1)
            r.send(1, 0, SECOND, (SIDE,))
            r.send(0, 1, FIRST, (IN,))
            r.pair(1, 0)
            r.pair(0, 1)
            r.pass_on(2, 0, FIRST, (SIDE,))

        @pl.when(end & (j == 2))
        def _():
            r = at_end
            take(r.done(2, 0, SECOND), rows + half_rows, 1)
            r.send(2, 0, SECOND, (SIDE,))
            r.pair(2, 0)
            r.pair(1, 1)
            r.arrived(3, 0, FIRST)
            r.send(3, 0, FIRST_A, (SIDE,))
            r.send(3, 0, FIRST_B, (SIDE,))
            r.send(3, 0, FIRST_TIP, (SIDE, SIDE_TWIN))

        @pl.when(end & (j == 3))
        def _():
            r = at_end
            take(r.done(3, 0, SECOND), rows + half_rows, 1)
            r.pair(3, 0)
            r.pair(2, 1)
            take(r.done(3, 1, FIRST_A), half_rows, 1)
            r.send(3, 1, FIRST_A, (PAIR,))
            r.send(3, 1, SECOND_A, (PAIR,))
            take(r.done(3, 1, FIRST_B), half_rows - 2 * tip)
            r.send(3, 1, FIRST_B, (PAIR,))
            r.send(3, 1, SECOND_B, (PAIR,))

        @pl.when(mid & (j == 1))
        def _():
            r = at_mid
            r.pass_on(2, 0, FIRST, (OUT, SIDE))
            r.pass_on(0, 0, FIRST, (IN,))
            r.pass_on(2, 0, SECOND, (OUT, SIDE))
            r.pair(2, 0)
            take(r.done(0, 0, SECOND), rows + half_rows, 1)
            r.send(0, 0, SECOND, (IN,))
            r.pair(0, 0)
            r.pair(1, 1)
            r.pass_on(3, 0, FIRST, (OUT, SIDE))
            r.pass_on(0, 1, SECOND_A, (IN,))
            r.pass_on(0, 1, SECOND_C, (IN,))

        @pl.when(mid & (j == 2))
        def _():
            r = at_mid
            r.pass_on(3, 0, SECOND, (OUT,))
            r.pair(3, 0)
            take(r.done(0, 1, FIRST), rows + half_rows, 2)
            r.pair(0, 1)
            r.pair(2, 1)

        @pl.when(mid & (j == 3))
        def _():
            r = at_mid
            r.arrived(3, 1, SECOND_A)
            r.send(3, 1, SECOND_A, (OUT,))
            r.arrived(3, 1, SECOND_C)
            r.send(3, 1, SECOND_B, (OUT,))
            r.send(3, 1, SECOND_TIP, (OUT, OUT_TWIN))
            r.send(3, 1, SECOND, (PAIR,))
            r.arrived(3, 1, FIRST)
            r.send(3, 1, FIRST, (PAIR,))

        slot = 2 * j - 1
        from_pair(j, 2)
        peak, total, scale, gained = absorb(slot, 2)
        row_max[...] = peak
        row_total[...] = total
        acc[...] = acc[...] * scale + gained
        return carry

    lax.fori_loop(1, planes, step, 0)

    @pl.when(end)
    def _():
        take(at_end.done(3, 1, FIRST_TIP), 4 * tip)
        take(pair_sem.at[planes], rows - 2 * tip, 1)

    @pl.when(mid)
    def _():
        from_pair(planes, 1)

    parts = []
    for cc in range(CORES):
        values = buf[pl.ds(((2 * planes - 1) * CORES + cc) * rows, rows), :]
        scores = lax.dot_general(
            buf[pl.ds(pl.multiple_of(core * rows, rows), rows), :], values,
            (((1,), (1,)), ((), ())), preferred_element_type=jnp.float32,
        ) * (kernel_gain / math.sqrt(width))
        tags = labs[(2 * planes - 1) * CORES + cc].astype(jnp.float32)
        parts.append((jnp.where(label_column == tags, scores, neg_large), values))
    before = row_max[...]
    peak = jnp.maximum(before, jnp.max(jnp.maximum(parts[0][0], parts[1][0]), axis=1, keepdims=True))
    scale = jnp.exp(before - peak)
    weights = [jnp.exp(masked - peak) for masked, _ in parts]
    total = row_total[...] * scale + jnp.sum(weights[0] + weights[1], axis=1, keepdims=True)
    inverse = 1.0 / total
    gained = jnp.dot(
        jnp.concatenate([w.astype(jnp.bfloat16) for w in weights], axis=1),
        buf[pl.ds((2 * planes - 1) * CORES * rows, CORES * rows), :], preferred_element_type=jnp.float32,
    )
    mean_ref[...] = ((acc[...] * scale + gained) * inverse).astype(mean_ref.dtype)
    density = peak + jnp.log(total)
    dens_ref[...] = jnp.transpose(jnp.broadcast_to(density, (rows, rows)))[:1, :]

    def sent(data_rows, labels):
        amount = meter.at[pl.ds(0, data_rows * row_units + labels)]
        pltpu.make_async_remote_copy(
            amount, amount, send_sem.at[0], pair_sem.at[0],
            device_id={"docs": targets[PAIR]}, device_id_type=MESH,
        ).wait_send()

    @pl.when(end)
    def _():
        sent(27 * half_rows - tip, 14)

    @pl.when(mid)
    def _():
        sent(33 * half_rows + tip, 16)


def publish_kernel(dens_ref, mean_ref, dens_out, mean_out, sem):
    copies = (
        pltpu.make_async_copy(mean_ref, mean_out, sem.at[0]),
        pltpu.make_async_copy(dens_ref, dens_out, sem.at[1]),
    )
    for copy in copies:
        copy.start()
    for copy in copies:
        copy.wait()


def publish(density, mean):
    held = [pltpu.with_memory_space_constraint(a, pltpu.VMEM) for a in (density, mean)]
    return pl.pallas_call(
        publish_kernel,
        out_shape=tuple(jax.ShapeDtypeStruct(a.shape, a.dtype) for a in (density, mean)),
        in_specs=[pl.BlockSpec(memory_space=pltpu.VMEM)] * 2,
        out_specs=(pl.BlockSpec(memory_space=pltpu.HBM),) * 2,
        scratch_shapes=[pltpu.SemaphoreType.DMA((2,))],
    )(*held)


def general_call(device_count, rows, width):
    grid_slow, grid_fast = chip_grid(device_count)
    chips = device_count // CORES
    vmem = pl.BlockSpec(memory_space=pltpu.VMEM)
    return pl.pallas_call(
        functools.partial(kernel, grid_slow, grid_fast),
        out_shape=(
            pltpu.VMEM((1, rows), jnp.float32),
            pltpu.VMEM((rows, width), jnp.bfloat16),
        ),
        in_specs=[pl.BlockSpec(memory_space=pl.ANY), pl.BlockSpec(memory_space=pl.ANY)],
        out_specs=(vmem, vmem),
        scratch_shapes=[
            pltpu.VMEM((device_count * rows, width), jnp.bfloat16),
            pltpu.VMEM((device_count, 1, rows), jnp.int32),
            pltpu.VMEM((rows, width), jnp.bfloat16),
            pltpu.VMEM((rows, width), jnp.float32),
            pltpu.VMEM((rows, 1), jnp.float32),
            pltpu.VMEM((rows, 1), jnp.float32),
            pltpu.SemaphoreType.DMA((5, chips * PIECES)),
            pltpu.SemaphoreType.DMA((device_count * PIECES,)),
            pltpu.SemaphoreType.DMA((5, chips)),
            pltpu.SemaphoreType.DMA((device_count,)),
            pltpu.SemaphoreType.DMA((PIECES + 1,)),
            pltpu.SemaphoreType.DMA((1,)),
        ],
        compiler_params=pltpu.CompilerParams(collective_id=0, has_side_effects=True),
    )


def folded_call(device_count, rows, width):
    chips = device_count // CORES
    vmem = pl.BlockSpec(memory_space=pltpu.VMEM)
    return pl.pallas_call(
        functools.partial(folded_kernel, chips // 2),
        out_shape=(
            pltpu.VMEM((1, rows), jnp.float32),
            pltpu.VMEM((rows, width), jnp.bfloat16),
        ),
        in_specs=[pl.BlockSpec(memory_space=pl.ANY), pl.BlockSpec(memory_space=pl.ANY)],
        out_specs=(vmem, vmem),
        scratch_shapes=[
            pltpu.VMEM((device_count * rows, width), jnp.bfloat16),
            pltpu.VMEM((device_count, 1, rows), jnp.int32),
            pltpu.VMEM(((33 * rows // 2 + rows // 8) * width // (2 * rows) + 2 * chips, 1, rows), jnp.int32),
            pltpu.VMEM((rows, width), jnp.float32),
            pltpu.VMEM((rows, 1), jnp.float32),
            pltpu.VMEM((rows, 1), jnp.float32),
            pltpu.SemaphoreType.DMA((1,)),
            pltpu.SemaphoreType.DMA((12,)),
            pltpu.SemaphoreType.DMA((chips // 2 + 1,)),
            pltpu.SemaphoreType.REGULAR((2,)),
        ],
        compiler_params=pltpu.CompilerParams(collective_id=0, has_side_effects=True),
    )


def per_device(device_count, embeddings, labels, row_slot):
    rows, width = embeddings.shape
    call = folded_call if chip_grid(device_count) == FOLDED_GRID else general_call
    density, mean = call(device_count, rows, width)(embeddings, labels.reshape(1, rows))
    density, mean = publish(density, mean)
    return density.reshape(rows), mean


def solution(mesh):
    return jax.shard_map(
        functools.partial(per_device, mesh.shape["docs"]),
        mesh=mesh,
        in_specs=(P(("groups", "docs"), None), P(("groups", "docs")), P(("groups", "docs"))),
        out_specs=(P(("groups", "docs")), P(("groups", "docs"), None)),
        check_vma=False,
    )
```
